32 devices in a mesh: groups: 2 (over y), space: 4 (over z), freq: 2 (over x), band: 2 (over core).
Axes of the slice: x: 2, y: 2, z: 4, core: 2. Of those that a mesh axis runs over, the one named last changes fastest.
Arguments:
- snapshots: bfloat16 [16, 256, 32768], P(('freq', 'band'), None, ('groups', 'space')), parts along dimension 2, may hold values from -6 to 6
- weights: float32 [32768], P(('groups', 'space')), parts along dimension 0, may hold values from 0.25 to 2.5
- triads: int32 [64, 2], replicated, may hold values from 0 to 63, as said below
Outputs:
- bispectra: float32 [128, 512], P(('groups', 'space', 'freq', 'band')), parts along dimension 0
The draws below stay inside these ranges and needn't reach their ends.
There are 2 independent parts, one for each index of `groups`. The reference program is written for one: setup_inputs(seed, part) draws one part's arguments, and reference() takes and returns one part's arrays. A program takes and returns all parts, laid end to end along the dimension named above; an argument that names none is the same for every part. Nothing has to cross between parts.
Inputs may be any that keep to these rules, and one draw needn't show every extreme that they name: `triads`: each row is a pair (k, l) with k >= l and k + l <= 63; all pairs are distinct; the pair (63, 0) is always present.
All inputs are finite; a program needn't handle non-finite values.
Results may differ from the reference program's by a relative error of at most 0.0078.
Values may be sent and summed in bfloat16 or wider, within the bound.
No kernel may reach another device: no remote copies, remote signals or barrier semaphores. Data moves between devices by JAX's collectives and lax.ppermute only.
A program may use at most 128 MiB of HBM per device.

```python
import math
import jax
import jax.numpy as jnp
from jax import lax

NB = 16
NFFT = 256
NF = 64
P_SIZE = 16384
NTRI = 64


def draw_triads(key, part):
    cell_count = NF * NF
    cell_index = jnp.arange(cell_count, dtype=jnp.int32)
    first_freq = cell_index // NF
    second_freq = cell_index % NF
    valid_cell = (first_freq >= second_freq) & (first_freq + second_freq <= NF - 1)
    random_bits = jax.random.randint(key, (cell_count,), 0, 65536, dtype=jnp.int32)
    scores = random_bits * cell_count + cell_index
    scores = jnp.where(valid_cell, scores, -1)
    forced_cell = (first_freq == NF - 1) & (second_freq == 0)
    scores = jnp.where(forced_cell, 65536 * cell_count, scores)
    top_scores, picked = lax.top_k(scores, NTRI)
    return jnp.stack([first_freq[picked], second_freq[picked]], axis=1).astype(jnp.int32)


def block_scale(own_key, extent, cuts, smallest, top_value):
    loudness = 1.0
    for position, blocks in cuts:
        draws = jax.random.uniform(jax.random.fold_in(jax.random.fold_in(own_key, 6), position), (blocks,), jnp.float32, smallest / len(cuts), top_value / len(cuts))
        loudness = loudness * jnp.repeat(jnp.exp(draws), extent[position] // blocks).reshape((-1,) + (1,) * (len(extent) - 1 - position))
    return loudness


def centred(rng, dims, spread, most, shards=(), held_as=jnp.bfloat16):
    array = jax.random.normal(rng, dims, jnp.float32) * spread
    if len(shards) > 0:
        array = block_scale(rng, dims, shards, -0.22, 0.18) * array
    return jnp.clip(array, min=-most, max=most).astype(held_as)


def setup_inputs(seed: int = 0, part: int = 0) -> dict:
    key_list = jax.random.split(jax.random.key(seed), 4)
    own_keys = jax.random.split(jax.random.fold_in(key_list[3], part), 4)
    snapshots = centred(own_keys[0], (NB, NFFT, P_SIZE), 1.0, 6.0, ((0, 4), (2, 4)))
    weights = jnp.clip(jnp.exp(math.log(2.5) - 2.3025851 * jax.random.uniform(own_keys[1], (P_SIZE,), jnp.float32) ** block_scale(own_keys[1], (P_SIZE,), ((0, 4),), -0.2, 0.2)), 0.25, 2.5)
    triads = draw_triads(jax.random.fold_in(key_list[3], 71), part)
    return dict(snapshots=snapshots, weights=weights, triads=triads)


def make_table():
    time_steps = jnp.arange(NFFT, dtype=jnp.int32)
    frequency = jnp.arange(NF, dtype=jnp.int32)
    phase_index = frequency[:, None] * time_steps[None, :] % NFFT
    angle_grid = phase_index.astype(jnp.float32) * (2.0 * math.pi / NFFT)
    hann_window = 0.5 - 0.5 * jnp.cos(time_steps.astype(jnp.float32) * (2.0 * math.pi / NFFT))
    gain_factor = 1.0 / math.sqrt(3.0 * NFFT / 8.0)
    cos_rows = hann_window[None, :] * jnp.cos(angle_grid) * gain_factor
    sin_rows = -hann_window[None, :] * jnp.sin(angle_grid) * gain_factor
    return jnp.concatenate([cos_rows, sin_rows], axis=0).astype(jnp.bfloat16)

def triad_block(spectra_grid, weights, triad_block_ids):
    first_freq = triad_block_ids[:, 0]
    second_freq = triad_block_ids[:, 1]
    third_freq = first_freq + second_freq
    first_spec = jnp.take(spectra_grid, first_freq, axis=2).astype(jnp.float32)
    second_spec = jnp.take(spectra_grid, second_freq, axis=2).astype(jnp.float32)
    third_spec = jnp.take(spectra_grid, third_freq, axis=2)
    prod_re = weights * (first_spec[:, 0] * second_spec[:, 0] - first_spec[:, 1] * second_spec[:, 1])
    prod_im = weights * (first_spec[:, 0] * second_spec[:, 1] + first_spec[:, 1] * second_spec[:, 0])
    field_a = jnp.stack([prod_re, prod_im], axis=1).astype(jnp.bfloat16)
    field_a = lax.optimization_barrier(field_a)
    products = jnp.einsum('ictx,jdtx->tcdij', field_a.astype(jnp.float32), third_spec.astype(jnp.float32))
    real_part = products[:, 0, 0] + products[:, 1, 1]
    imag_part = products[:, 0, 1] - products[:, 1, 0]
    stacked = jnp.stack([real_part, imag_part], axis=1)
    return stacked.reshape(triad_block_ids.shape[0], 2 * NB * NB)

def reference(snapshots, weights, triads):
    dft_table = make_table()

    def transform(block_data):
        return jnp.dot(dft_table, block_data, preferred_element_type=jnp.float32).astype(jnp.bfloat16)
    spectra = lax.map(transform, snapshots)
    spectra = lax.optimization_barrier(spectra)
    spectra_grid = spectra.reshape(NB, 2, NF, P_SIZE)
    point_scale = 1.0 / math.sqrt(P_SIZE)
    block_size = math.gcd(NTRI, 8)
    grouped = triads.reshape(NTRI // block_size, block_size, 2)

    def one_group(triad_block_ids):
        return triad_block(spectra_grid, weights, triad_block_ids) * point_scale
    result = lax.map(one_group, grouped)
    return result.reshape(NTRI, 2 * NB * NB)
```

```python
import functools
import math

import jax
import jax.numpy as jnp
from jax import lax
from jax.experimental import pallas as pl
from jax.experimental.pallas import tpu as pltpu
from jax.sharding import PartitionSpec as P

NB = 16
NF = 64
LANES = 128
PACK = 4


def make_table(length):
    time_steps = jnp.arange(length, dtype=jnp.int32)
    frequency = jnp.arange(NF, dtype=jnp.int32)
    phase_index = frequency[:, None] * time_steps[None, :] % length
    angle_grid = phase_index.astype(jnp.float32) * (2.0 * math.pi / length)
    hann_window = 0.5 - 0.5 * jnp.cos(time_steps.astype(jnp.float32) * (2.0 * math.pi / length))
    gain_factor = 1.0 / math.sqrt(3.0 * length / 8.0)
    cos_rows = hann_window[None, :] * jnp.cos(angle_grid) * gain_factor
    sin_rows = -hann_window[None, :] * jnp.sin(angle_grid) * gain_factor
    return jnp.concatenate([cos_rows, sin_rows], axis=0).astype(jnp.bfloat16)


def dft_kernel(count, where_ref, table_ref, *refs):
    table = table_ref[...]
    for source, target in zip(refs[:count], refs[count:]):
        for block in range(source.shape[0]):
            target[block] = jnp.dot(
                table, source[block], preferred_element_type=jnp.float32
            ).astype(jnp.bfloat16)


def dft_chunk(table, snapshots, where, slots, chunk, chunks, width):
    blocks, length, _ = snapshots.shape
    count = len(slots)

    def column(slot):
        return lambda i, where_ref: (0, 0, where_ref[slot] * chunks + chunk)

    return pl.pallas_call(
        functools.partial(dft_kernel, count),
        out_shape=[jax.ShapeDtypeStruct((blocks, 2 * NF, width), jnp.bfloat16)] * count,
        grid_spec=pltpu.PrefetchScalarGridSpec(
            num_scalar_prefetch=1,
            grid=(1,),
            in_specs=[pl.BlockSpec((2 * NF, length), lambda i, where_ref: (0, 0))]
            + [pl.BlockSpec((blocks, length, width), column(slot)) for slot in slots],
            out_specs=[pl.BlockSpec((blocks, 2 * NF, width), lambda i, where_ref: (0, 0, 0))]
            * count,
        ),
        cost_estimate=pl.CostEstimate(
            flops=4 * NF * length * width * blocks * count,
            bytes_accessed=count * blocks * width * (2 * length + 4 * NF),
            transcendentals=0,
        ),
    )(where, table, *([snapshots] * count))


def triad_kernel(count, has_prior, scale, ids_ref, group_ref, *refs):
    sources = refs[:count]
    weights_ref = refs[count]
    prior_ref = refs[count + 1] if has_prior else None
    out_ref, spec_ref, third_ref = refs[count + 1 + has_prior :]
    blocks, rows, width = sources[0].shape
    tiles = width // LANES

    for position, source in enumerate(sources):
        first = group_ref[position] * blocks
        for block in range(blocks):
            for tile in range(tiles):
                piece = source[block, :, tile * LANES : (tile + 1) * LANES].astype(jnp.float32)
                spec_ref[tile, pl.ds(first + block, rows, stride=NB), :] = piece

    def pack(freq, carry):
        for tile in range(tiles):
            lanes = slice(tile * LANES, (tile + 1) * LANES)
            for part in range(2):
                start = pl.multiple_of((freq + part * NF) * NB, NB)
                target = pl.multiple_of(freq * 2 * NB + part * NB, NB)
                third_ref[pl.ds(target, NB), lanes] = spec_ref[
                    tile, pl.ds(start, NB), :
                ].astype(jnp.bfloat16)
        return carry

    lax.fori_loop(0, NF, pack, 0, unroll=8)

    lane = lax.broadcasted_iota(jnp.int32, (NB, LANES), 1)
    lower = lane % (2 * NB) < NB

    def one_pack(group, carry):
        fields = []
        thirds = []
        for member in range(PACK):
            index = (group * PACK + member) * 2
            first = ids_ref[index]
            second = ids_ref[index + 1]
            third = first + second
            parts_re = []
            parts_im = []
            for tile in range(tiles):
                def load(freq, part):
                    start = pl.multiple_of((freq + part * NF) * NB, NB)
                    return spec_ref[tile, pl.ds(start, NB), :]

                weight = weights_ref[:, tile * LANES : (tile + 1) * LANES]
                first_re, first_im = load(first, 0), load(first, 1)
                second_re, second_im = load(second, 0), load(second, 1)
                parts_re.append(weight * (first_re * second_re - first_im * second_im))
                parts_im.append(weight * (first_re * second_im + first_im * second_re))
            fields.append(jnp.concatenate(parts_re, axis=1).astype(jnp.bfloat16))
            fields.append(jnp.concatenate(parts_im, axis=1).astype(jnp.bfloat16))
            start = pl.multiple_of(third * 2 * NB, 2 * NB)
            thirds.append(third_ref[pl.ds(start, 2 * NB), :])
        field = jnp.concatenate(fields, axis=0)
        other = jnp.concatenate(thirds, axis=0)
        product = lax.dot_general(
            field, other, (((1,), (1,)), ((), ())), preferred_element_type=jnp.float32
        )
        upper_rows = product[0:NB]
        lower_rows = product[NB : 2 * NB]
        for member in range(1, PACK):
            base = member * 2 * NB
            mine = lane >= member * 2 * NB
            upper_rows = jnp.where(mine, product[base : base + NB], upper_rows)
            lower_rows = jnp.where(mine, product[base + NB : base + 2 * NB], lower_rows)
        from_right = pltpu.roll(lower_rows, LANES - NB, 1)
        from_left = pltpu.roll(lower_rows, NB, 1)
        total = (upper_rows + jnp.where(lower, from_right, -from_left)) * scale
        if has_prior:
            total = total + prior_ref[group]
        out_ref[group] = total
        return carry

    lax.fori_loop(0, out_ref.shape[0], one_pack, 0, unroll=2)


def triad_chunk(ids, groups, sources, weights, chunk, prior, scale):
    count = len(sources)
    blocks, rows, width = sources[0].shape
    packs = ids.shape[0] // (2 * PACK)
    has_prior = prior is not None
    whole = lambda *shape: pl.BlockSpec(shape, lambda i, *_: (0,) * len(shape))
    operands = list(sources) + [weights] + ([prior] if has_prior else [])
    in_specs = [whole(blocks, rows, width)] * count
    in_specs.append(pl.BlockSpec((1, width), lambda i, *_: (0, chunk)))
    if has_prior:
        in_specs.append(whole(packs, NB, LANES))
    return pl.pallas_call(
        functools.partial(triad_kernel, count, int(has_prior), scale),
        out_shape=jax.ShapeDtypeStruct((packs, NB, LANES), jnp.float32),
        grid_spec=pltpu.PrefetchScalarGridSpec(
            num_scalar_prefetch=2,
            grid=(1,),
            in_specs=in_specs,
            out_specs=whole(packs, NB, LANES),
            scratch_shapes=[
                pltpu.VMEM((width // LANES, rows * NB, LANES), jnp.float32),
                pltpu.VMEM((rows * NB, width), jnp.bfloat16),
            ],
        ),
        cost_estimate=pl.CostEstimate(
            flops=packs * 2 * LANES * LANES * width,
            bytes_accessed=count * blocks * rows * width * 2,
            transcendentals=0,
        ),
    )(ids, groups, *operands)


def per_device(snapshots, weights, triads):
    blocks, length, points = snapshots.shape
    freqs, bands = lax.axis_size("freq"), lax.axis_size("band")
    shards = freqs * bands
    own_points = points // shards
    chunks = math.gcd(4, own_points // LANES)
    width = own_points // chunks
    scale = 1.0 / math.sqrt(points * lax.axis_size("space"))
    my_freq, my_band = lax.axis_index("freq"), lax.axis_index("band")
    step = jnp.arange(shards, dtype=jnp.int32)
    step_freq, step_band = step // bands, step % bands
    where = (my_freq + step_freq) % freqs * bands + (my_band + step_band) % bands
    origin = (my_freq + freqs - step_freq) % freqs * bands + (
        my_band + bands - step_band
    ) % bands
    table = make_table(length)
    ids = triads.reshape(-1)
    own_weights = lax.dynamic_slice_in_dim(
        weights, (my_freq * bands + my_band) * own_points, own_points
    ).reshape(1, own_points)

    def send(value, slot):
        if slot == 0:
            return value
        shift_freq, shift_band = divmod(slot, bands)
        pairs = [
            (f * bands + b, (f + shift_freq) % freqs * bands + (b + shift_band) % bands)
            for f in range(freqs)
            for b in range(bands)
        ]
        return lax.ppermute(value, ("freq", "band"), pairs)

    far = list(range(bands, shards))
    near = list(range(bands))
    received = [[None] * shards for _ in range(chunks)]
    for slots in (far, near):
        for chunk in range(chunks):
            outs = dft_chunk(table, snapshots, where, slots, chunk, chunks, width)
            for slot, value in zip(slots, outs):
                received[chunk][slot] = send(value, slot)
    total = None
    for chunk in range(chunks):
        total = triad_chunk(ids, origin, received[chunk], own_weights, chunk, total, scale)

    axes = ("space", "freq", "band")
    devices = lax.axis_size("space") * shards
    packs = total.shape[0]
    pieces = lax.all_to_all(total, axes, split_axis=0, concat_axis=0, tiled=True)
    mine = pieces.reshape(devices, packs // devices, NB, LANES).sum(axis=0)
    mine = mine.reshape(packs // devices, NB, PACK, 2, NB).transpose(0, 2, 3, 1, 4)
    return mine.reshape(packs // devices * PACK, 2 * NB * NB)


def solution(mesh):
    return jax.shard_map(
        per_device,
        mesh=mesh,
        in_specs=(P(("freq", "band"), None, ("groups", "space")), P(("groups", "space")), P()),
        out_specs=P(("groups", "space", "freq", "band"), None),
        check_vma=False,
    )
```

```python
import functools
import math

import jax
import jax.numpy as jnp
from jax import lax
from jax.experimental import pallas as pl
from jax.experimental.pallas import tpu as pltpu
from jax.sharding import PartitionSpec as P


NB = 16
NF = 64
LANES = 128
PACK = 4
MIB = 1 << 20


def make_table(length):
    row = lax.broadcasted_iota(jnp.int32, (2 * NF, length), 0)
    time = lax.broadcasted_iota(jnp.int32, (2 * NF, length), 1)
    phase = (row % NF * time + row // NF * (length // 4)) % length
    turn = 2.0 * math.pi / length
    window = 0.5 - 0.5 * jnp.cos(time.astype(jnp.float32) * turn)
    gain = 1.0 / math.sqrt(3.0 * length / 8.0)
    return (window * jnp.cos(phase.astype(jnp.float32) * turn) * gain).astype(jnp.bfloat16)


def split_widths(points):
    tiles = points // LANES
    first = max(1, tiles // 4)
    rest = tiles - first - 1
    middle = [(rest + 1) // 2, rest // 2] if rest > 2 else [rest]
    return [w * LANES for w in [first] + [m for m in middle if m > 0] + [1]]


def dft_first_kernel(where_ref, table_ref, *refs):
    table = table_ref[...]
    count = len(refs) // 2
    for source, target in zip(refs[:count], refs[count:]):
        for block in range(source.shape[0]):
            target[block] = jnp.dot(
                table, source[block], preferred_element_type=jnp.float32
            ).astype(jnp.bfloat16)


def dft_first(table, snapshots, where, slots, points, width):
    blocks, length, _ = snapshots.shape
    count = len(slots)

    def column(slot):
        return lambda i, where_ref: (0, 0, where_ref[slot] * (points // width))

    whole = lambda *shape: pl.BlockSpec(shape, lambda i, *_: (0,) * len(shape))
    return pl.pallas_call(
        dft_first_kernel,
        out_shape=[jax.ShapeDtypeStruct((blocks, 2 * NF, width), jnp.bfloat16)] * count,
        grid_spec=pltpu.PrefetchScalarGridSpec(
            num_scalar_prefetch=1,
            grid=(1,),
            in_specs=[whole(2 * NF, length)]
            + [pl.BlockSpec((blocks, length, width), column(slot)) for slot in slots],
            out_specs=[whole(blocks, 2 * NF, width)] * count,
        ),
        compiler_params=pltpu.CompilerParams(vmem_limit_bytes=16 * MIB),
        name="dft_first",
    )(where, table, *([snapshots] * count))


def dft_rest_kernel(plan, points, where_ref, table_ref, snap_ref, after_ref, *outs):
    table = table_ref[...]
    for (slot, offset, width), target in zip(plan, outs):
        step = math.gcd(width, 2 * LANES)
        for piece in range(0, width, step):
            start = pl.multiple_of(where_ref[slot] * points + (offset + piece), LANES)
            target[0, :, piece : piece + step] = jnp.dot(
                table, snap_ref[0, :, pl.ds(start, step)], preferred_element_type=jnp.float32
            ).astype(jnp.bfloat16)


def dft_rest(table, snapshots, where, plan, points, after):
    blocks, length, columns = snapshots.shape
    return pl.pallas_call(
        functools.partial(dft_rest_kernel, plan, points),
        out_shape=[
            jax.ShapeDtypeStruct((blocks, 2 * NF, width), jnp.bfloat16) for _, _, width in plan
        ],
        grid_spec=pltpu.PrefetchScalarGridSpec(
            num_scalar_prefetch=1,
            grid=(blocks,),
            in_specs=[
                pl.BlockSpec((2 * NF, length), lambda i, *_: (0, 0)),
                pl.BlockSpec((1, length, columns), lambda i, *_: (i, 0, 0)),
                pl.BlockSpec(memory_space=pl.ANY),
            ],
            out_specs=[
                pl.BlockSpec((1, 2 * NF, width), lambda i, *_: (i, 0, 0)) for _, _, width in plan
            ],
        ),
        compiler_params=pltpu.CompilerParams(vmem_limit_bytes=16 * MIB),
        cost_estimate=pl.CostEstimate(
            flops=4 * NF * length * columns * blocks,
            bytes_accessed=blocks * columns * (2 * length + 4 * NF),
            transcendentals=0,
        ),
        name="dft_rest",
    )(where, table, snapshots, after)


def triad_kernel(near, offset, has_prior, scale, ids_ref, group_ref, *refs):
    spec_ref = refs[-1]
    out_ref = refs[-2]
    sources = refs[: -3 - has_prior]
    weights_ref = refs[len(sources)]
    prior_ref = refs[len(sources) + 1] if has_prior else None
    blocks, rows, width = sources[-1].shape
    tiles = width // LANES

    for position, source in enumerate(sources):
        base = offset if position < near else 0
        first = group_ref[position] * blocks
        for block in range(blocks):
            for tile in range(tiles):
                lanes = slice(base + tile * LANES, base + (tile + 1) * LANES)
                spec_ref[tile, pl.ds(first + block, rows, stride=NB), :] = source[
                    block, :, lanes
                ].astype(jnp.float32)

    lane = lax.broadcasted_iota(jnp.int32, (NB, LANES), 1)
    lower = lane % (2 * NB) < NB

    def one_pack(group, carry):
        fields = []
        thirds = []
        for member in range(PACK):
            index = (group * PACK + member) * 2
            first = ids_ref[index]
            second = ids_ref[index + 1]
            third = first + second
            field_re, field_im, third_re, third_im = [], [], [], []
            for tile in range(tiles):
                def load(freq, part):
                    start = pl.multiple_of((freq + part * NF) * NB, NB)
                    return spec_ref[tile, pl.ds(start, NB), :]

                lanes = slice(offset + tile * LANES, offset + (tile + 1) * LANES)
                weight = weights_ref[:, lanes]
                first_re, first_im = load(first, 0), load(first, 1)
                second_re, second_im = load(second, 0), load(second, 1)
                field_re.append(weight * (first_re * second_re - first_im * second_im))
                field_im.append(weight * (first_re * second_im + first_im * second_re))
                third_re.append(load(third, 0))
                third_im.append(load(third, 1))
            for parts, rows_of in (
                (field_re, fields), (field_im, fields), (third_re, thirds), (third_im, thirds)
            ):
                rows_of.append(jnp.concatenate(parts, axis=1).astype(jnp.bfloat16))
        product = lax.dot_general(
            jnp.concatenate(fields, axis=0),
            jnp.concatenate(thirds, axis=0),
            (((1,), (1,)), ((), ())),
            preferred_element_type=jnp.float32,
        )
        upper_rows = product[0:NB]
        lower_rows = product[NB : 2 * NB]
        for member in range(1, PACK):
            base = member * 2 * NB
            mine = lane >= base
            upper_rows = jnp.where(mine, product[base : base + NB], upper_rows)
            lower_rows = jnp.where(mine, product[base + NB : base + 2 * NB], lower_rows)
        from_right = pltpu.roll(lower_rows, LANES - NB, 1)
        from_left = pltpu.roll(lower_rows, NB, 1)
        total = (upper_rows + jnp.where(lower, from_right, -from_left)) * scale
        if has_prior:
            total = total + prior_ref[group]
        out_ref[group] = total
        return carry

    lax.fori_loop(0, out_ref.shape[0], one_pack, 0, unroll=4)


def triad_chunk(ids, groups, near_sources, far_sources, weights, offset, prior, scale):
    _, rows, width = far_sources[0].shape
    packs = ids.shape[0] // (2 * PACK)
    vmem = pl.BlockSpec(memory_space=pltpu.VMEM)
    smem = pl.BlockSpec(memory_space=pltpu.SMEM)
    operands = list(near_sources) + list(far_sources) + [weights]
    if prior is not None:
        operands.append(prior)
    return pl.pallas_call(
        functools.partial(
            triad_kernel, len(near_sources), offset, int(prior is not None), scale
        ),
        out_shape=jax.ShapeDtypeStruct((packs, NB, LANES), jnp.float32),
        in_specs=[smem, smem] + [vmem] * len(operands),
        out_specs=vmem,
        scratch_shapes=[pltpu.VMEM((width // LANES, rows * NB, LANES), jnp.float32)],
        compiler_params=pltpu.CompilerParams(vmem_limit_bytes=16 * MIB),
        cost_estimate=pl.CostEstimate(
            flops=packs * 2 * LANES * LANES * width,
            bytes_accessed=NB * rows * width * 2,
            transcendentals=0,
        ),
        name="triads",
    )(ids, groups, *operands)


def mode_decomposition(snapshots, weights, triads):
    length, points = snapshots.shape[1:]
    snapshots = pltpu.with_memory_space_constraint(snapshots, pltpu.HBM)
    freqs, bands = lax.axis_size("freq"), lax.axis_size("band")
    shards = freqs * bands
    own_points = points // shards
    widths = split_widths(own_points)
    offsets = [sum(widths[:i]) for i in range(len(widths))]
    scale = 1.0 / math.sqrt(points * lax.axis_size("space"))
    my_freq, my_band = lax.axis_index("freq"), lax.axis_index("band")
    step = jnp.arange(shards, dtype=jnp.int32)
    step_freq, step_band = step // bands, step % bands
    where = (my_freq + step_freq) % freqs * bands + (my_band + step_band) % bands
    origin = (my_freq + freqs - step_freq) % freqs * bands + (
        my_band + bands - step_band
    ) % bands
    table = make_table(length)
    ids = triads.reshape(-1)
    own_weights = lax.dynamic_slice_in_dim(
        weights, (my_freq * bands + my_band) * own_points, own_points
    ).reshape(1, own_points)

    def send(value, slot):
        if slot == 0:
            return value
        shift_freq, shift_band = divmod(slot, bands)
        pairs = [
            (f * bands + b, (f + shift_freq) % freqs * bands + (b + shift_band) % bands)
            for f in range(freqs)
            for b in range(bands)
        ]
        return lax.ppermute(value, ("freq", "band"), pairs)

    near = list(range(bands))
    far = list(range(bands, shards))
    firsts = dft_first(table, snapshots, where, far, own_points, widths[0])
    far_arrived = [[send(value, slot) for slot, value in zip(far, firsts)]]
    plan = [
        (slot, offset, width)
        for offset, width in list(zip(offsets, widths))[1:]
        for slot in far
    ] + [(slot, 0, own_points) for slot in near]
    rest = dft_rest(table, snapshots, where, plan, own_points, firsts[0])
    for chunk in range(1, len(widths)):
        base = (chunk - 1) * len(far)
        far_arrived.append(
            [send(value, slot) for slot, value in zip(far, rest[base : base + len(far)])]
        )
    near_arrived = [send(value, slot) for slot, value in zip(near, rest[-len(near) :])]

    total = None
    for chunk, offset in enumerate(offsets):
        total = triad_chunk(
            ids, origin, near_arrived, far_arrived[chunk], own_weights, offset, total, scale
        )

    axes = ("space", "freq", "band")
    devices = lax.axis_size("space") * shards
    packs = total.shape[0]
    pieces = lax.all_to_all(total, axes, split_axis=0, concat_axis=0, tiled=True)
    mine = pieces.reshape(devices, packs // devices, NB, LANES).sum(axis=0)
    mine = mine.reshape(packs // devices, NB, PACK, 2, NB).transpose(0, 2, 3, 1, 4)
    return mine.reshape(packs // devices * PACK, 2 * NB * NB)


def solution(mesh):
    return jax.shard_map(
        mode_decomposition,
        mesh=mesh,
        in_specs=(P(("freq", "band"), None, ("groups", "space")), P(("groups", "space")), P()),
        out_specs=P(("groups", "space", "freq", "band"), None),
        check_vma=False,
    )
```

```python
import functools
import math

import jax
import jax.numpy as jnp
from jax import lax
from jax.experimental import pallas as pl
from jax.experimental.pallas import tpu as pltpu
from jax.sharding import PartitionSpec as P


NB = 16
NF = 64
LANES = 128
PACK = 4
MIB = 1 << 20


VMEM = pl.BlockSpec(memory_space=pltpu.VMEM)
ANY = pl.BlockSpec(memory_space=pl.ANY)


def split_widths(points):
    tiles = points // LANES
    rest = max(0, tiles - 2)
    count = -(-rest // 2)
    middle = [rest // count + (i < rest % count) for i in range(count)] if count else []
    return [w * LANES for w in ([1] if tiles > 1 else []) + middle + [1]]


def make_table(length):
    turn = 2.0 * math.pi / length
    gain = 1.0 / math.sqrt(3.0 * length / 8.0)
    time = lax.broadcasted_iota(jnp.int32, (8, length), 1)
    window = (0.5 - 0.5 * jnp.cos(time.astype(jnp.float32) * turn)) * gain
    row = lax.broadcasted_iota(jnp.int32, (2 * NF, length), 0)
    time = lax.broadcasted_iota(jnp.int32, (2 * NF, length), 1)
    phase = (row & (NF - 1)) * time + jnp.where(row < NF, 0, length // 4)
    phase = phase & (length - 1) if length & (length - 1) == 0 else phase % length
    wave = jnp.cos(phase.astype(jnp.float32) * turn)
    return (jnp.concatenate([window] * (NF // 4), axis=0) * wave).astype(jnp.bfloat16)


def shifted_part(slot, sign, freqs, bands):
    step_freq, step_band = divmod(slot, bands)
    freq = lax.axis_index("freq") + (step_freq if sign > 0 else freqs - step_freq)
    band = lax.axis_index("band") + (step_band if sign > 0 else bands - step_band)
    return lax.rem(freq, freqs) * bands + lax.rem(band, bands)


def dft_far_kernel(sizes, far, points, offset, own_table, *refs):
    count = len(far)
    snap_ref = refs[0]
    outs = refs[len(refs) - 2 - count : len(refs) - 2]
    buffer, arrived = refs[-2:]
    blocks, length, width = buffer.shape[1:]
    copies = []
    for position, slot in enumerate(far):
        start = shifted_part(slot, 1, *sizes) * points + offset
        for block in range(blocks):
            copy = pltpu.make_async_copy(
                snap_ref.at[block, :, pl.ds(pl.multiple_of(start, LANES), width)],
                buffer.at[position, block],
                arrived.at[position, block],
            )
            copy.start()
            copies.append(copy)
    if own_table:
        table_ref = refs[1]
        table_ref[...] = make_table(length)
    else:
        table_ref = refs[1]
    table = table_ref[...]
    for position in range(count):
        for block in range(blocks):
            copies[position * blocks + block].wait()
            outs[position][block] = jnp.dot(
                table, buffer[position, block], preferred_element_type=jnp.float32
            ).astype(jnp.bfloat16)


def dft_far(snapshots, table, sizes, far, points, offset, width):
    blocks, length, _ = snapshots.shape
    count = len(far)
    own_table = table is None
    out_shape = [jax.ShapeDtypeStruct((blocks, 2 * NF, width), jnp.bfloat16)] * count
    if own_table:
        out_shape = [jax.ShapeDtypeStruct((2 * NF, length), jnp.bfloat16)] + out_shape
    return pl.pallas_call(
        functools.partial(dft_far_kernel, sizes, far, points, offset, own_table),
        out_shape=out_shape,
        in_specs=[ANY] + ([] if own_table else [VMEM]),
        out_specs=[VMEM] * len(out_shape),
        scratch_shapes=[
            pltpu.VMEM((count, blocks, length, width), jnp.bfloat16),
            pltpu.SemaphoreType.DMA((count, blocks)),
        ],
        compiler_params=pltpu.CompilerParams(vmem_limit_bytes=8 * MIB),
        name="dft_far",
    )(snapshots, *([] if own_table else [table]))


def dft_rest_kernel(sizes, plan, points, table_ref, snap_ref, after_ref, *outs):
    table = table_ref[...]
    for (slot, offset, width), target in zip(plan, outs):
        step = math.gcd(width, 2 * LANES)
        part = shifted_part(slot, 1, *sizes) * points
        for piece in range(0, width, step):
            start = pl.multiple_of(part + (offset + piece), LANES)
            target[0, :, piece : piece + step] = jnp.dot(
                table, snap_ref[0, :, pl.ds(start, step)], preferred_element_type=jnp.float32
            ).astype(jnp.bfloat16)


def dft_rest(snapshots, table, sizes, plan, points, after):
    blocks, length, columns = snapshots.shape
    return pl.pallas_call(
        functools.partial(dft_rest_kernel, sizes, plan, points),
        out_shape=[
            jax.ShapeDtypeStruct((blocks, 2 * NF, width), jnp.bfloat16) for _, _, width in plan
        ],
        grid=(blocks,),
        in_specs=[
            pl.BlockSpec((2 * NF, length), lambda i: (0, 0)),
            pl.BlockSpec((1, length, columns), lambda i: (i, 0, 0)),
            ANY,
        ],
        out_specs=[pl.BlockSpec((1, 2 * NF, width), lambda i: (i, 0, 0)) for _, _, width in plan],
        compiler_params=pltpu.CompilerParams(vmem_limit_bytes=16 * MIB),
        cost_estimate=pl.CostEstimate(
            flops=4 * NF * length * columns * blocks,
            bytes_accessed=blocks * columns * (2 * length + 4 * NF),
            transcendentals=0,
        ),
        name="dft_rest",
    )(table, snapshots, after)


def interleave(spec_ref, source, slot, sizes, base):
    blocks, rows, _ = source.shape
    first = shifted_part(slot, -1, *sizes) * blocks
    for block in range(blocks):
        for tile in range(spec_ref.shape[0]):
            lanes = slice(base + tile * LANES, base + (tile + 1) * LANES)
            spec_ref[tile, pl.ds(first + block, rows, stride=NB), :] = source[
                block, :, lanes
            ].astype(jnp.float32)


def prepare_kernel(sizes, near, offset, *refs):
    for slot, source in zip(near, refs[:-1]):
        interleave(refs[-1], source, slot, sizes, offset)


def prepare(near_sources, sizes, near, offset, width):
    rows = near_sources[0].shape[1]
    return pl.pallas_call(
        functools.partial(prepare_kernel, sizes, near, offset),
        out_shape=jax.ShapeDtypeStruct((width // LANES, rows * NB, LANES), jnp.float32),
        in_specs=[VMEM] * len(near),
        out_specs=VMEM,
        compiler_params=pltpu.CompilerParams(vmem_limit_bytes=8 * MIB),
        name="prepare",
    )(*near_sources)


def triad_kernel(sizes, slots, offset, prepared, has_prior, scale, *refs):
    ids_any, weights_ref = refs[:2]
    rest = list(refs[2:])
    prior_ref = rest.pop(0) if has_prior else None
    if prepared:
        rest.pop(0)
    sources = [rest.pop(0) for _ in slots]
    out_ref, spec_ref, ids_ref, ids_arrived = rest
    ids_copy = pltpu.make_async_copy(ids_any, ids_ref, ids_arrived)
    ids_copy.start()
    tiles = spec_ref.shape[0]
    own_points = weights_ref.shape[1] // (sizes[0] * sizes[1])
    here = shifted_part(0, 1, *sizes) * own_points + offset

    for (slot, base), source in zip(slots, sources):
        interleave(spec_ref, source, slot, sizes, base)
    weights = [
        weights_ref[:, pl.ds(pl.multiple_of(here + tile * LANES, LANES), LANES)]
        for tile in range(tiles)
    ]
    ids_copy.wait()
    lane = lax.broadcasted_iota(jnp.int32, (NB, LANES), 1)

    def one_pack(group, carry):
        fields = []
        thirds = []
        for member in range(PACK):
            index = (group * PACK + member) * 2
            first = ids_ref[index]
            second = ids_ref[index + 1]
            third = first + second
            field_re, field_im, third_re, third_im, third_neg = [], [], [], [], []
            for tile in range(tiles):
                def load(freq, part):
                    start = pl.multiple_of((freq + part * NF) * NB, NB)
                    return spec_ref[tile, pl.ds(start, NB), :]

                first_re, first_im = load(first, 0), load(first, 1)
                second_re, second_im = load(second, 0), load(second, 1)
                weight = weights[tile]
                field_re.append(weight * (first_re * second_re - first_im * second_im))
                field_im.append(weight * (first_re * second_im + first_im * second_re))
                third_re.append(load(third, 0))
                third_im.append(load(third, 1))
                third_neg.append(-third_re[-1])
            for parts, rows_of in (
                (field_re + field_im, fields),
                (third_re + third_im, thirds),
                (third_im + third_neg, thirds),
            ):
                rows_of.append(jnp.concatenate(parts, axis=1).astype(jnp.bfloat16))
        product = lax.dot_general(
            jnp.concatenate(fields, axis=0),
            jnp.concatenate(thirds, axis=0),
            (((1,), (1,)), ((), ())),
            preferred_element_type=jnp.float32,
        )
        total = product[0:NB]
        for member in range(1, PACK):
            total = jnp.where(
                lane >= member * 2 * NB, product[member * NB : (member + 1) * NB], total
            )
        total = total * scale
        if has_prior:
            total = total + prior_ref[group]
        out_ref[group] = total
        return carry

    lax.fori_loop(0, out_ref.shape[0], one_pack, 0, unroll=4)


def triad_chunk(ids, weights, sources, slots, sizes, offset, width, prior, scale, prepared=None):
    rows = sources[0].shape[1]
    packs = ids.shape[0] // (2 * PACK)
    spec_shape = (width // LANES, rows * NB, LANES)
    operands = [ids, weights] + ([] if prior is None else [prior])
    aliases = {}
    out_shape = [jax.ShapeDtypeStruct((packs, NB, LANES), jnp.float32)]
    scratch = [pltpu.SMEM(ids.shape, jnp.int32), pltpu.SemaphoreType.DMA]
    if prepared is None:
        scratch = [pltpu.VMEM(spec_shape, jnp.float32)] + scratch
    else:
        aliases = {len(operands): 1}
        operands.append(prepared)
        out_shape.append(jax.ShapeDtypeStruct(spec_shape, jnp.float32))
    operands += sources
    return pl.pallas_call(
        functools.partial(
            triad_kernel, sizes, slots, offset, prepared is not None, prior is not None, scale
        ),
        out_shape=out_shape,
        in_specs=[ANY] + [VMEM] * (len(operands) - 1),
        out_specs=[VMEM] * len(out_shape),
        scratch_shapes=scratch,
        input_output_aliases=aliases,
        compiler_params=pltpu.CompilerParams(vmem_limit_bytes=8 * MIB),
        cost_estimate=pl.CostEstimate(
            flops=packs * 2 * LANES * LANES * width,
            bytes_accessed=NB * rows * width * 2,
            transcendentals=0,
        ),
        name="triads",
    )(*operands)[0]


def mode_decomposition(snapshots, weights, triads):
    points = snapshots.shape[2]
    snapshots = pltpu.with_memory_space_constraint(snapshots, pltpu.HBM)
    freqs, bands = sizes = lax.axis_size("freq"), lax.axis_size("band")
    shards = freqs * bands
    own_points = points // shards
    widths = split_widths(own_points)
    offsets = [sum(widths[:i]) for i in range(len(widths))]
    scale = 1.0 / math.sqrt(points * lax.axis_size("space"))
    ids = triads.reshape(-1)
    weights = weights.reshape(1, points)

    def send(value, slot):
        if slot == 0:
            return value
        shift_freq, shift_band = divmod(slot, bands)
        pairs = [
            (f * bands + b, (f + shift_freq) % freqs * bands + (b + shift_band) % bands)
            for f in range(freqs)
            for b in range(bands)
        ]
        return lax.ppermute(value, ("freq", "band"), pairs)

    def send_all(values, slots):
        return [send(value, slot) for slot, value in zip(slots, values)]

    near = list(range(bands))
    far = list(range(bands, shards))
    table, *outs = dft_far(snapshots, None, sizes, far, own_points, 0, widths[0])
    arrived = [send_all(outs, far)]
    outs = dft_far(snapshots, table, sizes, far, own_points, offsets[1], widths[1])
    arrived.append(send_all(outs, far))
    plan = [
        (slot, offset, width)
        for offset, width in list(zip(offsets, widths))[2:]
        for slot in far
    ] + [(slot, 0, own_points) for slot in near]
    rest = dft_rest(snapshots, table, sizes, plan, own_points, outs[0])
    for _ in range(2, len(widths)):
        arrived.append(send_all(rest[: len(far)], far))
        rest = rest[len(far) :]
    near_sources = send_all(rest, near)

    total = None
    for chunk, (offset, width) in enumerate(zip(offsets, widths)):
        slots = [(slot, 0) for slot in far]
        sources = arrived[chunk]
        prepared = None
        if chunk == len(widths) - 1:
            prepared = prepare(near_sources, sizes, near, offset, width)
        else:
            slots = [(slot, offset) for slot in near] + slots
            sources = near_sources + sources
        total = triad_chunk(
            ids, weights, sources, slots, sizes, offset, width, total, scale, prepared
        )

    axes = ("space", "freq", "band")
    devices = lax.axis_size("space") * shards
    packs = total.shape[0]
    pieces = lax.all_to_all(total, axes, split_axis=0, concat_axis=0, tiled=True)
    mine = pieces.reshape(devices, packs // devices, NB, LANES).sum(axis=0)
    mine = mine.reshape(packs // devices, NB, PACK, 2, NB).transpose(0, 2, 3, 1, 4)
    return mine.reshape(packs // devices * PACK, 2 * NB * NB)


def solution(mesh):
    return jax.shard_map(
        mode_decomposition,
        mesh=mesh,
        in_specs=(P(("freq", "band"), None, ("groups", "space")), P(("groups", "space")), P()),
        out_specs=P(("groups", "space", "freq", "band"), None),
        check_vma=False,
    )
```

```python
import functools
import math

import jax
import jax.numpy as jnp
from jax import lax
from jax.experimental import pallas as pl
from jax.experimental.pallas import tpu as pltpu
from jax.sharding import PartitionSpec as P


NB = 16
NF = 64
LANES = 128
PACK = 4
MIB = 1 << 20


VMEM = pl.BlockSpec(memory_space=pltpu.VMEM)
ANY = pl.BlockSpec(memory_space=pl.ANY)


def split_widths(points):
    tiles = points // LANES
    first = max(1, tiles // 4)
    rest = tiles - first - 1
    count = max(1, -(-rest // 3))
    middle = [rest // count + (i < rest % count) for i in range(count)]
    return [w * LANES for w in [first] + middle + [1]]


def make_table(length):
    turn = 2.0 * math.pi / length
    gain = 1.0 / math.sqrt(3.0 * length / 8.0)
    quarter = length // 4

    def cosine(phase):
        moved = phase + quarter // 2
        quadrant = lax.div(moved, quarter) & 3
        angle = (lax.rem(moved, quarter) - quarter // 2).astype(jnp.float32) * turn
        square = angle * angle
        even = 1.0 + square * (
            -1 / 2 + square * (1 / 24 + square * (-1 / 720 + square * (1 / 40320)))
        )
        odd = angle * (
            1.0 + square * (-1 / 6 + square * (1 / 120 + square * (-1 / 5040 + square / 362880)))
        )
        value = jnp.where(quadrant & 1 == 0, even, odd)
        return jnp.where((quadrant == 1) | (quadrant == 2), -value, value)

    time = lax.broadcasted_iota(jnp.int32, (8, length), 1)
    window = (0.5 - 0.5 * cosine(time)) * gain
    row = lax.broadcasted_iota(jnp.int32, (2 * NF, length), 0)
    time = lax.broadcasted_iota(jnp.int32, (2 * NF, length), 1)
    wave = cosine((row & (NF - 1)) * time + jnp.where(row < NF, 0, quarter))
    return (jnp.concatenate([window] * (NF // 4), axis=0) * wave).astype(jnp.bfloat16)


def shifted_part(slot, sign, freqs, bands):
    step_freq, step_band = divmod(slot, bands)
    freq = lax.axis_index("freq") + (step_freq if sign > 0 else freqs - step_freq)
    band = lax.axis_index("band") + (step_band if sign > 0 else bands - step_band)
    return lax.rem(freq, freqs) * bands + lax.rem(band, bands)


def dft_far_kernel(sizes, far, points, offset, own_table, *refs):
    count = len(far)
    snap_ref = refs[0]
    outs = refs[len(refs) - 2 - count : len(refs) - 2]
    buffer, arrived = refs[-2:]
    blocks, length, width = buffer.shape[1:]
    copies = []
    for position, slot in enumerate(far):
        start = shifted_part(slot, 1, *sizes) * points + offset
        for block in range(blocks):
            copy = pltpu.make_async_copy(
                snap_ref.at[block, :, pl.ds(pl.multiple_of(start, LANES), width)],
                buffer.at[position, block],
                arrived.at[position, block],
            )
            copy.start()
            copies.append(copy)
    if own_table:
        table_ref = refs[1]
        table_ref[...] = make_table(length)
    else:
        table_ref = refs[1]
    table = table_ref[...]
    for position in range(count):
        for block in range(blocks):
            copies[position * blocks + block].wait()
            outs[position][block] = jnp.dot(
                table, buffer[position, block], preferred_element_type=jnp.float32
            ).astype(jnp.bfloat16)


def dft_far(snapshots, table, sizes, far, points, offset, width):
    blocks, length, _ = snapshots.shape
    count = len(far)
    own_table = table is None
    out_shape = [pltpu.VMEM((blocks, 2 * NF, width), jnp.bfloat16)] * count
    if own_table:
        out_shape = [pltpu.VMEM((2 * NF, length), jnp.bfloat16)] + out_shape
    return pl.pallas_call(
        functools.partial(dft_far_kernel, sizes, far, points, offset, own_table),
        out_shape=out_shape,
        in_specs=[ANY] + ([] if own_table else [VMEM]),
        out_specs=[VMEM] * len(out_shape),
        scratch_shapes=[
            pltpu.VMEM((count, blocks, length, width), jnp.bfloat16),
            pltpu.SemaphoreType.DMA((count, blocks)),
        ],
        compiler_params=pltpu.CompilerParams(vmem_limit_bytes=8 * MIB),
        name="dft_far",
    )(snapshots, *([] if own_table else [table]))


def dft_rest_kernel(sizes, plan, points, table_ref, snap_ref, after_ref, *outs):
    table = table_ref[...]
    for (slot, offset, width), target in zip(plan, outs):
        step = math.gcd(width, 2 * LANES)
        part = shifted_part(slot, 1, *sizes) * points
        for piece in range(0, width, step):
            start = pl.multiple_of(part + (offset + piece), LANES)
            target[0, :, piece : piece + step] = jnp.dot(
                table, snap_ref[0, :, pl.ds(start, step)], preferred_element_type=jnp.float32
            ).astype(jnp.bfloat16)


def dft_rest(snapshots, table, sizes, plan, points, after):
    blocks, length, columns = snapshots.shape
    return pl.pallas_call(
        functools.partial(dft_rest_kernel, sizes, plan, points),
        out_shape=[
            jax.ShapeDtypeStruct((blocks, 2 * NF, width), jnp.bfloat16) for _, _, width in plan
        ],
        grid=(blocks,),
        in_specs=[
            pl.BlockSpec((2 * NF, length), lambda i: (0, 0)),
            pl.BlockSpec((1, length, columns), lambda i: (i, 0, 0)),
            ANY,
        ],
        out_specs=[pl.BlockSpec((1, 2 * NF, width), lambda i: (i, 0, 0)) for _, _, width in plan],
        compiler_params=pltpu.CompilerParams(vmem_limit_bytes=16 * MIB),
        cost_estimate=pl.CostEstimate(
            flops=4 * NF * length * columns * blocks,
            bytes_accessed=blocks * columns * (2 * length + 4 * NF),
            transcendentals=0,
        ),
        name="dft_rest",
    )(table, snapshots, after)


def interleave(spec_ref, source, slot, sizes, base):
    blocks, rows, _ = source.shape
    first = shifted_part(slot, -1, *sizes) * blocks
    for block in range(blocks):
        for tile in range(spec_ref.shape[0]):
            lanes = slice(base + tile * LANES, base + (tile + 1) * LANES)
            spec_ref[tile, pl.ds(first + block, rows, stride=NB), :] = source[
                block, :, lanes
            ].astype(jnp.float32)


def prepare_kernel(sizes, near, offset, *refs):
    for slot, source in zip(near, refs[:-1]):
        interleave(refs[-1], source, slot, sizes, offset)


def prepare(near_sources, sizes, near, offset, width):
    rows = near_sources[0].shape[1]
    return pl.pallas_call(
        functools.partial(prepare_kernel, sizes, near, offset),
        out_shape=jax.ShapeDtypeStruct((width // LANES, rows * NB, LANES), jnp.float32),
        in_specs=[VMEM] * len(near),
        out_specs=VMEM,
        compiler_params=pltpu.CompilerParams(vmem_limit_bytes=8 * MIB),
        name="prepare",
    )(*near_sources)


def triad_kernel(sizes, slots, offset, prepared, has_prior, scale, *refs):
    ids_any, weights_ref = refs[:2]
    rest = list(refs[2:])
    prior_ref = rest.pop(0) if has_prior else None
    if prepared:
        rest.pop(0)
    sources = [rest.pop(0) for _ in slots]
    out_ref, spec_ref, ids_ref, ids_arrived = rest
    ids_copy = pltpu.make_async_copy(ids_any, ids_ref, ids_arrived)
    ids_copy.start()
    tiles = spec_ref.shape[0]
    own_points = weights_ref.shape[1] // (sizes[0] * sizes[1])
    here = shifted_part(0, 1, *sizes) * own_points + offset

    for (slot, base), source in zip(slots, sources):
        interleave(spec_ref, source, slot, sizes, base)
    weights = [
        weights_ref[:, pl.ds(pl.multiple_of(here + tile * LANES, LANES), LANES)]
        for tile in range(tiles)
    ]
    ids_copy.wait()
    lane = lax.broadcasted_iota(jnp.int32, (NB, LANES), 1)

    def one_pack(group, carry):
        fields = []
        thirds = []
        for member in range(PACK):
            first = ids_ref[0, group * PACK + member]
            second = ids_ref[1, group * PACK + member]
            third = first + second
            field_re, field_im, third_re, third_im, third_neg = [], [], [], [], []
            for tile in range(tiles):
                def load(freq, part):
                    start = pl.multiple_of((freq + part * NF) * NB, NB)
                    return spec_ref[tile, pl.ds(start, NB), :]

                first_re, first_im = load(first, 0), load(first, 1)
                second_re, second_im = load(second, 0), load(second, 1)
                weight = weights[tile]
                field_re.append(weight * (first_re * second_re - first_im * second_im))
                field_im.append(weight * (first_re * second_im + first_im * second_re))
                third_re.append(load(third, 0))
                third_im.append(load(third, 1))
                third_neg.append(-third_re[-1])
            for parts, rows_of in (
                (field_re + field_im, fields),
                (third_re + third_im, thirds),
                (third_im + third_neg, thirds),
            ):
                rows_of.append(jnp.concatenate(parts, axis=1).astype(jnp.bfloat16))
        product = lax.dot_general(
            jnp.concatenate(fields, axis=0),
            jnp.concatenate(thirds, axis=0),
            (((1,), (1,)), ((), ())),
            preferred_element_type=jnp.float32,
        )
        total = product[0:NB]
        for member in range(1, PACK):
            total = jnp.where(
                lane >= member * 2 * NB, product[member * NB : (member + 1) * NB], total
            )
        total = total * scale
        if has_prior:
            total = total + prior_ref[group]
        out_ref[group] = total
        return carry

    lax.fori_loop(0, out_ref.shape[0], one_pack, 0, unroll=4)


def triad_chunk(ids, weights, sources, slots, sizes, offset, width, prior, scale, prepared=None):
    rows = sources[0].shape[1]
    packs = ids.shape[1] // PACK
    spec_shape = (width // LANES, rows * NB, LANES)
    operands = [ids, weights] + ([] if prior is None else [prior])
    aliases = {}
    out_shape = [jax.ShapeDtypeStruct((packs, NB, LANES), jnp.float32)]
    scratch = [pltpu.SMEM(ids.shape, jnp.int32), pltpu.SemaphoreType.DMA]
    if prepared is None:
        scratch = [pltpu.VMEM(spec_shape, jnp.float32)] + scratch
    else:
        aliases = {len(operands): 1}
        operands.append(prepared)
        out_shape.append(jax.ShapeDtypeStruct(spec_shape, jnp.float32))
    operands += [pltpu.with_memory_space_constraint(x, pltpu.VMEM) for x in sources]
    return pl.pallas_call(
        functools.partial(
            triad_kernel, sizes, slots, offset, prepared is not None, prior is not None, scale
        ),
        out_shape=out_shape,
        in_specs=[ANY] + [VMEM] * (len(operands) - 1),
        out_specs=[VMEM] * len(out_shape),
        scratch_shapes=scratch,
        input_output_aliases=aliases,
        compiler_params=pltpu.CompilerParams(vmem_limit_bytes=8 * MIB),
        cost_estimate=pl.CostEstimate(
            flops=packs * 2 * LANES * LANES * width,
            bytes_accessed=NB * rows * width * 2,
            transcendentals=0,
        ),
        name="triads",
    )(*operands)[0]


def mode_decomposition(snapshots, weights, triads):
    points = snapshots.shape[2]
    snapshots = pltpu.with_memory_space_constraint(snapshots, pltpu.HBM)
    freqs, bands = sizes = lax.axis_size("freq"), lax.axis_size("band")
    shards = freqs * bands
    own_points = points // shards
    widths = split_widths(own_points)
    offsets = [sum(widths[:i]) for i in range(len(widths))]
    scale = 1.0 / math.sqrt(points * lax.axis_size("space"))
    ids = triads.T
    weights = weights.reshape(1, points)

    def send(value, slot):
        if slot == 0:
            return value
        shift_freq, shift_band = divmod(slot, bands)
        pairs = [
            (f * bands + b, (f + shift_freq) % freqs * bands + (b + shift_band) % bands)
            for f in range(freqs)
            for b in range(bands)
        ]
        return lax.ppermute(value, ("freq", "band"), pairs)

    def send_all(values, slots):
        return [send(value, slot) for slot, value in zip(slots, values)]

    near = list(range(bands))
    far = list(range(bands, shards))
    table, *outs = dft_far(snapshots, None, sizes, far, own_points, 0, widths[0])
    arrived = [send_all(outs, far)]
    outs = dft_far(snapshots, table, sizes, far, own_points, offsets[1], widths[1])
    arrived.append(send_all(outs, far))
    plan = [
        (slot, offset, width)
        for offset, width in list(zip(offsets, widths))[2:]
        for slot in far
    ] + [(slot, 0, own_points) for slot in near]
    rest = dft_rest(snapshots, table, sizes, plan, own_points, outs[0])
    for _ in range(2, len(widths)):
        arrived.append(send_all(rest[: len(far)], far))
        rest = rest[len(far) :]
    near_sources = send_all(rest, near)

    total = None
    for chunk, (offset, width) in enumerate(zip(offsets, widths)):
        slots = [(slot, 0) for slot in far]
        sources = arrived[chunk]
        prepared = None
        if chunk == len(widths) - 1:
            prepared = prepare(near_sources, sizes, near, offset, width)
        else:
            slots = [(slot, offset) for slot in near] + slots
            sources = near_sources + sources
        total = triad_chunk(
            ids, weights, sources, slots, sizes, offset, width, total, scale, prepared
        )

    axes = ("space", "freq", "band")
    devices = lax.axis_size("space") * shards
    packs = total.shape[0]
    pieces = lax.all_to_all(total, axes, split_axis=0, concat_axis=0, tiled=True)
    mine = pieces.reshape(devices, packs // devices, NB, LANES).sum(axis=0)
    mine = mine.reshape(packs // devices, NB, PACK, 2, NB).transpose(0, 2, 3, 1, 4)
    return mine.reshape(packs // devices * PACK, 2 * NB * NB)


def solution(mesh):
    return jax.shard_map(
        mode_decomposition,
        mesh=mesh,
        in_specs=(P(("freq", "band"), None, ("groups", "space")), P(("groups", "space")), P()),
        out_specs=P(("groups", "space", "freq", "band"), None),
        check_vma=False,
    )
```

```python
import functools
import math

import jax
import jax.numpy as jnp
from jax import lax
from jax.experimental import pallas as pl
from jax.experimental.pallas import tpu as pltpu
from jax.sharding import PartitionSpec as P


NB = 16
NF = 64
LANES = 128
PACK = 4
MIB = 1 << 20


VMEM = pl.BlockSpec(memory_space=pltpu.VMEM)
ANY = pl.BlockSpec(memory_space=pl.ANY)


def split_widths(points):
    tiles = points // LANES
    rest = tiles - 2
    count = -(-rest // 3)
    middle = [rest // count + (i < rest % count) for i in range(count)]
    return [w * LANES for w in [1] + middle + [1]]


def make_table(length):
    turn = 2.0 * math.pi / length
    gain = 1.0 / math.sqrt(3.0 * length / 8.0)
    quarter = length // 4

    def cosine(phase):
        moved = phase + quarter // 2
        quadrant = lax.div(moved, quarter) & 3
        angle = (lax.rem(moved, quarter) - quarter // 2).astype(jnp.float32) * turn
        square = angle * angle
        even = 1.0 + square * (
            -1 / 2 + square * (1 / 24 + square * (-1 / 720 + square * (1 / 40320)))
        )
        odd = angle * (
            1.0 + square * (-1 / 6 + square * (1 / 120 + square * (-1 / 5040 + square / 362880)))
        )
        value = jnp.where(quadrant & 1 == 0, even, odd)
        return jnp.where((quadrant == 1) | (quadrant == 2), -value, value)

    time = lax.broadcasted_iota(jnp.int32, (8, length), 1)
    window = (0.5 - 0.5 * cosine(time)) * gain
    row = lax.broadcasted_iota(jnp.int32, (2 * NF, length), 0)
    time = lax.broadcasted_iota(jnp.int32, (2 * NF, length), 1)
    wave = cosine((row & (NF - 1)) * time + jnp.where(row < NF, 0, quarter))
    return (jnp.concatenate([window] * (NF // 4), axis=0) * wave).astype(jnp.bfloat16)


def shifted_part(slot, sign, freqs, bands):
    step_freq, step_band = divmod(slot, bands)
    freq = lax.axis_index("freq") + (step_freq if sign > 0 else freqs - step_freq)
    band = lax.axis_index("band") + (step_band if sign > 0 else bands - step_band)
    return lax.rem(freq, freqs) * bands + lax.rem(band, bands)


def dft_far_kernel(sizes, far, points, offset, own_table, *refs):
    count = len(far)
    snap_ref = refs[0]
    outs = refs[len(refs) - 2 - count : len(refs) - 2]
    buffer, arrived = refs[-2:]
    blocks, length, width = buffer.shape[1:]
    copies = []
    for position, slot in enumerate(far):
        start = shifted_part(slot, 1, *sizes) * points + offset
        for block in range(blocks):
            copy = pltpu.make_async_copy(
                snap_ref.at[block, :, pl.ds(pl.multiple_of(start, LANES), width)],
                buffer.at[position, block],
                arrived.at[position, block],
            )
            copy.start()
            copies.append(copy)
    if own_table:
        table_ref = refs[1]
        table_ref[...] = make_table(length)
    else:
        table_ref = refs[1]
    table = table_ref[...]
    for position in range(count):
        for block in range(blocks):
            copies[position * blocks + block].wait()
            outs[position][block] = jnp.dot(
                table, buffer[position, block], preferred_element_type=jnp.float32
            ).astype(jnp.bfloat16)


def dft_far(snapshots, table, sizes, far, points, offset, width):
    blocks, length, _ = snapshots.shape
    count = len(far)
    own_table = table is None
    out_shape = [pltpu.VMEM((blocks, 2 * NF, width), jnp.bfloat16)] * count
    if own_table:
        out_shape = [pltpu.VMEM((2 * NF, length), jnp.bfloat16)] + out_shape
    return pl.pallas_call(
        functools.partial(dft_far_kernel, sizes, far, points, offset, own_table),
        out_shape=out_shape,
        in_specs=[ANY] + ([] if own_table else [VMEM]),
        out_specs=[VMEM] * len(out_shape),
        scratch_shapes=[
            pltpu.VMEM((count, blocks, length, width), jnp.bfloat16),
            pltpu.SemaphoreType.DMA((count, blocks)),
        ],
        compiler_params=pltpu.CompilerParams(vmem_limit_bytes=8 * MIB),
        name="dft_far",
    )(snapshots, *([] if own_table else [table]))


def dft_rest_kernel(sizes, plan, points, table_ref, snap_ref, after_ref, *outs):
    table = table_ref[...]
    for (slot, offset, width), target in zip(plan, outs):
        step = math.gcd(width, 2 * LANES)
        part = shifted_part(slot, 1, *sizes) * points
        for piece in range(0, width, step):
            start = pl.multiple_of(part + (offset + piece), LANES)
            target[0, :, piece : piece + step] = jnp.dot(
                table, snap_ref[0, :, pl.ds(start, step)], preferred_element_type=jnp.float32
            ).astype(jnp.bfloat16)


def dft_rest(snapshots, table, sizes, plan, points, after):
    blocks, length, columns = snapshots.shape
    return pl.pallas_call(
        functools.partial(dft_rest_kernel, sizes, plan, points),
        out_shape=[
            jax.ShapeDtypeStruct((blocks, 2 * NF, width), jnp.bfloat16) for _, _, width in plan
        ],
        grid=(blocks,),
        in_specs=[
            pl.BlockSpec((2 * NF, length), lambda i: (0, 0)),
            pl.BlockSpec((1, length, columns), lambda i: (i, 0, 0)),
            ANY,
        ],
        out_specs=[pl.BlockSpec((1, 2 * NF, width), lambda i: (i, 0, 0)) for _, _, width in plan],
        compiler_params=pltpu.CompilerParams(vmem_limit_bytes=16 * MIB),
        cost_estimate=pl.CostEstimate(
            flops=4 * NF * length * columns * blocks,
            bytes_accessed=blocks * columns * (2 * length + 4 * NF),
            transcendentals=0,
        ),
        name="dft_rest",
    )(table, snapshots, after)


def interleave(spec_ref, source, slot, sizes, base):
    blocks, rows, _ = source.shape
    first = shifted_part(slot, -1, *sizes) * blocks
    for block in range(blocks):
        for tile in range(spec_ref.shape[0]):
            lanes = slice(base + tile * LANES, base + (tile + 1) * LANES)
            spec_ref[tile, pl.ds(first + block, rows, stride=NB), :] = source[
                block, :, lanes
            ].astype(jnp.float32)


def prepare_kernel(sizes, near, offset, *refs):
    for slot, source in zip(near, refs[:-1]):
        interleave(refs[-1], source, slot, sizes, offset)


def prepare(near_sources, sizes, near, offset, width):
    rows = near_sources[0].shape[1]
    return pl.pallas_call(
        functools.partial(prepare_kernel, sizes, near, offset),
        out_shape=jax.ShapeDtypeStruct((width // LANES, rows * NB, LANES), jnp.float32),
        in_specs=[VMEM] * len(near),
        out_specs=VMEM,
        compiler_params=pltpu.CompilerParams(vmem_limit_bytes=8 * MIB),
        name="prepare",
    )(*near_sources)


def triad_kernel(sizes, slots, offset, prepared, has_prior, scale, *refs):
    ids_any, weights_ref = refs[:2]
    rest = list(refs[2:])
    prior_ref = rest.pop(0) if has_prior else None
    if prepared:
        rest.pop(0)
    sources = [rest.pop(0) for _ in slots]
    out_ref, spec_ref, ids_ref, ids_arrived = rest
    ids_copy = pltpu.make_async_copy(ids_any, ids_ref, ids_arrived)
    ids_copy.start()
    tiles = spec_ref.shape[0]
    own_points = weights_ref.shape[1] // (sizes[0] * sizes[1])
    here = shifted_part(0, 1, *sizes) * own_points + offset

    for (slot, base), source in zip(slots, sources):
        interleave(spec_ref, source, slot, sizes, base)
    weights = [
        weights_ref[:, pl.ds(pl.multiple_of(here + tile * LANES, LANES), LANES)]
        for tile in range(tiles)
    ]
    ids_copy.wait()
    lane = lax.broadcasted_iota(jnp.int32, (NB, LANES), 1)

    def one_pack(group, carry):
        fields = []
        thirds = []
        for member in range(PACK):
            first = ids_ref[0, group * PACK + member]
            second = ids_ref[1, group * PACK + member]
            third = first + second
            field_re, field_im, third_re, third_im, third_neg = [], [], [], [], []
            for tile in range(tiles):
                def load(freq, part):
                    start = pl.multiple_of((freq + part * NF) * NB, NB)
                    return spec_ref[tile, pl.ds(start, NB), :]

                first_re, first_im = load(first, 0), load(first, 1)
                second_re, second_im = load(second, 0), load(second, 1)
                weight = weights[tile]
                field_re.append(weight * (first_re * second_re - first_im * second_im))
                field_im.append(weight * (first_re * second_im + first_im * second_re))
                third_re.append(load(third, 0))
                third_im.append(load(third, 1))
                third_neg.append(-third_re[-1])
            for parts, rows_of in (
                (field_re + field_im, fields),
                (third_re + third_im, thirds),
                (third_im + third_neg, thirds),
            ):
                rows_of.append(jnp.concatenate(parts, axis=1).astype(jnp.bfloat16))
        product = lax.dot_general(
            jnp.concatenate(fields, axis=0),
            jnp.concatenate(thirds, axis=0),
            (((1,), (1,)), ((), ())),
            preferred_element_type=jnp.float32,
        )
        total = product[0:NB]
        for member in range(1, PACK):
            total = jnp.where(
                lane >= member * 2 * NB, product[member * NB : (member + 1) * NB], total
            )
        total = total * scale
        if has_prior:
            total = total + prior_ref[group]
        out_ref[group] = total.astype(out_ref.dtype)
        return carry

    lax.fori_loop(0, out_ref.shape[0], one_pack, 0, unroll=4)


def triad_chunk(ids, weights, sources, slots, sizes, offset, width, prior, scale, prepared=None):
    rows = sources[0].shape[1]
    packs = ids.shape[1] // PACK
    spec_shape = (width // LANES, rows * NB, LANES)
    operands = [ids, weights] + ([] if prior is None else [prior])
    aliases = {}
    kept = jnp.float32 if prepared is None else jnp.bfloat16
    out_shape = [jax.ShapeDtypeStruct((packs, NB, LANES), kept)]
    scratch = [pltpu.SMEM(ids.shape, jnp.int32), pltpu.SemaphoreType.DMA]
    if prepared is None:
        scratch = [pltpu.VMEM(spec_shape, jnp.float32)] + scratch
    else:
        aliases = {len(operands): 1}
        operands.append(prepared)
        out_shape.append(jax.ShapeDtypeStruct(spec_shape, jnp.float32))
    operands += [pltpu.with_memory_space_constraint(x, pltpu.VMEM) for x in sources]
    return pl.pallas_call(
        functools.partial(
            triad_kernel, sizes, slots, offset, prepared is not None, prior is not None, scale
        ),
        out_shape=out_shape,
        in_specs=[ANY] + [VMEM] * (len(operands) - 1),
        out_specs=[VMEM] * len(out_shape),
        scratch_shapes=scratch,
        input_output_aliases=aliases,
        compiler_params=pltpu.CompilerParams(vmem_limit_bytes=8 * MIB),
        cost_estimate=pl.CostEstimate(
            flops=packs * 2 * LANES * LANES * width,
            bytes_accessed=NB * rows * width * 2,
            transcendentals=0,
        ),
        name="triads",
    )(*operands)[0]


def finish_kernel(part_ref, out_ref):
    packs = out_ref.shape[0] // PACK
    sublane = lax.broadcasted_iota(jnp.int32, (8, LANES), 0)
    lane = lax.broadcasted_iota(jnp.int32, (8, LANES), 1)
    mine = lane // NB == sublane
    for pack in range(packs):
        total = part_ref[pack].astype(jnp.float32)
        for device in range(1, part_ref.shape[0] // packs):
            total = total + part_ref[device * packs + pack].astype(jnp.float32)
        for half in range(2):
            spread = pltpu.roll(total[half * 8 : half * 8 + 8], 0, 1, stride=NB, stride_axis=0)
            for column in range(2 * PACK):
                moved = pltpu.roll(spread, (-column * NB) % LANES, 1)
                row = jnp.sum(jnp.where(mine, moved, 0.0), axis=0, keepdims=True)
                triad, part = divmod(column, 2)
                start = part * NB * NB + half * LANES
                out_ref[pack * PACK + triad : pack * PACK + triad + 1, start : start + LANES] = row


def finish(pieces, devices):
    rows = pieces.shape[0] // devices * PACK
    return pl.pallas_call(
        finish_kernel,
        out_shape=jax.ShapeDtypeStruct((rows, 2 * NB * NB), jnp.float32),
        in_specs=[VMEM],
        out_specs=VMEM,
        compiler_params=pltpu.CompilerParams(vmem_limit_bytes=8 * MIB),
        name="finish",
    )(pieces)


def mode_decomposition(snapshots, weights, triads):
    points = snapshots.shape[2]
    snapshots = pltpu.with_memory_space_constraint(snapshots, pltpu.HBM)
    freqs, bands = sizes = lax.axis_size("freq"), lax.axis_size("band")
    shards = freqs * bands
    own_points = points // shards
    widths = split_widths(own_points)
    offsets = [sum(widths[:i]) for i in range(len(widths))]
    scale = 1.0 / math.sqrt(points * lax.axis_size("space"))
    ids = triads.T
    weights = weights.reshape(1, points)

    def send(value, slot):
        if slot == 0:
            return value
        shift_freq, shift_band = divmod(slot, bands)
        pairs = [
            (f * bands + b, (f + shift_freq) % freqs * bands + (b + shift_band) % bands)
            for f in range(freqs)
            for b in range(bands)
        ]
        return lax.ppermute(value, ("freq", "band"), pairs)

    def send_all(values, slots):
        return [send(value, slot) for slot, value in zip(slots, values)]

    near = list(range(bands))
    far = list(range(bands, shards))
    table, *outs = dft_far(snapshots, None, sizes, far, own_points, 0, widths[0])
    arrived = [send_all(outs, far)]
    outs = dft_far(snapshots, table, sizes, far, own_points, offsets[1], widths[1])
    arrived.append(send_all(outs, far))
    plan = [
        (slot, offset, width)
        for offset, width in list(zip(offsets, widths))[2:]
        for slot in far
    ] + [(slot, 0, own_points) for slot in near]
    rest = dft_rest(snapshots, table, sizes, plan, own_points, outs[0])
    for _ in range(2, len(widths)):
        arrived.append(send_all(rest[: len(far)], far))
        rest = rest[len(far) :]
    near_sources = send_all(rest, near)

    total = None
    for chunk, (offset, width) in enumerate(zip(offsets, widths)):
        slots = [(slot, 0) for slot in far]
        sources = arrived[chunk]
        prepared = None
        if chunk == len(widths) - 1:
            prepared = prepare(near_sources, sizes, near, offset, width)
        else:
            slots = [(slot, offset) for slot in near] + slots
            sources = near_sources + sources
        total = triad_chunk(
            ids, weights, sources, slots, sizes, offset, width, total, scale, prepared
        )

    axes = ("space", "freq", "band")
    devices = lax.axis_size("space") * shards
    pieces = lax.all_to_all(total, axes, split_axis=0, concat_axis=0, tiled=True)
    return finish(pieces, devices)


def solution(mesh):
    return jax.shard_map(
        mode_decomposition,
        mesh=mesh,
        in_specs=(P(("freq", "band"), None, ("groups", "space")), P(("groups", "space")), P()),
        out_specs=P(("groups", "space", "freq", "band"), None),
        check_vma=False,
    )
```

```python
import functools
import math

import jax
import jax.numpy as jnp
from jax import lax
from jax.experimental import pallas as pl
from jax.experimental.pallas import tpu as pltpu
from jax.sharding import PartitionSpec as P


NB = 16
NF = 64
LANES = 128
PACK = 4
MIB = 1 << 20


VMEM = pl.BlockSpec(memory_space=pltpu.VMEM)
ANY = pl.BlockSpec(memory_space=pl.ANY)


def split_widths(points):
    tiles = points // LANES
    rest = tiles - 2
    count = -(-rest // 3)
    middle = [rest // count + (i < rest % count) for i in range(count)]
    return [w * LANES for w in [1] + middle + [1]]


def make_table(table_ref):
    rows, length = table_ref.shape
    turn = 2.0 * math.pi / length
    gain = 1.0 / math.sqrt(3.0 * length / 8.0)
    quarter = length // 4

    def cosine(phase):
        moved = phase + quarter // 2
        quadrant = lax.div(moved, quarter) & 3
        angle = (lax.rem(moved, quarter) - quarter // 2).astype(jnp.float32) * turn
        square = angle * angle
        even = 1.0 + square * (
            -1 / 2 + square * (1 / 24 + square * (-1 / 720 + square * (1 / 40320)))
        )
        odd = angle * (
            1.0 + square * (-1 / 6 + square * (1 / 120 + square * (-1 / 5040 + square / 362880)))
        )
        value = jnp.where(quadrant & 1 == 0, even, odd)
        return jnp.where((quadrant == 1) | (quadrant == 2), -value, value)

    step = 16
    row = lax.broadcasted_iota(jnp.int32, (step, length), 0)
    time = lax.broadcasted_iota(jnp.int32, (step, length), 1)
    window = (0.5 - 0.5 * cosine(time)) * gain

    def some_rows(index, carry):
        first = pl.multiple_of(index * step, step)
        freq = (row + first) & (NF - 1)
        ahead = jnp.where(first < NF, 0, quarter)
        table_ref[pl.ds(first, step), :] = (window * cosine(freq * time + ahead)).astype(
            table_ref.dtype
        )
        return carry

    lax.fori_loop(0, rows // step, some_rows, 0)


def shifted_part(slot, sign, freqs, bands):
    step_freq, step_band = divmod(slot, bands)
    freq = lax.axis_index("freq") + (step_freq if sign > 0 else freqs - step_freq)
    band = lax.axis_index("band") + (step_band if sign > 0 else bands - step_band)
    return lax.rem(freq, freqs) * bands + lax.rem(band, bands)


def dft_far_kernel(sizes, far, points, offset, own_table, *refs):
    snap_ref, table_ref = refs[:2]
    outs = refs[len(refs) - 2 - len(far) : len(refs) - 2]
    buffer, arrived = refs[-2:]
    blocks, _, width = outs[0].shape
    copies = []
    for position, slot in enumerate(far):
        start = shifted_part(slot, 1, *sizes) * points + offset
        for block in range(blocks):
            index = position * blocks + block
            copy = pltpu.make_async_copy(
                snap_ref.at[block, :, pl.ds(pl.multiple_of(start, LANES), width)],
                buffer.at[:, index * width : (index + 1) * width],
                arrived.at[index],
            )
            copy.start()
            copies.append(copy)
    if own_table:
        make_table(table_ref)
    for copy in copies:
        copy.wait()
    spectra = jnp.dot(
        table_ref[...], buffer[...], preferred_element_type=jnp.float32
    ).astype(jnp.bfloat16)
    for index in range(len(copies)):
        position, block = divmod(index, blocks)
        outs[position][block] = spectra[:, index * width : (index + 1) * width]


def dft_far(snapshots, table, sizes, far, points, offset, width):
    blocks, length, _ = snapshots.shape
    count = len(far)
    own_table = table is None
    out_shape = [pltpu.VMEM((blocks, 2 * NF, width), jnp.bfloat16)] * count
    if own_table:
        out_shape = [pltpu.VMEM((2 * NF, length), jnp.bfloat16)] + out_shape
    return pl.pallas_call(
        functools.partial(dft_far_kernel, sizes, far, points, offset, own_table),
        out_shape=out_shape,
        in_specs=[ANY] + ([] if own_table else [VMEM]),
        out_specs=[VMEM] * len(out_shape),
        scratch_shapes=[
            pltpu.VMEM((length, count * blocks * width), jnp.bfloat16),
            pltpu.SemaphoreType.DMA((count * blocks,)),
        ],
        compiler_params=pltpu.CompilerParams(vmem_limit_bytes=12 * MIB),
        name="dft_far",
    )(snapshots, *([] if own_table else [table]))


def dft_rest_kernel(sizes, plan, points, table_ref, snap_ref, after_ref, *outs):
    table = table_ref[...]
    for (slot, offset, width), target in zip(plan, outs):
        step = math.gcd(width, 2 * LANES)
        part = shifted_part(slot, 1, *sizes) * points
        for piece in range(0, width, step):
            start = pl.multiple_of(part + (offset + piece), LANES)
            target[0, :, piece : piece + step] = jnp.dot(
                table, snap_ref[0, :, pl.ds(start, step)], preferred_element_type=jnp.float32
            ).astype(jnp.bfloat16)


def dft_rest(snapshots, table, sizes, plan, points, after):
    blocks, length, columns = snapshots.shape
    return pl.pallas_call(
        functools.partial(dft_rest_kernel, sizes, plan, points),
        out_shape=[
            jax.ShapeDtypeStruct((blocks, 2 * NF, width), jnp.bfloat16) for _, _, width in plan
        ],
        grid=(blocks,),
        in_specs=[
            pl.BlockSpec((2 * NF, length), lambda i: (0, 0)),
            pl.BlockSpec((1, length, columns), lambda i: (i, 0, 0)),
            ANY,
        ],
        out_specs=[pl.BlockSpec((1, 2 * NF, width), lambda i: (i, 0, 0)) for _, _, width in plan],
        compiler_params=pltpu.CompilerParams(vmem_limit_bytes=16 * MIB),
        cost_estimate=pl.CostEstimate(
            flops=4 * NF * length * columns * blocks,
            bytes_accessed=blocks * columns * (2 * length + 4 * NF),
            transcendentals=0,
        ),
        name="dft_rest",
    )(table, snapshots, after)


def interleave(spec_ref, source, slot, sizes, base):
    blocks, rows, _ = source.shape
    first = shifted_part(slot, -1, *sizes) * blocks
    for block in range(blocks):
        for tile in range(spec_ref.shape[0]):
            lanes = slice(base + tile * LANES, base + (tile + 1) * LANES)
            spec_ref[tile, pl.ds(first + block, rows, stride=NB), :] = source[
                block, :, lanes
            ].astype(jnp.float32)


def prepare_kernel(sizes, near, offset, *refs):
    for slot, source in zip(near, refs[:-1]):
        interleave(refs[-1], source, slot, sizes, offset)


def prepare(near_sources, sizes, near, offset, width):
    rows = near_sources[0].shape[1]
    return pl.pallas_call(
        functools.partial(prepare_kernel, sizes, near, offset),
        out_shape=jax.ShapeDtypeStruct((width // LANES, rows * NB, LANES), jnp.float32),
        in_specs=[VMEM] * len(near),
        out_specs=VMEM,
        compiler_params=pltpu.CompilerParams(vmem_limit_bytes=8 * MIB),
        name="prepare",
    )(*near_sources)


def triad_kernel(sizes, slots, offset, prepared, has_prior, scale, *refs):
    ids_any, weights_ref = refs[:2]
    rest = list(refs[2:])
    prior_ref = rest.pop(0) if has_prior else None
    if prepared:
        rest.pop(0)
    sources = [rest.pop(0) for _ in slots]
    out_ref, spec_ref, ids_ref, ids_arrived = rest
    ids_copy = pltpu.make_async_copy(ids_any, ids_ref, ids_arrived)
    ids_copy.start()
    tiles = spec_ref.shape[0]
    own_points = weights_ref.shape[1] // (sizes[0] * sizes[1])
    here = shifted_part(0, 1, *sizes) * own_points + offset

    for (slot, base), source in zip(slots, sources):
        interleave(spec_ref, source, slot, sizes, base)
    weights = [
        weights_ref[:, pl.ds(pl.multiple_of(here + tile * LANES, LANES), LANES)]
        for tile in range(tiles)
    ]
    ids_copy.wait()
    lane = lax.broadcasted_iota(jnp.int32, (NB, LANES), 1)

    def one_pack(group, carry):
        fields = []
        thirds = []
        for member in range(PACK):
            first = ids_ref[0, group * PACK + member]
            second = ids_ref[1, group * PACK + member]
            third = first + second
            field_re, field_im, third_re, third_im, third_neg = [], [], [], [], []
            for tile in range(tiles):
                def load(freq, part):
                    start = pl.multiple_of((freq + part * NF) * NB, NB)
                    return spec_ref[tile, pl.ds(start, NB), :]

                first_re, first_im = load(first, 0), load(first, 1)
                second_re, second_im = load(second, 0), load(second, 1)
                weight = weights[tile]
                field_re.append(weight * (first_re * second_re - first_im * second_im))
                field_im.append(weight * (first_re * second_im + first_im * second_re))
                third_re.append(load(third, 0))
                third_im.append(load(third, 1))
                third_neg.append(-third_re[-1])
            for parts, rows_of in (
                (field_re + field_im, fields),
                (third_re + third_im, thirds),
                (third_im + third_neg, thirds),
            ):
                rows_of.append(jnp.concatenate(parts, axis=1).astype(jnp.bfloat16))
        product = lax.dot_general(
            jnp.concatenate(fields, axis=0),
            jnp.concatenate(thirds, axis=0),
            (((1,), (1,)), ((), ())),
            preferred_element_type=jnp.float32,
        )
        total = product[0:NB]
        for member in range(1, PACK):
            total = jnp.where(
                lane >= member * 2 * NB, product[member * NB : (member + 1) * NB], total
            )
        total = total * scale
        if has_prior:
            total = total + prior_ref[group]
        out_ref[group] = total.astype(out_ref.dtype)
        return carry

    lax.fori_loop(0, out_ref.shape[0], one_pack, 0, unroll=16 if prepared else 4)


def triad_chunk(ids, weights, sources, slots, sizes, offset, width, prior, scale, prepared=None):
    rows = sources[0].shape[1]
    packs = ids.shape[1] // PACK
    spec_shape = (width // LANES, rows * NB, LANES)
    operands = [ids, weights] + ([] if prior is None else [prior])
    aliases = {}
    kept = jnp.float32 if prepared is None else jnp.bfloat16
    out_shape = [jax.ShapeDtypeStruct((packs, NB, LANES), kept)]
    scratch = [pltpu.SMEM(ids.shape, jnp.int32), pltpu.SemaphoreType.DMA]
    if prepared is None:
        scratch = [pltpu.VMEM(spec_shape, jnp.float32)] + scratch
    else:
        aliases = {len(operands): 1}
        operands.append(prepared)
        out_shape.append(jax.ShapeDtypeStruct(spec_shape, jnp.float32))
    operands += [pltpu.with_memory_space_constraint(x, pltpu.VMEM) for x in sources]
    return pl.pallas_call(
        functools.partial(
            triad_kernel, sizes, slots, offset, prepared is not None, prior is not None, scale
        ),
        out_shape=out_shape,
        in_specs=[ANY] + [VMEM] * (len(operands) - 1),
        out_specs=[VMEM] * len(out_shape),
        scratch_shapes=scratch,
        input_output_aliases=aliases,
        compiler_params=pltpu.CompilerParams(vmem_limit_bytes=8 * MIB),
        cost_estimate=pl.CostEstimate(
            flops=packs * 2 * LANES * LANES * width,
            bytes_accessed=NB * rows * width * 2,
            transcendentals=0,
        ),
        name="triads",
    )(*operands)[0]


def finish_kernel(part_ref, out_ref):
    packs = out_ref.shape[0] // PACK
    sublane = lax.broadcasted_iota(jnp.int32, (8, LANES), 0)
    lane = lax.broadcasted_iota(jnp.int32, (8, LANES), 1)
    mine = lane // NB == sublane
    for pack in range(packs):
        total = part_ref[pack].astype(jnp.float32)
        for device in range(1, part_ref.shape[0] // packs):
            total = total + part_ref[device * packs + pack].astype(jnp.float32)
        for half in range(2):
            spread = pltpu.roll(total[half * 8 : half * 8 + 8], 0, 1, stride=NB, stride_axis=0)
            for column in range(2 * PACK):
                moved = pltpu.roll(spread, (-column * NB) % LANES, 1)
                row = jnp.sum(jnp.where(mine, moved, 0.0), axis=0, keepdims=True)
                triad, part = divmod(column, 2)
                start = part * NB * NB + half * LANES
                out_ref[pack * PACK + triad : pack * PACK + triad + 1, start : start + LANES] = row


def finish(pieces, devices):
    rows = pieces.shape[0] // devices * PACK
    return pl.pallas_call(
        finish_kernel,
        out_shape=jax.ShapeDtypeStruct((rows, 2 * NB * NB), jnp.float32),
        in_specs=[VMEM],
        out_specs=VMEM,
        compiler_params=pltpu.CompilerParams(vmem_limit_bytes=8 * MIB),
        name="finish",
    )(pieces)


def mode_decomposition(snapshots, weights, triads):
    points = snapshots.shape[2]
    snapshots = pltpu.with_memory_space_constraint(snapshots, pltpu.HBM)
    freqs, bands = sizes = lax.axis_size("freq"), lax.axis_size("band")
    shards = freqs * bands
    own_points = points // shards
    widths = split_widths(own_points)
    offsets = [sum(widths[:i]) for i in range(len(widths))]
    scale = 1.0 / math.sqrt(points * lax.axis_size("space"))
    ids = triads.T
    weights = weights.reshape(1, points)

    def send(value, slot):
        if slot == 0:
            return value
        shift_freq, shift_band = divmod(slot, bands)
        pairs = [
            (f * bands + b, (f + shift_freq) % freqs * bands + (b + shift_band) % bands)
            for f in range(freqs)
            for b in range(bands)
        ]
        return lax.ppermute(value, ("freq", "band"), pairs)

    def send_all(values, slots):
        return [send(value, slot) for slot, value in zip(slots, values)]

    near = list(range(bands))
    far = list(range(bands, shards))
    table, *outs = dft_far(snapshots, None, sizes, far, own_points, 0, widths[0])
    arrived = [send_all(outs, far)]
    outs = dft_far(snapshots, table, sizes, far, own_points, offsets[1], widths[1])
    arrived.append(send_all(outs, far))
    plan = [
        (slot, offset, width)
        for offset, width in list(zip(offsets, widths))[2:]
        for slot in far
    ] + [(slot, 0, own_points) for slot in near]
    rest = dft_rest(snapshots, table, sizes, plan, own_points, outs[0])
    for _ in range(2, len(widths)):
        arrived.append(send_all(rest[: len(far)], far))
        rest = rest[len(far) :]
    near_sources = send_all(rest, near)

    total = None
    for chunk, (offset, width) in enumerate(zip(offsets, widths)):
        slots = [(slot, 0) for slot in far]
        sources = arrived[chunk]
        prepared = None
        if chunk == len(widths) - 1:
            prepared = prepare(near_sources, sizes, near, offset, width)
        else:
            slots = [(slot, offset) for slot in near] + slots
            sources = near_sources + sources
        total = triad_chunk(
            ids, weights, sources, slots, sizes, offset, width, total, scale, prepared
        )

    axes = ("space", "freq", "band")
    devices = lax.axis_size("space") * shards
    pieces = lax.all_to_all(total, axes, split_axis=0, concat_axis=0, tiled=True)
    return finish(pieces, devices)


def solution(mesh):
    return jax.shard_map(
        mode_decomposition,
        mesh=mesh,
        in_specs=(P(("freq", "band"), None, ("groups", "space")), P(("groups", "space")), P()),
        out_specs=P(("groups", "space", "freq", "band"), None),
        check_vma=False,
    )
```

```python
import functools
import math

import jax
import jax.numpy as jnp
from jax import lax
from jax.experimental import pallas as pl
from jax.experimental.pallas import tpu as pltpu
from jax.sharding import PartitionSpec as P


NB = 16
NF = 64
LANES = 128
PACK = 4
MIB = 1 << 20


VMEM = pl.BlockSpec(memory_space=pltpu.VMEM)
SMEM = pl.BlockSpec(memory_space=pltpu.SMEM)
ANY = pl.BlockSpec(memory_space=pl.ANY)


def split_widths(points):
    tiles = points // LANES
    rest = tiles - 2
    count = -(-rest // 3)
    middle = [rest // count + (i < rest % count) for i in range(count)]
    return [w * LANES for w in [1] + middle + [1]]


def make_table(table_ref):
    rows, length = table_ref.shape
    turn = 2.0 * math.pi / length
    gain = 1.0 / math.sqrt(3.0 * length / 8.0)
    quarter = length // 4

    def cosine(phase):
        moved = phase + quarter // 2
        quadrant = lax.div(moved, quarter) & 3
        angle = (lax.rem(moved, quarter) - quarter // 2).astype(jnp.float32) * turn
        square = angle * angle
        even = 1.0 + square * (
            -1 / 2 + square * (1 / 24 + square * (-1 / 720 + square * (1 / 40320)))
        )
        odd = angle * (
            1.0 + square * (-1 / 6 + square * (1 / 120 + square * (-1 / 5040 + square / 362880)))
        )
        value = jnp.where(quadrant & 1 == 0, even, odd)
        return jnp.where((quadrant == 1) | (quadrant == 2), -value, value)

    step = 16
    row = lax.broadcasted_iota(jnp.int32, (step, length), 0)
    time = lax.broadcasted_iota(jnp.int32, (step, length), 1)
    window = (0.5 - 0.5 * cosine(time)) * gain

    def some_rows(index, carry):
        first = pl.multiple_of(index * step, step)
        freq = (row + first) & (NF - 1)
        ahead = jnp.where(first < NF, 0, quarter)
        table_ref[pl.ds(first, step), :] = (window * cosine(freq * time + ahead)).astype(
            table_ref.dtype
        )
        return carry

    lax.fori_loop(0, rows // step, some_rows, 0)


def shifted_part(slot, sign, freqs, bands):
    step_freq, step_band = divmod(slot, bands)
    freq = lax.axis_index("freq") + (step_freq if sign > 0 else freqs - step_freq)
    band = lax.axis_index("band") + (step_band if sign > 0 else bands - step_band)
    return lax.rem(freq, freqs) * bands + lax.rem(band, bands)


def dft_far_kernel(sizes, far, points, offset, own_table, *refs):
    snap_ref, table_ref = refs[:2]
    outs = refs[len(refs) - 2 - len(far) : len(refs) - 2]
    buffer, arrived = refs[-2:]
    blocks, _, width = outs[0].shape
    copies = []
    for position, slot in enumerate(far):
        start = shifted_part(slot, 1, *sizes) * points + offset
        for block in range(blocks):
            index = position * blocks + block
            copy = pltpu.make_async_copy(
                snap_ref.at[block, :, pl.ds(pl.multiple_of(start, LANES), width)],
                buffer.at[:, index * width : (index + 1) * width],
                arrived.at[index],
            )
            copy.start()
            copies.append(copy)
    if own_table:
        make_table(table_ref)
    for copy in copies:
        copy.wait()
    spectra = jnp.dot(
        table_ref[...], buffer[...], preferred_element_type=jnp.float32
    ).astype(jnp.bfloat16)
    for index in range(len(copies)):
        position, block = divmod(index, blocks)
        outs[position][block] = spectra[:, index * width : (index + 1) * width]


def dft_far(snapshots, table, sizes, far, points, offset, width):
    blocks, length, _ = snapshots.shape
    count = len(far)
    own_table = table is None
    out_shape = [pltpu.VMEM((blocks, 2 * NF, width), jnp.bfloat16)] * count
    if own_table:
        out_shape = [pltpu.VMEM((2 * NF, length), jnp.bfloat16)] + out_shape
    return pl.pallas_call(
        functools.partial(dft_far_kernel, sizes, far, points, offset, own_table),
        out_shape=out_shape,
        in_specs=[ANY] + ([] if own_table else [VMEM]),
        out_specs=[VMEM] * len(out_shape),
        scratch_shapes=[
            pltpu.VMEM((length, count * blocks * width), jnp.bfloat16),
            pltpu.SemaphoreType.DMA((count * blocks,)),
        ],
        compiler_params=pltpu.CompilerParams(vmem_limit_bytes=12 * MIB),
        name="dft_far",
    )(snapshots, *([] if own_table else [table]))


def dft_rest_kernel(sizes, plan, points, table_ref, snap_ref, after_ref, *outs):
    table = table_ref[...]
    for (slot, offset, width), target in zip(plan, outs):
        step = math.gcd(width, 2 * LANES)
        part = shifted_part(slot, 1, *sizes) * points
        for piece in range(0, width, step):
            start = pl.multiple_of(part + (offset + piece), LANES)
            target[0, :, piece : piece + step] = jnp.dot(
                table, snap_ref[0, :, pl.ds(start, step)], preferred_element_type=jnp.float32
            ).astype(jnp.bfloat16)


def dft_rest(snapshots, table, sizes, plan, points, after):
    blocks, length, columns = snapshots.shape
    return pl.pallas_call(
        functools.partial(dft_rest_kernel, sizes, plan, points),
        out_shape=[
            jax.ShapeDtypeStruct((blocks, 2 * NF, width), jnp.bfloat16) for _, _, width in plan
        ],
        grid=(blocks,),
        in_specs=[
            pl.BlockSpec((2 * NF, length), lambda i: (0, 0)),
            pl.BlockSpec((1, length, columns), lambda i: (i, 0, 0)),
            ANY,
        ],
        out_specs=[pl.BlockSpec((1, 2 * NF, width), lambda i: (i, 0, 0)) for _, _, width in plan],
        compiler_params=pltpu.CompilerParams(vmem_limit_bytes=16 * MIB),
        cost_estimate=pl.CostEstimate(
            flops=4 * NF * length * columns * blocks,
            bytes_accessed=blocks * columns * (2 * length + 4 * NF),
            transcendentals=0,
        ),
        name="dft_rest",
    )(table, snapshots, after)


def interleave(spec_ref, source, slot, sizes, base):
    blocks, rows, _ = source.shape
    first = shifted_part(slot, -1, *sizes) * blocks
    for block in range(blocks):
        for tile in range(spec_ref.shape[0]):
            lanes = slice(base + tile * LANES, base + (tile + 1) * LANES)
            spec_ref[tile, pl.ds(first + block, rows, stride=NB), :] = source[
                block, :, lanes
            ].astype(jnp.float32)


def prepare_kernel(sizes, near, offset, *refs):
    ids_any, *sources = refs[:-3]
    ids_ref, spec_ref, ids_arrived = refs[-3:]
    ids_copy = pltpu.make_async_copy(ids_any, ids_ref, ids_arrived)
    ids_copy.start()
    for slot, source in zip(near, sources):
        interleave(spec_ref, source, slot, sizes, offset)
    ids_copy.wait()


def prepare(ids, near_sources, sizes, near, offset, width):
    rows = near_sources[0].shape[1]
    return pl.pallas_call(
        functools.partial(prepare_kernel, sizes, near, offset),
        out_shape=[
            pltpu.SMEM(ids.shape, jnp.int32),
            pltpu.VMEM((width // LANES, rows * NB, LANES), jnp.float32),
        ],
        in_specs=[ANY] + [VMEM] * len(near),
        out_specs=[SMEM, VMEM],
        scratch_shapes=[pltpu.SemaphoreType.DMA],
        compiler_params=pltpu.CompilerParams(vmem_limit_bytes=8 * MIB),
        name="prepare",
    )(ids, *near_sources)


def triad_kernel(sizes, slots, offset, prepared, has_prior, scale, *refs):
    ids_ref, weights_ref = refs[:2]
    rest = list(refs[2:])
    prior_ref = rest.pop(0) if has_prior else None
    if prepared:
        rest.pop(0)
    sources = [rest.pop(0) for _ in slots]
    out_ref, spec_ref = rest
    tiles = spec_ref.shape[0]
    own_points = weights_ref.shape[1] // (sizes[0] * sizes[1])
    here = shifted_part(0, 1, *sizes) * own_points + offset

    for (slot, base), source in zip(slots, sources):
        interleave(spec_ref, source, slot, sizes, base)
    weights = [
        weights_ref[:, pl.ds(pl.multiple_of(here + tile * LANES, LANES), LANES)]
        for tile in range(tiles)
    ]
    lane = lax.broadcasted_iota(jnp.int32, (NB, LANES), 1)

    def one_pack(group, carry):
        fields = []
        thirds = []
        for member in range(PACK):
            first = ids_ref[0, group * PACK + member]
            second = ids_ref[1, group * PACK + member]
            third = first + second
            field_re, field_im, third_re, third_im, third_neg = [], [], [], [], []
            for tile in range(tiles):
                def load(freq, part):
                    start = pl.multiple_of((freq + part * NF) * NB, NB)
                    return spec_ref[tile, pl.ds(start, NB), :]

                first_re, first_im = load(first, 0), load(first, 1)
                second_re, second_im = load(second, 0), load(second, 1)
                weight = weights[tile]
                field_re.append(weight * (first_re * second_re - first_im * second_im))
                field_im.append(weight * (first_re * second_im + first_im * second_re))
                third_re.append(load(third, 0))
                third_im.append(load(third, 1))
                third_neg.append(-third_re[-1])
            for parts, rows_of in (
                (field_re + field_im, fields),
                (third_re + third_im, thirds),
                (third_im + third_neg, thirds),
            ):
                rows_of.append(jnp.concatenate(parts, axis=1).astype(jnp.bfloat16))
        product = lax.dot_general(
            jnp.concatenate(fields, axis=0),
            jnp.concatenate(thirds, axis=0),
            (((1,), (1,)), ((), ())),
            preferred_element_type=jnp.float32,
        )
        total = product[0:NB]
        for member in range(1, PACK):
            total = jnp.where(
                lane >= member * 2 * NB, product[member * NB : (member + 1) * NB], total
            )
        total = total * scale
        if has_prior:
            total = total + prior_ref[group]
        out_ref[group] = total.astype(out_ref.dtype)
        return carry

    lax.fori_loop(0, out_ref.shape[0], one_pack, 0, unroll=16 if prepared else 4)


def triad_chunk(ids, weights, sources, slots, sizes, offset, width, prior, scale, prepared=None):
    rows = sources[0].shape[1]
    packs = ids.shape[1] // PACK
    spec_shape = (width // LANES, rows * NB, LANES)
    operands = [ids, weights] + ([] if prior is None else [prior])
    aliases = {}
    kept = jnp.float32 if prepared is None else jnp.bfloat16
    out_shape = [jax.ShapeDtypeStruct((packs, NB, LANES), kept)]
    scratch = []
    if prepared is None:
        scratch.append(pltpu.VMEM(spec_shape, jnp.float32))
    else:
        aliases = {len(operands): 1}
        operands.append(prepared)
        out_shape.append(jax.ShapeDtypeStruct(spec_shape, jnp.float32))
    operands += [pltpu.with_memory_space_constraint(x, pltpu.VMEM) for x in sources]
    return pl.pallas_call(
        functools.partial(
            triad_kernel, sizes, slots, offset, prepared is not None, prior is not None, scale
        ),
        out_shape=out_shape,
        in_specs=[SMEM] + [VMEM] * (len(operands) - 1),
        out_specs=[VMEM] * len(out_shape),
        scratch_shapes=scratch,
        input_output_aliases=aliases,
        compiler_params=pltpu.CompilerParams(vmem_limit_bytes=8 * MIB),
        cost_estimate=pl.CostEstimate(
            flops=packs * 2 * LANES * LANES * width,
            bytes_accessed=NB * rows * width * 2,
            transcendentals=0,
        ),
        name="triads",
    )(*operands)[0]


def finish_kernel(part_ref, out_ref):
    packs = out_ref.shape[0] // PACK
    sublane = lax.broadcasted_iota(jnp.int32, (8, LANES), 0)
    lane = lax.broadcasted_iota(jnp.int32, (8, LANES), 1)
    mine = lane // NB == sublane
    for pack in range(packs):
        total = part_ref[pack].astype(jnp.float32)
        for device in range(1, part_ref.shape[0] // packs):
            total = total + part_ref[device * packs + pack].astype(jnp.float32)
        for half in range(2):
            spread = pltpu.roll(total[half * 8 : half * 8 + 8], 0, 1, stride=NB, stride_axis=0)
            for column in range(2 * PACK):
                moved = pltpu.roll(spread, (-column * NB) % LANES, 1)
                row = jnp.sum(jnp.where(mine, moved, 0.0), axis=0, keepdims=True)
                triad, part = divmod(column, 2)
                start = part * NB * NB + half * LANES
                out_ref[pack * PACK + triad : pack * PACK + triad + 1, start : start + LANES] = row


def finish(pieces, devices):
    rows = pieces.shape[0] // devices * PACK
    return pl.pallas_call(
        finish_kernel,
        out_shape=jax.ShapeDtypeStruct((rows, 2 * NB * NB), jnp.float32),
        in_specs=[VMEM],
        out_specs=VMEM,
        compiler_params=pltpu.CompilerParams(vmem_limit_bytes=8 * MIB),
        name="finish",
    )(pieces)


def mode_decomposition(snapshots, weights, triads):
    points = snapshots.shape[2]
    snapshots = pltpu.with_memory_space_constraint(snapshots, pltpu.HBM)
    freqs, bands = sizes = lax.axis_size("freq"), lax.axis_size("band")
    shards = freqs * bands
    own_points = points // shards
    widths = split_widths(own_points)
    offsets = [sum(widths[:i]) for i in range(len(widths))]
    scale = 1.0 / math.sqrt(points * lax.axis_size("space"))
    weights = weights.reshape(1, points)

    def send(value, slot):
        if slot == 0:
            return value
        shift_freq, shift_band = divmod(slot, bands)
        pairs = [
            (f * bands + b, (f + shift_freq) % freqs * bands + (b + shift_band) % bands)
            for f in range(freqs)
            for b in range(bands)
        ]
        return lax.ppermute(value, ("freq", "band"), pairs)

    def send_all(values, slots):
        return [send(value, slot) for slot, value in zip(slots, values)]

    near = list(range(bands))
    far = list(range(bands, shards))
    table, *outs = dft_far(snapshots, None, sizes, far, own_points, 0, widths[0])
    arrived = [send_all(outs, far)]
    outs = dft_far(snapshots, table, sizes, far, own_points, offsets[1], widths[1])
    arrived.append(send_all(outs, far))
    plan = [
        (slot, offset, width)
        for offset, width in list(zip(offsets, widths))[2:]
        for slot in far
    ] + [(slot, 0, own_points) for slot in near]
    rest = dft_rest(snapshots, table, sizes, plan, own_points, outs[0])
    for _ in range(2, len(widths)):
        arrived.append(send_all(rest[: len(far)], far))
        rest = rest[len(far) :]
    near_sources = send_all(rest, near)

    ids, ready = prepare(triads.T, near_sources, sizes, near, offsets[-1], widths[-1])
    total = None
    for chunk, (offset, width) in enumerate(zip(offsets, widths)):
        slots = [(slot, 0) for slot in far]
        sources = arrived[chunk]
        prepared = ready if chunk == len(widths) - 1 else None
        if prepared is None:
            slots = [(slot, offset) for slot in near] + slots
            sources = near_sources + sources
        total = triad_chunk(
            ids, weights, sources, slots, sizes, offset, width, total, scale, prepared
        )

    axes = ("space", "freq", "band")
    devices = lax.axis_size("space") * shards
    pieces = lax.all_to_all(total, axes, split_axis=0, concat_axis=0, tiled=True)
    return finish(pieces, devices)


def solution(mesh):
    return jax.shard_map(
        mode_decomposition,
        mesh=mesh,
        in_specs=(P(("freq", "band"), None, ("groups", "space")), P(("groups", "space")), P()),
        out_specs=P(("groups", "space", "freq", "band"), None),
        check_vma=False,
    )
```

```python
import functools
import math

import jax
import jax.numpy as jnp
from jax import lax
from jax.experimental import pallas as pl
from jax.experimental.pallas import tpu as pltpu
from jax.sharding import PartitionSpec as P


NB = 16
NF = 64
LANES = 128
PACK = 4
MIB = 1 << 20


VMEM = pl.BlockSpec(memory_space=pltpu.VMEM)
SMEM = pl.BlockSpec(memory_space=pltpu.SMEM)
ANY = pl.BlockSpec(memory_space=pl.ANY)


def split_widths(points):
    tiles = points // LANES
    rest = tiles - 2
    count = -(-rest // 3)
    middle = [rest // count + (i < rest % count) for i in range(count)]
    return [w * LANES for w in [1] + middle + [1]]


def make_table(table_ref):
    rows, length = table_ref.shape
    turn = 2.0 * math.pi / length
    gain = 1.0 / math.sqrt(3.0 * length / 8.0)
    quarter = length // 4

    def cosine(phase):
        moved = phase + quarter // 2
        quadrant = lax.div(moved, quarter) & 3
        angle = (lax.rem(moved, quarter) - quarter // 2).astype(jnp.float32) * turn
        square = angle * angle
        even = 1.0 + square * (
            -1 / 2 + square * (1 / 24 + square * (-1 / 720 + square * (1 / 40320)))
        )
        odd = angle * (
            1.0 + square * (-1 / 6 + square * (1 / 120 + square * (-1 / 5040 + square / 362880)))
        )
        value = jnp.where(quadrant & 1 == 0, even, odd)
        return jnp.where((quadrant == 1) | (quadrant == 2), -value, value)

    step = 16
    row = lax.broadcasted_iota(jnp.int32, (step, length), 0)
    time = lax.broadcasted_iota(jnp.int32, (step, length), 1)
    window = (0.5 - 0.5 * cosine(time)) * gain

    def some_rows(index, carry):
        first = pl.multiple_of(index * step, step)
        freq = (row + first) & (NF - 1)
        ahead = jnp.where(first < NF, 0, quarter)
        table_ref[pl.ds(first, step), :] = (window * cosine(freq * time + ahead)).astype(
            table_ref.dtype
        )
        return carry

    lax.fori_loop(0, rows // step, some_rows, 0)


def shifted_part(slot, sign, freqs, bands):
    step_freq, step_band = divmod(slot, bands)
    freq = lax.axis_index("freq") + (step_freq if sign > 0 else freqs - step_freq)
    band = lax.axis_index("band") + (step_band if sign > 0 else bands - step_band)
    return lax.rem(freq, freqs) * bands + lax.rem(band, bands)


def dft_far_kernel(sizes, far, points, offset, own_table, *refs):
    snap_ref, table_ref = refs[:2]
    outs = refs[len(refs) - 2 - len(far) : len(refs) - 2]
    buffer, arrived = refs[-2:]
    blocks, _, width = outs[0].shape
    copies = []
    for position, slot in enumerate(far):
        start = shifted_part(slot, 1, *sizes) * points + offset
        for block in range(blocks):
            index = position * blocks + block
            copy = pltpu.make_async_copy(
                snap_ref.at[block, :, pl.ds(pl.multiple_of(start, LANES), width)],
                buffer.at[:, index * width : (index + 1) * width],
                arrived.at[index],
            )
            copy.start()
            copies.append(copy)
    if own_table:
        make_table(table_ref)
    for copy in copies:
        copy.wait()
    spectra = jnp.dot(
        table_ref[...], buffer[...], preferred_element_type=jnp.float32
    ).astype(jnp.bfloat16)
    for index in range(len(copies)):
        position, block = divmod(index, blocks)
        outs[position][block] = spectra[:, index * width : (index + 1) * width]


def dft_far(snapshots, table, sizes, far, points, offset, width):
    blocks, length, _ = snapshots.shape
    count = len(far)
    own_table = table is None
    out_shape = [pltpu.VMEM((blocks, 2 * NF, width), jnp.bfloat16)] * count
    if own_table:
        out_shape = [pltpu.VMEM((2 * NF, length), jnp.bfloat16)] + out_shape
    return pl.pallas_call(
        functools.partial(dft_far_kernel, sizes, far, points, offset, own_table),
        out_shape=out_shape,
        in_specs=[ANY] + ([] if own_table else [VMEM]),
        out_specs=[VMEM] * len(out_shape),
        scratch_shapes=[
            pltpu.VMEM((length, count * blocks * width), jnp.bfloat16),
            pltpu.SemaphoreType.DMA((count * blocks,)),
        ],
        compiler_params=pltpu.CompilerParams(vmem_limit_bytes=12 * MIB),
        name="dft_far",
    )(snapshots, *([] if own_table else [table]))


def dft_rest_kernel(sizes, plan, points, table_ref, snap_ref, after_ref, *outs):
    table = table_ref[...]
    for (slot, offset, width), target in zip(plan, outs):
        step = math.gcd(width, 2 * LANES)
        part = shifted_part(slot, 1, *sizes) * points
        for piece in range(0, width, step):
            start = pl.multiple_of(part + (offset + piece), LANES)
            target[0, :, piece : piece + step] = jnp.dot(
                table, snap_ref[0, :, pl.ds(start, step)], preferred_element_type=jnp.float32
            ).astype(jnp.bfloat16)


def dft_rest(snapshots, table, sizes, plan, points, after):
    blocks, length, columns = snapshots.shape
    return pl.pallas_call(
        functools.partial(dft_rest_kernel, sizes, plan, points),
        out_shape=[
            jax.ShapeDtypeStruct((blocks, 2 * NF, width), jnp.bfloat16) for _, _, width in plan
        ],
        grid=(blocks,),
        in_specs=[
            pl.BlockSpec((2 * NF, length), lambda i: (0, 0)),
            pl.BlockSpec((1, length, columns), lambda i: (i, 0, 0)),
            ANY,
        ],
        out_specs=[pl.BlockSpec((1, 2 * NF, width), lambda i: (i, 0, 0)) for _, _, width in plan],
        compiler_params=pltpu.CompilerParams(vmem_limit_bytes=16 * MIB),
        cost_estimate=pl.CostEstimate(
            flops=4 * NF * length * columns * blocks,
            bytes_accessed=blocks * columns * (2 * length + 4 * NF),
            transcendentals=0,
        ),
        name="dft_rest",
    )(table, snapshots, after)


def interleave(spec_ref, source, slot, sizes, base):
    blocks, rows, _ = source.shape
    first = shifted_part(slot, -1, *sizes) * blocks
    for block in range(blocks):
        for tile in range(spec_ref.shape[0]):
            lanes = slice(base + tile * LANES, base + (tile + 1) * LANES)
            spec_ref[tile, pl.ds(first + block, rows, stride=NB), :] = source[
                block, :, lanes
            ].astype(jnp.float32)


def prepare_kernel(sizes, near, offset, *refs):
    ids_any, *sources = refs[:-3]
    ids_ref, spec_ref, ids_arrived = refs[-3:]
    ids_copy = pltpu.make_async_copy(ids_any, ids_ref, ids_arrived)
    ids_copy.start()
    for slot, source in zip(near, sources):
        interleave(spec_ref, source, slot, sizes, offset)
    ids_copy.wait()


def prepare(ids, near_sources, sizes, near, offset, width):
    rows = near_sources[0].shape[1]
    return pl.pallas_call(
        functools.partial(prepare_kernel, sizes, near, offset),
        out_shape=[
            pltpu.SMEM(ids.shape, jnp.int32),
            pltpu.VMEM((width // LANES, rows * NB, LANES), jnp.float32),
        ],
        in_specs=[ANY] + [VMEM] * len(near),
        out_specs=[SMEM, VMEM],
        scratch_shapes=[pltpu.SemaphoreType.DMA],
        compiler_params=pltpu.CompilerParams(vmem_limit_bytes=8 * MIB),
        name="prepare",
    )(ids, *near_sources)


def triad_kernel(sizes, slots, offset, prepared, has_prior, scale, *refs):
    ids_ref, weights_ref = refs[:2]
    rest = list(refs[2:])
    prior_ref = rest.pop(0) if has_prior else None
    if prepared:
        rest.pop(0)
    sources = [rest.pop(0) for _ in slots]
    out_ref, spec_ref = rest
    tiles = spec_ref.shape[0]
    own_points = weights_ref.shape[1] // (sizes[0] * sizes[1])
    here = shifted_part(0, 1, *sizes) * own_points + offset

    for (slot, base), source in zip(slots, sources):
        interleave(spec_ref, source, slot, sizes, base)
    weights = [
        weights_ref[:, pl.ds(pl.multiple_of(here + tile * LANES, LANES), LANES)]
        for tile in range(tiles)
    ]
    lane = lax.broadcasted_iota(jnp.int32, (NB, LANES), 1)

    def one_pack(group, carry):
        fields = []
        thirds = []
        for member in range(PACK):
            first = ids_ref[0, group * PACK + member]
            second = ids_ref[1, group * PACK + member]
            third = first + second
            field_re, field_im, third_re, third_im, third_neg = [], [], [], [], []
            for tile in range(tiles):
                def load(freq, part):
                    start = pl.multiple_of((freq + part * NF) * NB, NB)
                    return spec_ref[tile, pl.ds(start, NB), :]

                first_re, first_im = load(first, 0), load(first, 1)
                second_re, second_im = load(second, 0), load(second, 1)
                weight = weights[tile]
                field_re.append(weight * (first_re * second_re - first_im * second_im))
                field_im.append(weight * (first_re * second_im + first_im * second_re))
                third_re.append(load(third, 0))
                third_im.append(load(third, 1))
                third_neg.append(-third_re[-1])
            for parts, rows_of in (
                (field_re + field_im, fields),
                (third_re + third_im, thirds),
                (third_im + third_neg, thirds),
            ):
                rows_of.append(jnp.concatenate(parts, axis=1).astype(jnp.bfloat16))
        product = lax.dot_general(
            jnp.concatenate(fields, axis=0),
            jnp.concatenate(thirds, axis=0),
            (((1,), (1,)), ((), ())),
            preferred_element_type=jnp.float32,
        )
        total = product[0:NB]
        for member in range(1, PACK):
            total = jnp.where(
                lane >= member * 2 * NB, product[member * NB : (member + 1) * NB], total
            )
        total = total * scale
        if has_prior:
            total = total + prior_ref[group]
        out_ref[group] = total.astype(out_ref.dtype)
        return carry

    lax.fori_loop(0, out_ref.shape[0], one_pack, 0, unroll=16 if prepared else 4)


def triad_chunk(ids, weights, sources, slots, sizes, offset, width, prior, scale, prepared=None):
    rows = sources[0].shape[1]
    packs = ids.shape[1] // PACK
    spec_shape = (width // LANES, rows * NB, LANES)
    operands = [ids, weights] + ([] if prior is None else [prior])
    aliases = {}
    kept = jnp.float32 if prepared is None else jnp.bfloat16
    out_shape = [jax.ShapeDtypeStruct((packs, NB, LANES), kept)]
    scratch = []
    if prepared is None:
        scratch.append(pltpu.VMEM(spec_shape, jnp.float32))
    else:
        aliases = {len(operands): 1}
        operands.append(prepared)
        out_shape.append(jax.ShapeDtypeStruct(spec_shape, jnp.float32))
    operands += [pltpu.with_memory_space_constraint(x, pltpu.VMEM) for x in sources]
    return pl.pallas_call(
        functools.partial(
            triad_kernel, sizes, slots, offset, prepared is not None, prior is not None, scale
        ),
        out_shape=out_shape,
        in_specs=[SMEM] + [VMEM] * (len(operands) - 1),
        out_specs=[VMEM] * len(out_shape),
        scratch_shapes=scratch,
        input_output_aliases=aliases,
        compiler_params=pltpu.CompilerParams(vmem_limit_bytes=8 * MIB),
        cost_estimate=pl.CostEstimate(
            flops=packs * 2 * LANES * LANES * width,
            bytes_accessed=NB * rows * width * 2,
            transcendentals=0,
        ),
        name="triads",
    )(*operands)[0]


def finish_kernel(part_ref, out_ref):
    packs = out_ref.shape[0] // PACK
    sublane = lax.broadcasted_iota(jnp.int32, (8, LANES), 0)
    lane = lax.broadcasted_iota(jnp.int32, (8, LANES), 1)
    mine = lane // NB == sublane
    for pack in range(packs):
        total = part_ref[pack].astype(jnp.float32)
        for device in range(1, part_ref.shape[0] // packs):
            total = total + part_ref[device * packs + pack].astype(jnp.float32)
        for half in range(2):
            spread = pltpu.roll(total[half * 8 : half * 8 + 8], 0, 1, stride=NB, stride_axis=0)
            for column in range(2 * PACK):
                moved = pltpu.roll(spread, (-column * NB) % LANES, 1)
                row = jnp.sum(jnp.where(mine, moved, 0.0), axis=0, keepdims=True)
                triad, part = divmod(column, 2)
                start = part * NB * NB + half * LANES
                out_ref[pack * PACK + triad : pack * PACK + triad + 1, start : start + LANES] = row


def finish(pieces, devices):
    rows = pieces.shape[0] // devices * PACK
    return pl.pallas_call(
        finish_kernel,
        out_shape=jax.ShapeDtypeStruct((rows, 2 * NB * NB), jnp.float32),
        in_specs=[VMEM],
        out_specs=VMEM,
        compiler_params=pltpu.CompilerParams(vmem_limit_bytes=8 * MIB),
        name="finish",
    )(pieces)


def mode_decomposition(snapshots, weights, triads):
    points = snapshots.shape[2]
    snapshots = pltpu.with_memory_space_constraint(snapshots, pltpu.HBM)
    freqs, bands = sizes = lax.axis_size("freq"), lax.axis_size("band")
    shards = freqs * bands
    own_points = points // shards
    widths = split_widths(own_points)
    offsets = [sum(widths[:i]) for i in range(len(widths))]
    scale = 1.0 / math.sqrt(points * lax.axis_size("space"))
    weights = weights.reshape(1, points)

    def send(value, slot):
        if slot == 0:
            return value
        shift_freq, shift_band = divmod(slot, bands)
        pairs = [
            (f * bands + b, (f + shift_freq) % freqs * bands + (b + shift_band) % bands)
            for f in range(freqs)
            for b in range(bands)
        ]
        return lax.ppermute(value, ("freq", "band"), pairs)

    def send_all(values, slots):
        return [send(value, slot) for slot, value in zip(slots, values)]

    near = list(range(bands))
    far = list(range(bands, shards))
    table, *outs = dft_far(snapshots, None, sizes, far[:1], own_points, 0, widths[0])
    arrived = [send_all(outs, far[:1])]
    outs = dft_far(snapshots, table, sizes, far[1:], own_points, 0, widths[0])
    arrived[0] += send_all(outs, far[1:])
    outs = dft_far(snapshots, table, sizes, far, own_points, offsets[1], widths[1])
    arrived.append(send_all(outs, far))
    plan = [
        (slot, offset, width)
        for offset, width in list(zip(offsets, widths))[2:]
        for slot in far
    ] + [(slot, 0, own_points) for slot in near]
    rest = dft_rest(snapshots, table, sizes, plan, own_points, outs[0])
    for _ in range(2, len(widths)):
        arrived.append(send_all(rest[: len(far)], far))
        rest = rest[len(far) :]
    near_sources = send_all(rest, near)

    ids, ready = prepare(triads.T, near_sources, sizes, near, offsets[-1], widths[-1])
    total = None
    for chunk, (offset, width) in enumerate(zip(offsets, widths)):
        slots = [(slot, 0) for slot in far]
        sources = arrived[chunk]
        prepared = ready if chunk == len(widths) - 1 else None
        if prepared is None:
            slots = [(slot, offset) for slot in near] + slots
            sources = near_sources + sources
        total = triad_chunk(
            ids, weights, sources, slots, sizes, offset, width, total, scale, prepared
        )

    axes = ("space", "freq", "band")
    devices = lax.axis_size("space") * shards
    pieces = lax.all_to_all(total, axes, split_axis=0, concat_axis=0, tiled=True)
    return finish(pieces, devices)


def solution(mesh):
    return jax.shard_map(
        mode_decomposition,
        mesh=mesh,
        in_specs=(P(("freq", "band"), None, ("groups", "space")), P(("groups", "space")), P()),
        out_specs=P(("groups", "space", "freq", "band"), None),
        check_vma=False,
    )
```

```python
import functools
import math

import jax
import jax.numpy as jnp
from jax import lax
from jax.experimental import pallas as pl
from jax.experimental.pallas import tpu as pltpu
from jax.sharding import PartitionSpec as P


NB = 16
NF = 64
LANES = 128
PACK = 4
MIB = 1 << 20


VMEM = pl.BlockSpec(memory_space=pltpu.VMEM)
SMEM = pl.BlockSpec(memory_space=pltpu.SMEM)
ANY = pl.BlockSpec(memory_space=pl.ANY)


def split_widths(points):
    tiles = points // LANES
    rest = tiles - 2
    count = -(-rest // 3)
    middle = [rest // count + (i < rest % count) for i in range(count)]
    return [w * LANES for w in [1] + middle + [1]]


def make_table(table_ref):
    rows, length = table_ref.shape
    turn = 2.0 * math.pi / length
    gain = 1.0 / math.sqrt(3.0 * length / 8.0)
    quarter = length // 4

    def cosine(phase):
        moved = phase + quarter // 2
        quadrant = lax.div(moved, quarter) & 3
        angle = (lax.rem(moved, quarter) - quarter // 2).astype(jnp.float32) * turn
        square = angle * angle
        even = 1.0 + square * (
            -1 / 2 + square * (1 / 24 + square * (-1 / 720 + square * (1 / 40320)))
        )
        odd = angle * (
            1.0 + square * (-1 / 6 + square * (1 / 120 + square * (-1 / 5040 + square / 362880)))
        )
        value = jnp.where(quadrant & 1 == 0, even, odd)
        return jnp.where((quadrant == 1) | (quadrant == 2), -value, value)

    step = 16
    row = lax.broadcasted_iota(jnp.int32, (step, length), 0)
    time = lax.broadcasted_iota(jnp.int32, (step, length), 1)
    window = (0.5 - 0.5 * cosine(time)) * gain

    def some_rows(index, carry):
        first = pl.multiple_of(index * step, step)
        freq = (row + first) & (NF - 1)
        ahead = jnp.where(first < NF, 0, quarter)
        table_ref[pl.ds(first, step), :] = (window * cosine(freq * time + ahead)).astype(
            table_ref.dtype
        )
        return carry

    lax.fori_loop(0, rows // step, some_rows, 0)


def shifted_part(slot, sign, freqs, bands):
    step_freq, step_band = divmod(slot, bands)
    freq = lax.axis_index("freq") + (step_freq if sign > 0 else freqs - step_freq)
    band = lax.axis_index("band") + (step_band if sign > 0 else bands - step_band)
    return lax.rem(freq, freqs) * bands + lax.rem(band, bands)


def dft_far_kernel(sizes, far, points, offset, own_table, *refs):
    snap_ref, table_ref = refs[:2]
    outs = refs[len(refs) - 2 - len(far) : len(refs) - 2]
    buffer, arrived = refs[-2:]
    blocks, _, width = outs[0].shape
    copies = []
    for position, slot in enumerate(far):
        start = shifted_part(slot, 1, *sizes) * points + offset
        for block in range(blocks):
            index = position * blocks + block
            copy = pltpu.make_async_copy(
                snap_ref.at[block, :, pl.ds(pl.multiple_of(start, LANES), width)],
                buffer.at[:, index * width : (index + 1) * width],
                arrived.at[index],
            )
            copy.start()
            copies.append(copy)
    if own_table:
        make_table(table_ref)
    for copy in copies:
        copy.wait()
    spectra = jnp.dot(
        table_ref[...], buffer[...], preferred_element_type=jnp.float32
    ).astype(jnp.bfloat16)
    for index in range(len(copies)):
        position, block = divmod(index, blocks)
        outs[position][block] = spectra[:, index * width : (index + 1) * width]


def dft_far(snapshots, table, sizes, far, points, offset, width):
    blocks, length, _ = snapshots.shape
    count = len(far)
    own_table = table is None
    out_shape = [pltpu.VMEM((blocks, 2 * NF, width), jnp.bfloat16)] * count
    if own_table:
        out_shape = [pltpu.VMEM((2 * NF, length), jnp.bfloat16)] + out_shape
    return pl.pallas_call(
        functools.partial(dft_far_kernel, sizes, far, points, offset, own_table),
        out_shape=out_shape,
        in_specs=[ANY] + ([] if own_table else [VMEM]),
        out_specs=[VMEM] * len(out_shape),
        scratch_shapes=[
            pltpu.VMEM((length, count * blocks * width), jnp.bfloat16),
            pltpu.SemaphoreType.DMA((count * blocks,)),
        ],
        compiler_params=pltpu.CompilerParams(vmem_limit_bytes=12 * MIB),
        name="dft_far",
    )(snapshots, *([] if own_table else [table]))


def dft_rest_kernel(sizes, plan, points, table_ref, snap_ref, after_ref, *outs):
    table = table_ref[...]
    for (slot, offset, width), target in zip(plan, outs):
        step = math.gcd(width, 2 * LANES)
        part = shifted_part(slot, 1, *sizes) * points
        for piece in range(0, width, step):
            start = pl.multiple_of(part + (offset + piece), LANES)
            target[0, :, piece : piece + step] = jnp.dot(
                table, snap_ref[0, :, pl.ds(start, step)], preferred_element_type=jnp.float32
            ).astype(jnp.bfloat16)


def dft_rest(snapshots, table, sizes, plan, points, after):
    blocks, length, columns = snapshots.shape
    return pl.pallas_call(
        functools.partial(dft_rest_kernel, sizes, plan, points),
        out_shape=[
            jax.ShapeDtypeStruct((blocks, 2 * NF, width), jnp.bfloat16) for _, _, width in plan
        ],
        grid=(blocks,),
        in_specs=[
            pl.BlockSpec((2 * NF, length), lambda i: (0, 0)),
            pl.BlockSpec((1, length, columns), lambda i: (i, 0, 0)),
            ANY,
        ],
        out_specs=[pl.BlockSpec((1, 2 * NF, width), lambda i: (i, 0, 0)) for _, _, width in plan],
        compiler_params=pltpu.CompilerParams(vmem_limit_bytes=16 * MIB),
        cost_estimate=pl.CostEstimate(
            flops=4 * NF * length * columns * blocks,
            bytes_accessed=blocks * columns * (2 * length + 4 * NF),
            transcendentals=0,
        ),
        name="dft_rest",
    )(table, snapshots, after)


def interleave(spec_ref, source, slot, sizes, base):
    blocks, rows, _ = source.shape
    first = shifted_part(slot, -1, *sizes) * blocks
    for block in range(blocks):
        for tile in range(spec_ref.shape[0]):
            lanes = slice(base + tile * LANES, base + (tile + 1) * LANES)
            spec_ref[tile, pl.ds(first + block, rows, stride=NB), :] = source[
                block, :, lanes
            ].astype(jnp.float32)


def prepare_kernel(sizes, near, offset, *refs):
    ids_any, *sources = refs[:-3]
    ids_ref, spec_ref, ids_arrived = refs[-3:]
    ids_copy = pltpu.make_async_copy(ids_any, ids_ref, ids_arrived)
    ids_copy.start()
    for slot, source in zip(near, sources):
        interleave(spec_ref, source, slot, sizes, offset)
    ids_copy.wait()


def prepare(ids, near_sources, sizes, near, offset, width):
    rows = near_sources[0].shape[1]
    return pl.pallas_call(
        functools.partial(prepare_kernel, sizes, near, offset),
        out_shape=[
            pltpu.SMEM(ids.shape, jnp.int32),
            pltpu.VMEM((width // LANES, rows * NB, LANES), jnp.float32),
        ],
        in_specs=[ANY] + [VMEM] * len(near),
        out_specs=[SMEM, VMEM],
        scratch_shapes=[pltpu.SemaphoreType.DMA],
        compiler_params=pltpu.CompilerParams(vmem_limit_bytes=8 * MIB),
        name="prepare",
    )(ids, *near_sources)


def triad_kernel(sizes, slots, offset, prepared, has_prior, scale, *refs):
    ids_ref, weights_ref = refs[:2]
    rest = list(refs[2:])
    prior_ref = rest.pop(0) if has_prior else None
    if prepared:
        rest.pop(0)
    sources = [rest.pop(0) for _ in slots]
    out_ref, spec_ref = rest
    tiles = spec_ref.shape[0]
    own_points = weights_ref.shape[1] // (sizes[0] * sizes[1])
    here = shifted_part(0, 1, *sizes) * own_points + offset

    for (slot, base), source in zip(slots, sources):
        interleave(spec_ref, source, slot, sizes, base)
    weights = [
        weights_ref[:, pl.ds(pl.multiple_of(here + tile * LANES, LANES), LANES)]
        for tile in range(tiles)
    ]
    column = lax.broadcasted_iota(jnp.int32, (NB, LANES), 1) // NB
    owner = ((2 * PACK - column) & (2 * PACK - 1)) // 2

    def one_pack(group, carry):
        fields = []
        thirds = []
        for member in range(PACK):
            first = ids_ref[0, group * PACK + member]
            second = ids_ref[1, group * PACK + member]
            third = first + second
            field_re, field_im, third_re, third_im, third_neg = [], [], [], [], []
            for tile in range(tiles):
                def load(freq, part):
                    start = pl.multiple_of((freq + part * NF) * NB, NB)
                    return spec_ref[tile, pl.ds(start, NB), :]

                first_re, first_im = load(first, 0), load(first, 1)
                second_re, second_im = load(second, 0), load(second, 1)
                weight = weights[tile]
                field_re.append(weight * (first_re * second_re - first_im * second_im))
                field_im.append(weight * (first_re * second_im + first_im * second_re))
                third_re.append(load(third, 0))
                third_im.append(load(third, 1))
                third_neg.append(-third_re[-1])
            for parts, rows_of in (
                (field_re + field_im, fields),
                (third_re + third_im, thirds),
                (third_im + third_neg, thirds),
            ):
                rows_of.append(jnp.concatenate(parts, axis=1).astype(jnp.bfloat16))
        product = lax.dot_general(
            jnp.concatenate(fields, axis=0),
            jnp.concatenate([thirds[-column] for column in range(2 * PACK)], axis=0),
            (((1,), (1,)), ((), ())),
            preferred_element_type=jnp.float32,
        )
        total = product[0:NB]
        for member in range(1, PACK):
            total = jnp.where(owner == member, product[member * NB : (member + 1) * NB], total)
        total = total * scale
        if has_prior:
            total = total + prior_ref[group]
        out_ref[group] = total.astype(out_ref.dtype)
        return carry

    lax.fori_loop(0, out_ref.shape[0], one_pack, 0, unroll=16 if prepared else 4)


def triad_chunk(ids, weights, sources, slots, sizes, offset, width, prior, scale, prepared=None):
    rows = sources[0].shape[1]
    packs = ids.shape[1] // PACK
    spec_shape = (width // LANES, rows * NB, LANES)
    operands = [ids, weights] + ([] if prior is None else [prior])
    aliases = {}
    kept = jnp.float32 if prepared is None else jnp.bfloat16
    out_shape = [jax.ShapeDtypeStruct((packs, NB, LANES), kept)]
    scratch = []
    if prepared is None:
        scratch.append(pltpu.VMEM(spec_shape, jnp.float32))
    else:
        aliases = {len(operands): 1}
        operands.append(prepared)
        out_shape.append(jax.ShapeDtypeStruct(spec_shape, jnp.float32))
    operands += [pltpu.with_memory_space_constraint(x, pltpu.VMEM) for x in sources]
    return pl.pallas_call(
        functools.partial(
            triad_kernel, sizes, slots, offset, prepared is not None, prior is not None, scale
        ),
        out_shape=out_shape,
        in_specs=[SMEM] + [VMEM] * (len(operands) - 1),
        out_specs=[VMEM] * len(out_shape),
        scratch_shapes=scratch,
        input_output_aliases=aliases,
        compiler_params=pltpu.CompilerParams(vmem_limit_bytes=8 * MIB),
        cost_estimate=pl.CostEstimate(
            flops=packs * 2 * LANES * LANES * width,
            bytes_accessed=NB * rows * width * 2,
            transcendentals=0,
        ),
        name="triads",
    )(*operands)[0]


def finish_kernel(part_ref, out_ref):
    packs = out_ref.shape[0] // PACK
    group = lax.broadcasted_iota(jnp.int32, (8, LANES), 1) // NB
    for pack in range(packs):
        total = part_ref[pack].astype(jnp.float32)
        for device in range(1, part_ref.shape[0] // packs):
            total = total + part_ref[device * packs + pack].astype(jnp.float32)
        for half in range(2):
            skewed = pltpu.roll(total[half * 8 : half * 8 + 8], 0, 1, stride=NB, stride_axis=0)
            moved = skewed
            for shift in range(1, 8):
                moved = jnp.where(group == shift, pltpu.roll(skewed, 8 - shift, 0), moved)
            rows = pltpu.roll(moved, 0, 1, stride=NB, stride_axis=0)
            for column in range(2 * PACK):
                triad, part = divmod(column, 2)
                row = pack * PACK + triad
                start = part * NB * NB + half * LANES
                out_ref[row : row + 1, start : start + LANES] = rows[column : column + 1]


def finish(pieces, devices):
    rows = pieces.shape[0] // devices * PACK
    return pl.pallas_call(
        finish_kernel,
        out_shape=jax.ShapeDtypeStruct((rows, 2 * NB * NB), jnp.float32),
        in_specs=[VMEM],
        out_specs=VMEM,
        compiler_params=pltpu.CompilerParams(vmem_limit_bytes=8 * MIB),
        name="finish",
    )(pieces)


def mode_decomposition(snapshots, weights, triads):
    points = snapshots.shape[2]
    snapshots = pltpu.with_memory_space_constraint(snapshots, pltpu.HBM)
    freqs, bands = sizes = lax.axis_size("freq"), lax.axis_size("band")
    shards = freqs * bands
    own_points = points // shards
    widths = split_widths(own_points)
    offsets = [sum(widths[:i]) for i in range(len(widths))]
    scale = 1.0 / math.sqrt(points * lax.axis_size("space"))
    weights = weights.reshape(1, points)

    def send(value, slot):
        if slot == 0:
            return value
        shift_freq, shift_band = divmod(slot, bands)
        pairs = [
            (f * bands + b, (f + shift_freq) % freqs * bands + (b + shift_band) % bands)
            for f in range(freqs)
            for b in range(bands)
        ]
        return lax.ppermute(value, ("freq", "band"), pairs)

    def send_all(values, slots):
        return [send(value, slot) for slot, value in zip(slots, values)]

    near = list(range(bands))
    far = list(range(bands, shards))
    table, *outs = dft_far(snapshots, None, sizes, far, own_points, 0, widths[0])
    arrived = [send_all(outs, far)]
    outs = dft_far(snapshots, table, sizes, far, own_points, offsets[1], widths[1])
    arrived.append(send_all(outs, far))
    plan = [
        (slot, offset, width)
        for offset, width in list(zip(offsets, widths))[2:]
        for slot in far
    ] + [(slot, 0, own_points) for slot in near]
    rest = dft_rest(snapshots, table, sizes, plan, own_points, outs[0])
    for _ in range(2, len(widths)):
        arrived.append(send_all(rest[: len(far)], far))
        rest = rest[len(far) :]
    near_sources = send_all(rest, near)

    ids, ready = prepare(triads.T, near_sources, sizes, near, offsets[-1], widths[-1])
    total = None
    for chunk, (offset, width) in enumerate(zip(offsets, widths)):
        slots = [(slot, 0) for slot in far]
        sources = arrived[chunk]
        prepared = ready if chunk == len(widths) - 1 else None
        if prepared is None:
            slots = [(slot, offset) for slot in near] + slots
            sources = near_sources + sources
        total = triad_chunk(
            ids, weights, sources, slots, sizes, offset, width, total, scale, prepared
        )

    axes = ("space", "freq", "band")
    devices = lax.axis_size("space") * shards
    pieces = lax.all_to_all(total, axes, split_axis=0, concat_axis=0, tiled=True)
    return finish(pieces, devices)


def solution(mesh):
    return jax.shard_map(
        mode_decomposition,
        mesh=mesh,
        in_specs=(P(("freq", "band"), None, ("groups", "space")), P(("groups", "space")), P()),
        out_specs=P(("groups", "space", "freq", "band"), None),
        check_vma=False,
    )
```

```python
import functools
import math

import jax
import jax.numpy as jnp
from jax import lax
from jax.experimental import pallas as pl
from jax.experimental.pallas import tpu as pltpu
from jax.sharding import PartitionSpec as P


NB = 16
NF = 64
LANES = 128
PACK = 4
MIB = 1 << 20


VMEM = pl.BlockSpec(memory_space=pltpu.VMEM)
SMEM = pl.BlockSpec(memory_space=pltpu.SMEM)
ANY = pl.BlockSpec(memory_space=pl.ANY)


def split_widths(points):
    tiles = points // LANES
    rest = tiles - 2
    count = -(-rest // 3)
    middle = [rest // count + (i < rest % count) for i in range(count)]
    return [w * LANES for w in [1] + middle + [1]]


def make_table(table_ref):
    rows, length = table_ref.shape
    turn = 2.0 * math.pi / length
    gain = 1.0 / math.sqrt(3.0 * length / 8.0)
    quarter = length // 4

    def cosine(phase):
        moved = phase + quarter // 2
        quadrant = lax.div(moved, quarter) & 3
        angle = (lax.rem(moved, quarter) - quarter // 2).astype(jnp.float32) * turn
        square = angle * angle
        even = 1.0 + square * (
            -1 / 2 + square * (1 / 24 + square * (-1 / 720 + square * (1 / 40320)))
        )
        odd = angle * (
            1.0 + square * (-1 / 6 + square * (1 / 120 + square * (-1 / 5040 + square / 362880)))
        )
        value = jnp.where(quadrant & 1 == 0, even, odd)
        return jnp.where((quadrant == 1) | (quadrant == 2), -value, value)

    step = 16
    row = lax.broadcasted_iota(jnp.int32, (step, length), 0)
    time = lax.broadcasted_iota(jnp.int32, (step, length), 1)
    window = (0.5 - 0.5 * cosine(time)) * gain

    def some_rows(index, carry):
        first = pl.multiple_of(index * step, step)
        freq = (row + first) & (NF - 1)
        ahead = jnp.where(first < NF, 0, quarter)
        table_ref[pl.ds(first, step), :] = (window * cosine(freq * time + ahead)).astype(
            table_ref.dtype
        )
        return carry

    lax.fori_loop(0, rows // step, some_rows, 0)


def shifted_part(slot, sign, freqs, bands):
    step_freq, step_band = divmod(slot, bands)
    freq = lax.axis_index("freq") + (step_freq if sign > 0 else freqs - step_freq)
    band = lax.axis_index("band") + (step_band if sign > 0 else bands - step_band)
    return lax.rem(freq, freqs) * bands + lax.rem(band, bands)


def dft_far_kernel(sizes, far, points, offset, own_table, *refs):
    snap_ref, table_ref = refs[:2]
    outs = refs[len(refs) - 2 - len(far) : len(refs) - 2]
    buffer, arrived = refs[-2:]
    blocks, _, width = outs[0].shape
    copies = []
    for position, slot in enumerate(far):
        start = shifted_part(slot, 1, *sizes) * points + offset
        for block in range(blocks):
            index = position * blocks + block
            copy = pltpu.make_async_copy(
                snap_ref.at[block, :, pl.ds(pl.multiple_of(start, LANES), width)],
                buffer.at[:, index * width : (index + 1) * width],
                arrived.at[index],
            )
            copy.start()
            copies.append(copy)
    if own_table:
        make_table(table_ref)
    for copy in copies:
        copy.wait()
    spectra = jnp.dot(
        table_ref[...], buffer[...], preferred_element_type=jnp.float32
    ).astype(jnp.bfloat16)
    for index in range(len(copies)):
        position, block = divmod(index, blocks)
        outs[position][block] = spectra[:, index * width : (index + 1) * width]


def dft_far(snapshots, table, sizes, far, points, offset, width):
    blocks, length, _ = snapshots.shape
    count = len(far)
    own_table = table is None
    out_shape = [pltpu.VMEM((blocks, 2 * NF, width), jnp.bfloat16)] * count
    if own_table:
        out_shape = [pltpu.VMEM((2 * NF, length), jnp.bfloat16)] + out_shape
    return pl.pallas_call(
        functools.partial(dft_far_kernel, sizes, far, points, offset, own_table),
        out_shape=out_shape,
        in_specs=[ANY] + ([] if own_table else [VMEM]),
        out_specs=[VMEM] * len(out_shape),
        scratch_shapes=[
            pltpu.VMEM((length, count * blocks * width), jnp.bfloat16),
            pltpu.SemaphoreType.DMA((count * blocks,)),
        ],
        compiler_params=pltpu.CompilerParams(vmem_limit_bytes=12 * MIB),
        name="dft_far",
    )(snapshots, *([] if own_table else [table]))


def dft_rest_kernel(sizes, plan, points, table_ref, snap_ref, after_ref, *outs):
    table = table_ref[...]
    for (slot, offset, width), target in zip(plan, outs):
        step = math.gcd(width, 2 * LANES)
        part = shifted_part(slot, 1, *sizes) * points
        for piece in range(0, width, step):
            start = pl.multiple_of(part + (offset + piece), LANES)
            target[0, :, piece : piece + step] = jnp.dot(
                table, snap_ref[0, :, pl.ds(start, step)], preferred_element_type=jnp.float32
            ).astype(jnp.bfloat16)


def dft_rest(snapshots, table, sizes, plan, points, after):
    blocks, length, columns = snapshots.shape
    return pl.pallas_call(
        functools.partial(dft_rest_kernel, sizes, plan, points),
        out_shape=[
            jax.ShapeDtypeStruct((blocks, 2 * NF, width), jnp.bfloat16) for _, _, width in plan
        ],
        grid=(blocks,),
        in_specs=[
            pl.BlockSpec((2 * NF, length), lambda i: (0, 0)),
            pl.BlockSpec((1, length, columns), lambda i: (i, 0, 0)),
            ANY,
        ],
        out_specs=[pl.BlockSpec((1, 2 * NF, width), lambda i: (i, 0, 0)) for _, _, width in plan],
        compiler_params=pltpu.CompilerParams(vmem_limit_bytes=16 * MIB),
        cost_estimate=pl.CostEstimate(
            flops=4 * NF * length * columns * blocks,
            bytes_accessed=blocks * columns * (2 * length + 4 * NF),
            transcendentals=0,
        ),
        name="dft_rest",
    )(table, snapshots, after)


def interleave(spec_ref, source, slot, sizes, base):
    blocks, rows, _ = source.shape
    first = shifted_part(slot, -1, *sizes) * blocks
    for block in range(blocks):
        for tile in range(spec_ref.shape[0]):
            lanes = slice(base + tile * LANES, base + (tile + 1) * LANES)
            spec_ref[tile, pl.ds(first + block, rows, stride=NB), :] = source[
                block, :, lanes
            ].astype(jnp.float32)


def prepare_kernel(sizes, near, offset, *refs):
    ids_any, *sources = refs[:-3]
    ids_ref, spec_ref, ids_arrived = refs[-3:]
    ids_copy = pltpu.make_async_copy(ids_any, ids_ref, ids_arrived)
    ids_copy.start()
    for slot, source in zip(near, sources):
        interleave(spec_ref, source, slot, sizes, offset)
    ids_copy.wait()


def prepare(ids, near_sources, sizes, near, offset, width):
    rows = near_sources[0].shape[1]
    return pl.pallas_call(
        functools.partial(prepare_kernel, sizes, near, offset),
        out_shape=[
            pltpu.SMEM(ids.shape, jnp.int32),
            pltpu.VMEM((width // LANES, rows * NB, LANES), jnp.float32),
        ],
        in_specs=[ANY] + [VMEM] * len(near),
        out_specs=[SMEM, VMEM],
        scratch_shapes=[pltpu.SemaphoreType.DMA],
        compiler_params=pltpu.CompilerParams(vmem_limit_bytes=8 * MIB),
        name="prepare",
    )(ids, *near_sources)


def triad_kernel(sizes, slots, offset, prepared, has_prior, scale, *refs):
    ids_ref, weights_ref = refs[:2]
    rest = list(refs[2:])
    prior_ref = rest.pop(0) if has_prior else None
    if prepared:
        rest.pop(0)
    sources = [rest.pop(0) for _ in slots]
    out_ref, spec_ref = rest
    tiles = spec_ref.shape[0]
    own_points = weights_ref.shape[1] // (sizes[0] * sizes[1])
    here = shifted_part(0, 1, *sizes) * own_points + offset

    for (slot, base), source in zip(slots, sources):
        interleave(spec_ref, source, slot, sizes, base)
    weights = [
        weights_ref[:, pl.ds(pl.multiple_of(here + tile * LANES, LANES), LANES)]
        for tile in range(tiles)
    ]
    numbers = [-column % (2 * PACK) for column in range(2 * PACK)]
    column = lax.broadcasted_iota(jnp.int32, (NB, LANES), 1) // NB
    owner = (2 * PACK - column) & (PACK - 1)

    def one_pack(group, carry):
        fields = []
        thirds = []
        for member in range(PACK):
            first = ids_ref[0, group * PACK + member]
            second = ids_ref[1, group * PACK + member]
            third = first + second
            field_re, field_im, third_re, third_im, third_neg = [], [], [], [], []
            for tile in range(tiles):
                def load(freq, part):
                    start = pl.multiple_of((freq + part * NF) * NB, NB)
                    return spec_ref[tile, pl.ds(start, NB), :]

                first_re, first_im = load(first, 0), load(first, 1)
                second_re, second_im = load(second, 0), load(second, 1)
                weight = weights[tile]
                field_re.append(weight * (first_re * second_re - first_im * second_im))
                field_im.append(weight * (first_re * second_im + first_im * second_re))
                third_re.append(load(third, 0))
                third_im.append(load(third, 1))
                third_neg.append(-third_re[-1])
            for parts, rows_of in (
                (field_re + field_im, fields),
                (third_re + third_im, thirds),
                (third_im + third_neg, thirds),
            ):
                rows_of.append(jnp.concatenate(parts, axis=1).astype(jnp.bfloat16))
        product = lax.dot_general(
            jnp.concatenate(fields, axis=0),
            jnp.concatenate(
                [thirds[number % PACK * 2 + number // PACK] for number in numbers], axis=0
            ),
            (((1,), (1,)), ((), ())),
            preferred_element_type=jnp.float32,
        )
        total = product[0:NB]
        for member in range(1, PACK):
            total = jnp.where(owner == member, product[member * NB : (member + 1) * NB], total)
        total = total * scale
        if has_prior:
            total = total + prior_ref[group]
        out_ref[group] = total.astype(out_ref.dtype)
        return carry

    lax.fori_loop(0, out_ref.shape[0], one_pack, 0, unroll=16 if prepared else 4)


def triad_chunk(ids, weights, sources, slots, sizes, offset, width, prior, scale, prepared=None):
    rows = sources[0].shape[1]
    packs = ids.shape[1] // PACK
    spec_shape = (width // LANES, rows * NB, LANES)
    operands = [ids, weights] + ([] if prior is None else [prior])
    aliases = {}
    kept = jnp.float32 if prepared is None else jnp.bfloat16
    out_shape = [jax.ShapeDtypeStruct((packs, NB, LANES), kept)]
    scratch = []
    if prepared is None:
        scratch.append(pltpu.VMEM(spec_shape, jnp.float32))
    else:
        aliases = {len(operands): 1}
        operands.append(prepared)
        out_shape.append(jax.ShapeDtypeStruct(spec_shape, jnp.float32))
    operands += [pltpu.with_memory_space_constraint(x, pltpu.VMEM) for x in sources]
    return pl.pallas_call(
        functools.partial(
            triad_kernel, sizes, slots, offset, prepared is not None, prior is not None, scale
        ),
        out_shape=out_shape,
        in_specs=[SMEM] + [VMEM] * (len(operands) - 1),
        out_specs=[VMEM] * len(out_shape),
        scratch_shapes=scratch,
        input_output_aliases=aliases,
        compiler_params=pltpu.CompilerParams(vmem_limit_bytes=8 * MIB),
        cost_estimate=pl.CostEstimate(
            flops=packs * 2 * LANES * LANES * width,
            bytes_accessed=NB * rows * width * 2,
            transcendentals=0,
        ),
        name="triads",
    )(*operands)[0]


def finish_kernel(part_ref, out_ref):
    packs = out_ref.shape[0] // PACK
    group = lax.broadcasted_iota(jnp.int32, (8, LANES), 1) // NB
    for pack in range(packs):
        total = part_ref[pack].astype(jnp.float32)
        for device in range(1, part_ref.shape[0] // packs):
            total = total + part_ref[device * packs + pack].astype(jnp.float32)
        for half in range(2):
            skewed = pltpu.roll(total[half * 8 : half * 8 + 8], 0, 1, stride=NB, stride_axis=0)
            moved = skewed
            for shift in range(1, 8):
                moved = jnp.where(group == shift, pltpu.roll(skewed, 8 - shift, 0), moved)
            rows = pltpu.roll(moved, 0, 1, stride=NB, stride_axis=0)
            for part in range(2):
                start = part * NB * NB + half * LANES
                out_ref[pack * PACK : (pack + 1) * PACK, start : start + LANES] = rows[
                    part * PACK : (part + 1) * PACK
                ]


def finish(pieces, devices):
    rows = pieces.shape[0] // devices * PACK
    return pl.pallas_call(
        finish_kernel,
        out_shape=jax.ShapeDtypeStruct((rows, 2 * NB * NB), jnp.float32),
        in_specs=[VMEM],
        out_specs=VMEM,
        compiler_params=pltpu.CompilerParams(vmem_limit_bytes=8 * MIB),
        name="finish",
    )(pieces)


def mode_decomposition(snapshots, weights, triads):
    points = snapshots.shape[2]
    snapshots = pltpu.with_memory_space_constraint(snapshots, pltpu.HBM)
    freqs, bands = sizes = lax.axis_size("freq"), lax.axis_size("band")
    shards = freqs * bands
    own_points = points // shards
    widths = split_widths(own_points)
    offsets = [sum(widths[:i]) for i in range(len(widths))]
    scale = 1.0 / math.sqrt(points * lax.axis_size("space"))
    weights = weights.reshape(1, points)

    def send(value, slot):
        if slot == 0:
            return value
        shift_freq, shift_band = divmod(slot, bands)
        pairs = [
            (f * bands + b, (f + shift_freq) % freqs * bands + (b + shift_band) % bands)
            for f in range(freqs)
            for b in range(bands)
        ]
        return lax.ppermute(value, ("freq", "band"), pairs)

    def send_all(values, slots):
        return [send(value, slot) for slot, value in zip(slots, values)]

    near = list(range(bands))
    far = list(range(bands, shards))
    table, *outs = dft_far(snapshots, None, sizes, far, own_points, 0, widths[0])
    arrived = [send_all(outs, far)]
    outs = dft_far(snapshots, table, sizes, far, own_points, offsets[1], widths[1])
    arrived.append(send_all(outs, far))
    plan = [
        (slot, offset, width)
        for offset, width in list(zip(offsets, widths))[2:]
        for slot in far
    ] + [(slot, 0, own_points) for slot in near]
    rest = dft_rest(snapshots, table, sizes, plan, own_points, outs[0])
    for _ in range(2, len(widths)):
        arrived.append(send_all(rest[: len(far)], far))
        rest = rest[len(far) :]
    near_sources = send_all(rest, near)

    ids, ready = prepare(triads.T, near_sources, sizes, near, offsets[-1], widths[-1])
    total = None
    for chunk, (offset, width) in enumerate(zip(offsets, widths)):
        slots = [(slot, 0) for slot in far]
        sources = arrived[chunk]
        prepared = ready if chunk == len(widths) - 1 else None
        if prepared is None:
            slots = [(slot, offset) for slot in near] + slots
            sources = near_sources + sources
        total = triad_chunk(
            ids, weights, sources, slots, sizes, offset, width, total, scale, prepared
        )

    axes = ("space", "freq", "band")
    devices = lax.axis_size("space") * shards
    pieces = lax.all_to_all(total, axes, split_axis=0, concat_axis=0, tiled=True)
    return finish(pieces, devices)


def solution(mesh):
    return jax.shard_map(
        mode_decomposition,
        mesh=mesh,
        in_specs=(P(("freq", "band"), None, ("groups", "space")), P(("groups", "space")), P()),
        out_specs=P(("groups", "space", "freq", "band"), None),
        check_vma=False,
    )
```

```python
import functools
import math

import jax
import jax.numpy as jnp
from jax import lax
from jax.experimental import pallas as pl
from jax.experimental.pallas import tpu as pltpu
from jax.sharding import PartitionSpec as P


NB = 16
NF = 64
LANES = 128
PACK = 4
MIB = 1 << 20


VMEM = pl.BlockSpec(memory_space=pltpu.VMEM)
SMEM = pl.BlockSpec(memory_space=pltpu.SMEM)
ANY = pl.BlockSpec(memory_space=pl.ANY)


def split_widths(points):
    tiles = points // LANES
    rest = tiles - 2
    late = min(rest, 2)
    count = -(-(rest - late) // 4)
    middle = [(rest - late) // count + (i < (rest - late) % count) for i in range(count)] + [late]
    return [w * LANES for w in [1] + middle + [1]]


def make_table(table_ref):
    rows, length = table_ref.shape
    turn = 2.0 * math.pi / length
    gain = 1.0 / math.sqrt(3.0 * length / 8.0)
    quarter = length // 4

    def cosine(phase):
        moved = phase + quarter // 2
        quadrant = lax.div(moved, quarter) & 3
        angle = (lax.rem(moved, quarter) - quarter // 2).astype(jnp.float32) * turn
        square = angle * angle
        even = 1.0 + square * (
            -1 / 2 + square * (1 / 24 + square * (-1 / 720 + square * (1 / 40320)))
        )
        odd = angle * (
            1.0 + square * (-1 / 6 + square * (1 / 120 + square * (-1 / 5040 + square / 362880)))
        )
        value = jnp.where(quadrant & 1 == 0, even, odd)
        return jnp.where((quadrant == 1) | (quadrant == 2), -value, value)

    step = 16
    row = lax.broadcasted_iota(jnp.int32, (step, length), 0)
    time = lax.broadcasted_iota(jnp.int32, (step, length), 1)
    window = (0.5 - 0.5 * cosine(time)) * gain

    def some_rows(index, carry):
        first = pl.multiple_of(index * step, step)
        freq = (row + first) & (NF - 1)
        ahead = jnp.where(first < NF, 0, quarter)
        table_ref[pl.ds(first, step), :] = (window * cosine(freq * time + ahead)).astype(
            table_ref.dtype
        )
        return carry

    lax.fori_loop(0, rows // step, some_rows, 0)


def shifted_part(slot, sign, freqs, bands):
    step_freq, step_band = divmod(slot, bands)
    freq = lax.axis_index("freq") + (step_freq if sign > 0 else freqs - step_freq)
    band = lax.axis_index("band") + (step_band if sign > 0 else bands - step_band)
    return lax.rem(freq, freqs) * bands + lax.rem(band, bands)


def dft_far_kernel(sizes, far, points, offset, own_table, *refs):
    snap_ref, table_ref = refs[:2]
    outs = refs[len(refs) - 2 - len(far) : len(refs) - 2]
    buffer, arrived = refs[-2:]
    blocks, _, width = outs[0].shape
    copies = []
    for position, slot in enumerate(far):
        start = shifted_part(slot, 1, *sizes) * points + offset
        for block in range(blocks):
            index = position * blocks + block
            copy = pltpu.make_async_copy(
                snap_ref.at[block, :, pl.ds(pl.multiple_of(start, LANES), width)],
                buffer.at[:, index * width : (index + 1) * width],
                arrived.at[index],
            )
            copy.start()
            copies.append(copy)
    if own_table:
        make_table(table_ref)
    for copy in copies:
        copy.wait()
    spectra = jnp.dot(
        table_ref[...], buffer[...], preferred_element_type=jnp.float32
    ).astype(jnp.bfloat16)
    for index in range(len(copies)):
        position, block = divmod(index, blocks)
        outs[position][block] = spectra[:, index * width : (index + 1) * width]


def dft_far(snapshots, table, sizes, far, points, offset, width):
    blocks, length, _ = snapshots.shape
    count = len(far)
    own_table = table is None
    out_shape = [pltpu.VMEM((blocks, 2 * NF, width), jnp.bfloat16)] * count
    if own_table:
        out_shape = [pltpu.VMEM((2 * NF, length), jnp.bfloat16)] + out_shape
    return pl.pallas_call(
        functools.partial(dft_far_kernel, sizes, far, points, offset, own_table),
        out_shape=out_shape,
        in_specs=[ANY] + ([] if own_table else [VMEM]),
        out_specs=[VMEM] * len(out_shape),
        scratch_shapes=[
            pltpu.VMEM((length, count * blocks * width), jnp.bfloat16),
            pltpu.SemaphoreType.DMA((count * blocks,)),
        ],
        compiler_params=pltpu.CompilerParams(vmem_limit_bytes=12 * MIB),
        name="dft_far",
    )(snapshots, *([] if own_table else [table]))


def dft_rest_kernel(sizes, plan, points, table_ref, snap_ref, after_ref, *outs):
    table = table_ref[...]
    for (slot, offset, width), target in zip(plan, outs):
        step = math.gcd(width, 2 * LANES)
        part = shifted_part(slot, 1, *sizes) * points
        for piece in range(0, width, step):
            start = pl.multiple_of(part + (offset + piece), LANES)
            target[0, :, piece : piece + step] = jnp.dot(
                table, snap_ref[0, :, pl.ds(start, step)], preferred_element_type=jnp.float32
            ).astype(jnp.bfloat16)


def dft_rest(snapshots, table, sizes, plan, points, after):
    blocks, length, columns = snapshots.shape
    return pl.pallas_call(
        functools.partial(dft_rest_kernel, sizes, plan, points),
        out_shape=[
            jax.ShapeDtypeStruct((blocks, 2 * NF, width), jnp.bfloat16) for _, _, width in plan
        ],
        grid=(blocks,),
        in_specs=[
            pl.BlockSpec((2 * NF, length), lambda i: (0, 0)),
            pl.BlockSpec((1, length, columns), lambda i: (i, 0, 0)),
            ANY,
        ],
        out_specs=[pl.BlockSpec((1, 2 * NF, width), lambda i: (i, 0, 0)) for _, _, width in plan],
        compiler_params=pltpu.CompilerParams(vmem_limit_bytes=16 * MIB),
        cost_estimate=pl.CostEstimate(
            flops=4 * NF * length * columns * blocks,
            bytes_accessed=blocks * columns * (2 * length + 4 * NF),
            transcendentals=0,
        ),
        name="dft_rest",
    )(table, snapshots, after)


def interleave(spec_ref, source, slot, sizes, base):
    blocks, rows, _ = source.shape
    first = shifted_part(slot, -1, *sizes) * blocks
    for block in range(blocks):
        for tile in range(spec_ref.shape[0]):
            lanes = slice(base + tile * LANES, base + (tile + 1) * LANES)
            spec_ref[tile, pl.ds(first + block, rows, stride=NB), :] = source[
                block, :, lanes
            ].astype(jnp.float32)


def prepare_kernel(sizes, near, offset, *refs):
    ids_any, *sources = refs[:-3]
    ids_ref, spec_ref, ids_arrived = refs[-3:]
    ids_copy = pltpu.make_async_copy(ids_any, ids_ref, ids_arrived)
    ids_copy.start()
    for slot, source in zip(near, sources):
        interleave(spec_ref, source, slot, sizes, offset)
    ids_copy.wait()


def prepare(ids, near_sources, sizes, near, offset, width):
    rows = near_sources[0].shape[1]
    return pl.pallas_call(
        functools.partial(prepare_kernel, sizes, near, offset),
        out_shape=[
            pltpu.SMEM(ids.shape, jnp.int32),
            pltpu.VMEM((width // LANES, rows * NB, LANES), jnp.float32),
        ],
        in_specs=[ANY] + [VMEM] * len(near),
        out_specs=[SMEM, VMEM],
        scratch_shapes=[pltpu.SemaphoreType.DMA],
        compiler_params=pltpu.CompilerParams(vmem_limit_bytes=8 * MIB),
        name="prepare",
    )(ids, *near_sources)


def triad_kernel(sizes, slots, offset, prepared, has_prior, scale, *refs):
    ids_ref, weights_ref = refs[:2]
    rest = list(refs[2:])
    prior_ref = rest.pop(0) if has_prior else None
    if prepared:
        rest.pop(0)
    sources = [rest.pop(0) for _ in slots]
    out_ref, spec_ref = rest
    tiles = spec_ref.shape[0]
    own_points = weights_ref.shape[1] // (sizes[0] * sizes[1])
    here = shifted_part(0, 1, *sizes) * own_points + offset

    for (slot, base), source in zip(slots, sources):
        interleave(spec_ref, source, slot, sizes, base)
    weights = [
        weights_ref[:, pl.ds(pl.multiple_of(here + tile * LANES, LANES), LANES)]
        for tile in range(tiles)
    ]
    column = lax.broadcasted_iota(jnp.int32, (NB, LANES), 1) // NB
    owner = ((2 * PACK - column) & (2 * PACK - 1)) // 2

    def one_pack(group, carry):
        fields = []
        thirds = []
        for member in range(PACK):
            first = ids_ref[0, group * PACK + member]
            second = ids_ref[1, group * PACK + member]
            third = first + second
            field_re, field_im, third_re, third_im, third_neg = [], [], [], [], []
            for tile in range(tiles):
                def load(freq, part):
                    start = pl.multiple_of((freq + part * NF) * NB, NB)
                    return spec_ref[tile, pl.ds(start, NB), :]

                first_re, first_im = load(first, 0), load(first, 1)
                second_re, second_im = load(second, 0), load(second, 1)
                weight = weights[tile]
                field_re.append(weight * (first_re * second_re - first_im * second_im))
                field_im.append(weight * (first_re * second_im + first_im * second_re))
                third_re.append(load(third, 0))
                third_im.append(load(third, 1))
                third_neg.append(-third_re[-1])
            for parts, rows_of in (
                (field_re + field_im, fields),
                (third_re + third_im, thirds),
                (third_im + third_neg, thirds),
            ):
                rows_of.append(jnp.concatenate(parts, axis=1).astype(jnp.bfloat16))
        product = lax.dot_general(
            jnp.concatenate(fields, axis=0),
            jnp.concatenate([thirds[-column] for column in range(2 * PACK)], axis=0),
            (((1,), (1,)), ((), ())),
            preferred_element_type=jnp.float32,
        )
        total = product[0:NB]
        for member in range(1, PACK):
            total = jnp.where(owner == member, product[member * NB : (member + 1) * NB], total)
        total = total * scale
        if has_prior:
            total = total + prior_ref[group]
        out_ref[group] = total.astype(out_ref.dtype)
        return carry

    lax.fori_loop(0, out_ref.shape[0], one_pack, 0, unroll=16 if prepared else 4)


def triad_chunk(ids, weights, sources, slots, sizes, offset, width, prior, scale, prepared=None):
    rows = sources[0].shape[1]
    packs = ids.shape[1] // PACK
    spec_shape = (width // LANES, rows * NB, LANES)
    operands = [ids, weights] + ([] if prior is None else [prior])
    aliases = {}
    kept = jnp.float32 if prepared is None else jnp.bfloat16
    out_shape = [jax.ShapeDtypeStruct((packs, NB, LANES), kept)]
    scratch = []
    if prepared is None:
        scratch.append(pltpu.VMEM(spec_shape, jnp.float32))
    else:
        aliases = {len(operands): 1}
        operands.append(prepared)
        out_shape.append(jax.ShapeDtypeStruct(spec_shape, jnp.float32))
    operands += [pltpu.with_memory_space_constraint(x, pltpu.VMEM) for x in sources]
    return pl.pallas_call(
        functools.partial(
            triad_kernel, sizes, slots, offset, prepared is not None, prior is not None, scale
        ),
        out_shape=out_shape,
        in_specs=[SMEM] + [VMEM] * (len(operands) - 1),
        out_specs=[VMEM] * len(out_shape),
        scratch_shapes=scratch,
        input_output_aliases=aliases,
        compiler_params=pltpu.CompilerParams(vmem_limit_bytes=8 * MIB),
        cost_estimate=pl.CostEstimate(
            flops=packs * 2 * LANES * LANES * width,
            bytes_accessed=NB * rows * width * 2,
            transcendentals=0,
        ),
        name="triads",
    )(*operands)[0]


def finish_kernel(part_ref, out_ref):
    packs = out_ref.shape[0] // PACK
    group = lax.broadcasted_iota(jnp.int32, (8, LANES), 1) // NB
    for pack in range(packs):
        total = part_ref[pack].astype(jnp.float32)
        for device in range(1, part_ref.shape[0] // packs):
            total = total + part_ref[device * packs + pack].astype(jnp.float32)
        for half in range(2):
            skewed = pltpu.roll(total[half * 8 : half * 8 + 8], 0, 1, stride=NB, stride_axis=0)
            moved = skewed
            for shift in range(1, 8):
                moved = jnp.where(group == shift, pltpu.roll(skewed, 8 - shift, 0), moved)
            rows = pltpu.roll(moved, 0, 1, stride=NB, stride_axis=0)
            for column in range(2 * PACK):
                triad, part = divmod(column, 2)
                row = pack * PACK + triad
                start = part * NB * NB + half * LANES
                out_ref[row : row + 1, start : start + LANES] = rows[column : column + 1]


def finish(pieces, devices):
    rows = pieces.shape[0] // devices * PACK
    return pl.pallas_call(
        finish_kernel,
        out_shape=jax.ShapeDtypeStruct((rows, 2 * NB * NB), jnp.float32),
        in_specs=[VMEM],
        out_specs=VMEM,
        compiler_params=pltpu.CompilerParams(vmem_limit_bytes=8 * MIB),
        name="finish",
    )(pieces)


def mode_decomposition(snapshots, weights, triads):
    points = snapshots.shape[2]
    snapshots = pltpu.with_memory_space_constraint(snapshots, pltpu.HBM)
    freqs, bands = sizes = lax.axis_size("freq"), lax.axis_size("band")
    shards = freqs * bands
    own_points = points // shards
    widths = split_widths(own_points)
    offsets = [sum(widths[:i]) for i in range(len(widths))]
    scale = 1.0 / math.sqrt(points * lax.axis_size("space"))
    weights = weights.reshape(1, points)

    def send(value, slot):
        if slot == 0:
            return value
        shift_freq, shift_band = divmod(slot, bands)
        pairs = [
            (f * bands + b, (f + shift_freq) % freqs * bands + (b + shift_band) % bands)
            for f in range(freqs)
            for b in range(bands)
        ]
        return lax.ppermute(value, ("freq", "band"), pairs)

    def send_all(values, slots):
        return [send(value, slot) for slot, value in zip(slots, values)]

    near = list(range(bands))
    far = list(range(bands, shards))
    table, *outs = dft_far(snapshots, None, sizes, far, own_points, 0, widths[0])
    arrived = [send_all(outs, far)]
    outs = dft_far(snapshots, table, sizes, far, own_points, offsets[1], widths[1])
    arrived.append(send_all(outs, far))
    plan = [
        (slot, offset, width)
        for offset, width in list(zip(offsets, widths))[2:]
        for slot in far
    ] + [(slot, 0, own_points) for slot in near]
    rest = dft_rest(snapshots, table, sizes, plan, own_points, outs[0])
    for _ in range(2, len(widths)):
        arrived.append(send_all(rest[: len(far)], far))
        rest = rest[len(far) :]
    near_sources = send_all(rest, near)

    ids, ready = prepare(triads.T, near_sources, sizes, near, offsets[-1], widths[-1])
    total = None
    for chunk, (offset, width) in enumerate(zip(offsets, widths)):
        slots = [(slot, 0) for slot in far]
        sources = arrived[chunk]
        prepared = ready if chunk == len(widths) - 1 else None
        if prepared is None:
            slots = [(slot, offset) for slot in near] + slots
            sources = near_sources + sources
        total = triad_chunk(
            ids, weights, sources, slots, sizes, offset, width, total, scale, prepared
        )

    axes = ("space", "freq", "band")
    devices = lax.axis_size("space") * shards
    pieces = lax.all_to_all(total, axes, split_axis=0, concat_axis=0, tiled=True)
    return finish(pieces, devices)


def solution(mesh):
    return jax.shard_map(
        mode_decomposition,
        mesh=mesh,
        in_specs=(P(("freq", "band"), None, ("groups", "space")), P(("groups", "space")), P()),
        out_specs=P(("groups", "space", "freq", "band"), None),
        check_vma=False,
    )
```

```python
import functools
import math

import jax
import jax.numpy as jnp
from jax import lax
from jax.experimental import pallas as pl
from jax.experimental.pallas import tpu as pltpu
from jax.sharding import PartitionSpec as P


NB = 16
NF = 64
LANES = 128
PACK = 4
MIB = 1 << 20


VMEM = pl.BlockSpec(memory_space=pltpu.VMEM)
SMEM = pl.BlockSpec(memory_space=pltpu.SMEM)
ANY = pl.BlockSpec(memory_space=pl.ANY)


def split_widths(points):
    tiles = points // LANES
    rest = tiles - 2
    late = min(rest, 2)
    count = -(-(rest - late) // 4)
    middle = [(rest - late) // count + (i < (rest - late) % count) for i in range(count)] + [late]
    return [w * LANES for w in [1] + middle + [1]]


def make_table(table_ref):
    rows, length = table_ref.shape
    turn = 2.0 * math.pi / length
    gain = 1.0 / math.sqrt(3.0 * length / 8.0)
    quarter = length // 4

    def cosine(phase):
        moved = phase + quarter // 2
        quadrant = lax.div(moved, quarter) & 3
        angle = (lax.rem(moved, quarter) - quarter // 2).astype(jnp.float32) * turn
        square = angle * angle
        even = 1.0 + square * (
            -1 / 2 + square * (1 / 24 + square * (-1 / 720 + square * (1 / 40320)))
        )
        odd = angle * (
            1.0 + square * (-1 / 6 + square * (1 / 120 + square * (-1 / 5040 + square / 362880)))
        )
        value = jnp.where(quadrant & 1 == 0, even, odd)
        return jnp.where((quadrant == 1) | (quadrant == 2), -value, value)

    step = 16
    row = lax.broadcasted_iota(jnp.int32, (step, length), 0)
    time = lax.broadcasted_iota(jnp.int32, (step, length), 1)
    window = (0.5 - 0.5 * cosine(time)) * gain

    def some_rows(index, carry):
        first = pl.multiple_of(index * step, step)
        freq = (row + first) & (NF - 1)
        ahead = jnp.where(first < NF, 0, quarter)
        table_ref[pl.ds(first, step), :] = (window * cosine(freq * time + ahead)).astype(
            table_ref.dtype
        )
        return carry

    lax.fori_loop(0, rows // step, some_rows, 0)


def shifted_part(slot, sign, freqs, bands):
    step_freq, step_band = divmod(slot, bands)
    freq = lax.axis_index("freq") + (step_freq if sign > 0 else freqs - step_freq)
    band = lax.axis_index("band") + (step_band if sign > 0 else bands - step_band)
    return lax.rem(freq, freqs) * bands + lax.rem(band, bands)


def dft_far_kernel(sizes, far, points, offset, own_table, *refs):
    snap_ref, table_ref = refs[:2]
    outs = refs[len(refs) - 2 - len(far) : len(refs) - 2]
    buffer, arrived = refs[-2:]
    blocks, _, width = outs[0].shape
    copies = []
    for position, slot in enumerate(far):
        start = shifted_part(slot, 1, *sizes) * points + offset
        for block in range(blocks):
            index = position * blocks + block
            copy = pltpu.make_async_copy(
                snap_ref.at[block, :, pl.ds(pl.multiple_of(start, LANES), width)],
                buffer.at[:, index * width : (index + 1) * width],
                arrived.at[index],
            )
            copy.start()
            copies.append(copy)
    if own_table:
        make_table(table_ref)
    for copy in copies:
        copy.wait()
    spectra = jnp.dot(
        table_ref[...], buffer[...], preferred_element_type=jnp.float32
    ).astype(jnp.bfloat16)
    for index in range(len(copies)):
        position, block = divmod(index, blocks)
        outs[position][block] = spectra[:, index * width : (index + 1) * width]


def dft_far(snapshots, table, sizes, far, points, offset, width):
    blocks, length, _ = snapshots.shape
    count = len(far)
    own_table = table is None
    out_shape = [pltpu.VMEM((blocks, 2 * NF, width), jnp.bfloat16)] * count
    if own_table:
        out_shape = [pltpu.VMEM((2 * NF, length), jnp.bfloat16)] + out_shape
    return pl.pallas_call(
        functools.partial(dft_far_kernel, sizes, far, points, offset, own_table),
        out_shape=out_shape,
        in_specs=[ANY] + ([] if own_table else [VMEM]),
        out_specs=[VMEM] * len(out_shape),
        scratch_shapes=[
            pltpu.VMEM((length, count * blocks * width), jnp.bfloat16),
            pltpu.SemaphoreType.DMA((count * blocks,)),
        ],
        compiler_params=pltpu.CompilerParams(vmem_limit_bytes=12 * MIB),
        name="dft_far",
    )(snapshots, *([] if own_table else [table]))


def dft_rest_kernel(sizes, plan, points, table_ref, snap_ref, after_ref, *outs):
    table = table_ref[...]
    for (slot, offset, width), target in zip(plan, outs):
        step = math.gcd(width, 2 * LANES)
        part = shifted_part(slot, 1, *sizes) * points
        for piece in range(0, width, step):
            start = pl.multiple_of(part + (offset + piece), LANES)
            target[0, :, piece : piece + step] = jnp.dot(
                table, snap_ref[0, :, pl.ds(start, step)], preferred_element_type=jnp.float32
            ).astype(jnp.bfloat16)


def dft_rest(snapshots, table, sizes, plan, points, after):
    blocks, length, columns = snapshots.shape
    return pl.pallas_call(
        functools.partial(dft_rest_kernel, sizes, plan, points),
        out_shape=[
            jax.ShapeDtypeStruct((blocks, 2 * NF, width), jnp.bfloat16) for _, _, width in plan
        ],
        grid=(blocks,),
        in_specs=[
            pl.BlockSpec((2 * NF, length), lambda i: (0, 0)),
            pl.BlockSpec((1, length, columns), lambda i: (i, 0, 0)),
            ANY,
        ],
        out_specs=[pl.BlockSpec((1, 2 * NF, width), lambda i: (i, 0, 0)) for _, _, width in plan],
        compiler_params=pltpu.CompilerParams(vmem_limit_bytes=16 * MIB),
        cost_estimate=pl.CostEstimate(
            flops=4 * NF * length * columns * blocks,
            bytes_accessed=blocks * columns * (2 * length + 4 * NF),
            transcendentals=0,
        ),
        name="dft_rest",
    )(table, snapshots, after)


def interleave(spec_ref, source, slot, sizes, base):
    blocks, rows, _ = source.shape
    first = shifted_part(slot, -1, *sizes) * blocks
    for block in range(blocks):
        for tile in range(spec_ref.shape[0]):
            lanes = slice(base + tile * LANES, base + (tile + 1) * LANES)
            spec_ref[tile, pl.ds(first + block, rows, stride=NB), :] = source[
                block, :, lanes
            ].astype(jnp.float32)


def prepare_kernel(sizes, near, offset, *refs):
    ids_any, *sources = refs[:-3]
    ids_ref, spec_ref, ids_arrived = refs[-3:]
    ids_copy = pltpu.make_async_copy(ids_any, ids_ref, ids_arrived)
    ids_copy.start()
    for slot, source in zip(near, sources):
        interleave(spec_ref, source, slot, sizes, offset)
    ids_copy.wait()


def prepare(ids, near_sources, sizes, near, offset, width):
    rows = near_sources[0].shape[1]
    return pl.pallas_call(
        functools.partial(prepare_kernel, sizes, near, offset),
        out_shape=[
            pltpu.SMEM(ids.shape, jnp.int32),
            pltpu.VMEM((width // LANES, rows * NB, LANES), jnp.float32),
        ],
        in_specs=[ANY] + [VMEM] * len(near),
        out_specs=[SMEM, VMEM],
        scratch_shapes=[pltpu.SemaphoreType.DMA],
        compiler_params=pltpu.CompilerParams(vmem_limit_bytes=8 * MIB),
        name="prepare",
    )(ids, *near_sources)


def triad_kernel(sizes, slots, offset, prepared, has_prior, scale, *refs):
    ids_ref, weights_ref = refs[:2]
    rest = list(refs[2:])
    prior_ref = rest.pop(0) if has_prior else None
    if prepared:
        rest.pop(0)
    sources = [rest.pop(0) for _ in slots]
    out_ref, spec_ref = rest
    tiles = spec_ref.shape[0]
    own_points = weights_ref.shape[1] // (sizes[0] * sizes[1])
    here = shifted_part(0, 1, *sizes) * own_points + offset

    for (slot, base), source in zip(slots, sources):
        interleave(spec_ref, source, slot, sizes, base)
    weights = [
        weights_ref[:, pl.ds(pl.multiple_of(here + tile * LANES, LANES), LANES)]
        for tile in range(tiles)
    ]
    column = lax.broadcasted_iota(jnp.int32, (NB, LANES), 1) // NB
    owner = ((2 * PACK - column) & (2 * PACK - 1)) // 2

    def one_pack(group, carry):
        fields = []
        thirds = []
        for member in range(PACK):
            first = ids_ref[0, group * PACK + member]
            second = ids_ref[1, group * PACK + member]
            third = first + second
            field_re, field_im, third_re, third_im, third_neg = [], [], [], [], []
            for tile in range(tiles):
                def load(freq, part):
                    start = pl.multiple_of((freq + part * NF) * NB, NB)
                    return spec_ref[tile, pl.ds(start, NB), :]

                first_re, first_im = load(first, 0), load(first, 1)
                second_re, second_im = load(second, 0), load(second, 1)
                weight = weights[tile]
                field_re.append(weight * (first_re * second_re - first_im * second_im))
                field_im.append(weight * (first_re * second_im + first_im * second_re))
                third_re.append(load(third, 0))
                third_im.append(load(third, 1))
                third_neg.append(-third_re[-1])
            for parts, rows_of in (
                (field_re + field_im, fields),
                (third_re + third_im, thirds),
                (third_im + third_neg, thirds),
            ):
                rows_of.append(jnp.concatenate(parts, axis=1).astype(jnp.bfloat16))
        product = lax.dot_general(
            jnp.concatenate(fields, axis=0),
            jnp.concatenate([thirds[-column] for column in range(2 * PACK)], axis=0),
            (((1,), (1,)), ((), ())),
            preferred_element_type=jnp.float32,
        )
        total = product[0:NB]
        for member in range(1, PACK):
            total = jnp.where(owner == member, product[member * NB : (member + 1) * NB], total)
        total = total * scale
        if has_prior:
            total = total + prior_ref[group]
        out_ref[group] = total.astype(out_ref.dtype)
        return carry

    lax.fori_loop(0, out_ref.shape[0], one_pack, 0, unroll=16 if prepared else 4)


def triad_chunk(ids, weights, sources, slots, sizes, offset, width, prior, scale, prepared=None):
    rows = sources[0].shape[1]
    packs = ids.shape[1] // PACK
    spec_shape = (width // LANES, rows * NB, LANES)
    operands = [ids, weights] + ([] if prior is None else [prior])
    aliases = {}
    kept = jnp.float32 if prepared is None else jnp.bfloat16
    out_shape = [jax.ShapeDtypeStruct((packs, NB, LANES), kept)]
    scratch = []
    if prepared is None:
        scratch.append(pltpu.VMEM(spec_shape, jnp.float32))
    else:
        aliases = {len(operands): 1}
        operands.append(prepared)
        out_shape.append(jax.ShapeDtypeStruct(spec_shape, jnp.float32))
    operands += [pltpu.with_memory_space_constraint(x, pltpu.VMEM) for x in sources]
    return pl.pallas_call(
        functools.partial(
            triad_kernel, sizes, slots, offset, prepared is not None, prior is not None, scale
        ),
        out_shape=out_shape,
        in_specs=[SMEM] + [VMEM] * (len(operands) - 1),
        out_specs=[VMEM] * len(out_shape),
        scratch_shapes=scratch,
        input_output_aliases=aliases,
        compiler_params=pltpu.CompilerParams(vmem_limit_bytes=8 * MIB),
        cost_estimate=pl.CostEstimate(
            flops=packs * 2 * LANES * LANES * width,
            bytes_accessed=NB * rows * width * 2,
            transcendentals=0,
        ),
        name="triads",
    )(*operands)[0]


def finish_kernel(part_ref, out_ref):
    packs = out_ref.shape[0] // PACK
    group = lax.broadcasted_iota(jnp.int32, (8, LANES), 1) // NB
    for pack in range(packs):
        total = part_ref[pack].astype(jnp.float32)
        for device in range(1, part_ref.shape[0] // packs):
            total = total + part_ref[device * packs + pack].astype(jnp.float32)
        for half in range(2):
            skewed = pltpu.roll(total[half * 8 : half * 8 + 8], 0, 1, stride=NB, stride_axis=0)
            moved = skewed
            for shift in range(1, 8):
                moved = jnp.where(group == shift, pltpu.roll(skewed, 8 - shift, 0), moved)
            rows = pltpu.roll(moved, 0, 1, stride=NB, stride_axis=0)
            for column in range(2 * PACK):
                triad, part = divmod(column, 2)
                row = pack * PACK + triad
                start = part * NB * NB + half * LANES
                out_ref[row : row + 1, start : start + LANES] = rows[column : column + 1]


def finish(pieces, devices):
    rows = pieces.shape[0] // devices * PACK
    return pl.pallas_call(
        finish_kernel,
        out_shape=jax.ShapeDtypeStruct((rows, 2 * NB * NB), jnp.float32),
        in_specs=[VMEM],
        out_specs=VMEM,
        compiler_params=pltpu.CompilerParams(vmem_limit_bytes=8 * MIB),
        name="finish",
    )(pieces)


def mode_decomposition(snapshots, weights, triads):
    points = snapshots.shape[2]
    snapshots = pltpu.with_memory_space_constraint(snapshots, pltpu.HBM)
    freqs, bands = sizes = lax.axis_size("freq"), lax.axis_size("band")
    shards = freqs * bands
    own_points = points // shards
    widths = split_widths(own_points)
    offsets = [sum(widths[:i]) for i in range(len(widths))]
    scale = 1.0 / math.sqrt(points * lax.axis_size("space"))
    weights = weights.reshape(1, points)

    def send(value, slot):
        if slot == 0:
            return value
        shift_freq, shift_band = divmod(slot, bands)
        pairs = [
            (f * bands + b, (f + shift_freq) % freqs * bands + (b + shift_band) % bands)
            for f in range(freqs)
            for b in range(bands)
        ]
        return lax.ppermute(value, ("freq", "band"), pairs)

    def send_all(values, slots):
        return [send(value, slot) for slot, value in zip(slots, values)]

    near = list(range(bands))
    far = list(range(bands, shards))
    table, *outs = dft_far(snapshots, None, sizes, far[:1], own_points, 0, widths[0])
    arrived = [send_all(outs, far[:1])]
    outs = dft_far(snapshots, table, sizes, far[1:], own_points, 0, widths[0])
    arrived[0] += send_all(outs, far[1:])
    outs = dft_far(snapshots, table, sizes, far, own_points, offsets[1], widths[1])
    arrived.append(send_all(outs, far))
    plan = [
        (slot, offset, width)
        for offset, width in list(zip(offsets, widths))[2:]
        for slot in far
    ] + [(slot, 0, own_points) for slot in near]
    rest = dft_rest(snapshots, table, sizes, plan, own_points, outs[0])
    for _ in range(2, len(widths)):
        arrived.append(send_all(rest[: len(far)], far))
        rest = rest[len(far) :]
    near_sources = send_all(rest, near)

    ids, ready = prepare(triads.T, near_sources, sizes, near, offsets[-1], widths[-1])
    total = None
    for chunk, (offset, width) in enumerate(zip(offsets, widths)):
        slots = [(slot, 0) for slot in far]
        sources = arrived[chunk]
        prepared = ready if chunk == len(widths) - 1 else None
        if prepared is None:
            slots = [(slot, offset) for slot in near] + slots
            sources = near_sources + sources
        total = triad_chunk(
            ids, weights, sources, slots, sizes, offset, width, total, scale, prepared
        )

    axes = ("space", "freq", "band")
    devices = lax.axis_size("space") * shards
    pieces = lax.all_to_all(total, axes, split_axis=0, concat_axis=0, tiled=True)
    return finish(pieces, devices)


def solution(mesh):
    return jax.shard_map(
        mode_decomposition,
        mesh=mesh,
        in_specs=(P(("freq", "band"), None, ("groups", "space")), P(("groups", "space")), P()),
        out_specs=P(("groups", "space", "freq", "band"), None),
        check_vma=False,
    )
```

```python
import functools
import math

import jax
import jax.numpy as jnp
from jax import lax
from jax.experimental import pallas as pl
from jax.experimental.pallas import tpu as pltpu
from jax.sharding import PartitionSpec as P


NB = 16
NF = 64
LANES = 128
PACK = 4
MIB = 1 << 20


VMEM = pl.BlockSpec(memory_space=pltpu.VMEM)
SMEM = pl.BlockSpec(memory_space=pltpu.SMEM)
ANY = pl.BlockSpec(memory_space=pl.ANY)


def split_widths(points):
    tiles = points // LANES
    rest = tiles - 2
    late = min(rest, 2)
    count = -(-(rest - late) // 4)
    middle = [(rest - late) // count + (i < (rest - late) % count) for i in range(count)] + [late]
    return [w * LANES for w in [1] + middle + [1]]


def make_table(table_ref):
    rows, length = table_ref.shape
    turn = 2.0 * math.pi / length
    gain = 1.0 / math.sqrt(3.0 * length / 8.0)
    quarter = length // 4

    def cosine(phase):
        moved = phase + quarter // 2
        quadrant = lax.div(moved, quarter) & 3
        angle = (lax.rem(moved, quarter) - quarter // 2).astype(jnp.float32) * turn
        square = angle * angle
        even = 1.0 + square * (
            -1 / 2 + square * (1 / 24 + square * (-1 / 720 + square * (1 / 40320)))
        )
        odd = angle * (
            1.0 + square * (-1 / 6 + square * (1 / 120 + square * (-1 / 5040 + square / 362880)))
        )
        value = jnp.where(quadrant & 1 == 0, even, odd)
        return jnp.where((quadrant == 1) | (quadrant == 2), -value, value)

    step = 16
    row = lax.broadcasted_iota(jnp.int32, (step, length), 0)
    time = lax.broadcasted_iota(jnp.int32, (step, length), 1)
    window = (0.5 - 0.5 * cosine(time)) * gain

    def some_rows(index, carry):
        first = pl.multiple_of(index * step, step)
        freq = (row + first) & (NF - 1)
        ahead = jnp.where(first < NF, 0, quarter)
        table_ref[pl.ds(first, step), :] = (window * cosine(freq * time + ahead)).astype(
            table_ref.dtype
        )
        return carry

    lax.fori_loop(0, rows // step, some_rows, 0)


def shifted_part(slot, sign, freqs, bands):
    step_freq, step_band = divmod(slot, bands)
    freq = lax.axis_index("freq") + (step_freq if sign > 0 else freqs - step_freq)
    band = lax.axis_index("band") + (step_band if sign > 0 else bands - step_band)
    return lax.rem(freq, freqs) * bands + lax.rem(band, bands)


def dft_far_kernel(sizes, far, points, offset, own_table, *refs):
    snap_ref, table_ref = refs[:2]
    outs = refs[len(refs) - 2 - len(far) : len(refs) - 2]
    buffer, arrived = refs[-2:]
    blocks, _, width = outs[0].shape
    copies = []
    for position, slot in enumerate(far):
        start = shifted_part(slot, 1, *sizes) * points + offset
        for block in range(blocks):
            index = position * blocks + block
            copy = pltpu.make_async_copy(
                snap_ref.at[block, :, pl.ds(pl.multiple_of(start, LANES), width)],
                buffer.at[:, index * width : (index + 1) * width],
                arrived.at[index],
            )
            copy.start()
            copies.append(copy)
    if own_table:
        make_table(table_ref)
    for copy in copies:
        copy.wait()
    spectra = jnp.dot(
        table_ref[...], buffer[...], preferred_element_type=jnp.float32
    ).astype(jnp.bfloat16)
    for index in range(len(copies)):
        position, block = divmod(index, blocks)
        outs[position][block] = spectra[:, index * width : (index + 1) * width]


def dft_far(snapshots, table, sizes, far, points, offset, width):
    blocks, length, _ = snapshots.shape
    count = len(far)
    own_table = table is None
    out_shape = [pltpu.VMEM((blocks, 2 * NF, width), jnp.bfloat16)] * count
    if own_table:
        out_shape = [pltpu.VMEM((2 * NF, length), jnp.bfloat16)] + out_shape
    return pl.pallas_call(
        functools.partial(dft_far_kernel, sizes, far, points, offset, own_table),
        out_shape=out_shape,
        in_specs=[ANY] + ([] if own_table else [VMEM]),
        out_specs=[VMEM] * len(out_shape),
        scratch_shapes=[
            pltpu.VMEM((length, count * blocks * width), jnp.bfloat16),
            pltpu.SemaphoreType.DMA((count * blocks,)),
        ],
        compiler_params=pltpu.CompilerParams(vmem_limit_bytes=12 * MIB),
        name="dft_far",
    )(snapshots, *([] if own_table else [table]))


def dft_rest_kernel(sizes, plan, points, table_ref, snap_ref, after_ref, *outs):
    table = table_ref[...]
    for (slot, offset, width), target in zip(plan, outs):
        step = math.gcd(width, 2 * LANES)
        part = shifted_part(slot, 1, *sizes) * points
        for piece in range(0, width, step):
            start = pl.multiple_of(part + (offset + piece), LANES)
            target[0, :, piece : piece + step] = jnp.dot(
                table, snap_ref[0, :, pl.ds(start, step)], preferred_element_type=jnp.float32
            ).astype(jnp.bfloat16)


def dft_rest(snapshots, table, sizes, plan, points, after):
    blocks, length, columns = snapshots.shape
    return pl.pallas_call(
        functools.partial(dft_rest_kernel, sizes, plan, points),
        out_shape=[
            jax.ShapeDtypeStruct((blocks, 2 * NF, width), jnp.bfloat16) for _, _, width in plan
        ],
        grid=(blocks,),
        in_specs=[
            pl.BlockSpec((2 * NF, length), lambda i: (0, 0)),
            pl.BlockSpec((1, length, columns), lambda i: (i, 0, 0)),
            ANY,
        ],
        out_specs=[pl.BlockSpec((1, 2 * NF, width), lambda i: (i, 0, 0)) for _, _, width in plan],
        compiler_params=pltpu.CompilerParams(vmem_limit_bytes=16 * MIB),
        cost_estimate=pl.CostEstimate(
            flops=4 * NF * length * columns * blocks,
            bytes_accessed=blocks * columns * (2 * length + 4 * NF),
            transcendentals=0,
        ),
        name="dft_rest",
    )(table, snapshots, after)


def interleave(spec_ref, source, slot, sizes, base):
    blocks, rows, _ = source.shape
    first = shifted_part(slot, -1, *sizes) * blocks
    for block in range(blocks):
        for tile in range(spec_ref.shape[0]):
            lanes = slice(base + tile * LANES, base + (tile + 1) * LANES)
            spec_ref[tile, pl.ds(first + block, rows, stride=NB), :] = source[
                block, :, lanes
            ].astype(jnp.float32)


def prepare_kernel(sizes, near, offset, *refs):
    ids_any, *sources = refs[:-3]
    ids_ref, spec_ref, ids_arrived = refs[-3:]
    ids_copy = pltpu.make_async_copy(ids_any, ids_ref, ids_arrived)
    ids_copy.start()
    for slot, source in zip(near, sources):
        interleave(spec_ref, source, slot, sizes, offset)
    ids_copy.wait()


def prepare(ids, near_sources, sizes, near, offset, width):
    rows = near_sources[0].shape[1]
    return pl.pallas_call(
        functools.partial(prepare_kernel, sizes, near, offset),
        out_shape=[
            pltpu.SMEM(ids.shape, jnp.int32),
            pltpu.VMEM((width // LANES, rows * NB, LANES), jnp.float32),
        ],
        in_specs=[ANY] + [VMEM] * len(near),
        out_specs=[SMEM, VMEM],
        scratch_shapes=[pltpu.SemaphoreType.DMA],
        compiler_params=pltpu.CompilerParams(vmem_limit_bytes=8 * MIB),
        name="prepare",
    )(ids, *near_sources)


def extend_kernel(sizes, slots, *refs):
    for slot, source in zip(slots, refs[1:-1]):
        interleave(refs[-1], source, slot, sizes, 0)


def extend(spec, sources, sizes, slots):
    return pl.pallas_call(
        functools.partial(extend_kernel, sizes, slots),
        out_shape=pltpu.VMEM(spec.shape, jnp.float32),
        in_specs=[VMEM] * (1 + len(sources)),
        out_specs=VMEM,
        input_output_aliases={0: 0},
        compiler_params=pltpu.CompilerParams(vmem_limit_bytes=8 * MIB),
        name="extend",
    )(spec, *sources)


def triad_kernel(sizes, slots, offset, prepared, has_prior, scale, *refs):
    ids_ref, weights_ref = refs[:2]
    rest = list(refs[2:])
    prior_ref = rest.pop(0) if has_prior else None
    if prepared:
        rest.pop(0)
    sources = [rest.pop(0) for _ in slots]
    out_ref, spec_ref = rest
    tiles = spec_ref.shape[0]
    own_points = weights_ref.shape[1] // (sizes[0] * sizes[1])
    here = shifted_part(0, 1, *sizes) * own_points + offset

    for (slot, base), source in zip(slots, sources):
        interleave(spec_ref, source, slot, sizes, base)
    weights = [
        weights_ref[:, pl.ds(pl.multiple_of(here + tile * LANES, LANES), LANES)]
        for tile in range(tiles)
    ]
    column = lax.broadcasted_iota(jnp.int32, (NB, LANES), 1) // NB
    owner = ((2 * PACK - column) & (2 * PACK - 1)) // 2

    def one_pack(group, carry):
        fields = []
        thirds = []
        for member in range(PACK):
            first = ids_ref[0, group * PACK + member]
            second = ids_ref[1, group * PACK + member]
            third = first + second
            field_re, field_im, third_re, third_im, third_neg = [], [], [], [], []
            for tile in range(tiles):
                def load(freq, part):
                    start = pl.multiple_of((freq + part * NF) * NB, NB)
                    return spec_ref[tile, pl.ds(start, NB), :]

                first_re, first_im = load(first, 0), load(first, 1)
                second_re, second_im = load(second, 0), load(second, 1)
                weight = weights[tile]
                field_re.append(weight * (first_re * second_re - first_im * second_im))
                field_im.append(weight * (first_re * second_im + first_im * second_re))
                third_re.append(load(third, 0))
                third_im.append(load(third, 1))
                third_neg.append(-third_re[-1])
            for parts, rows_of in (
                (field_re + field_im, fields),
                (third_re + third_im, thirds),
                (third_im + third_neg, thirds),
            ):
                rows_of.append(jnp.concatenate(parts, axis=1).astype(jnp.bfloat16))
        product = lax.dot_general(
            jnp.concatenate(fields, axis=0),
            jnp.concatenate([thirds[-column] for column in range(2 * PACK)], axis=0),
            (((1,), (1,)), ((), ())),
            preferred_element_type=jnp.float32,
        )
        total = product[0:NB]
        for member in range(1, PACK):
            total = jnp.where(owner == member, product[member * NB : (member + 1) * NB], total)
        total = total * scale
        if has_prior:
            total = total + prior_ref[group]
        out_ref[group] = total.astype(out_ref.dtype)
        return carry

    lax.fori_loop(0, out_ref.shape[0], one_pack, 0, unroll=16 if prepared else 4)


def triad_chunk(ids, weights, sources, slots, sizes, offset, width, prior, scale, prepared=None):
    rows = sources[0].shape[1]
    packs = ids.shape[1] // PACK
    spec_shape = (width // LANES, rows * NB, LANES)
    operands = [ids, weights] + ([] if prior is None else [prior])
    aliases = {}
    kept = jnp.float32 if prepared is None else jnp.bfloat16
    out_shape = [jax.ShapeDtypeStruct((packs, NB, LANES), kept)]
    scratch = []
    if prepared is None:
        scratch.append(pltpu.VMEM(spec_shape, jnp.float32))
    else:
        aliases = {len(operands): 1}
        operands.append(prepared)
        out_shape.append(jax.ShapeDtypeStruct(spec_shape, jnp.float32))
    operands += [pltpu.with_memory_space_constraint(x, pltpu.VMEM) for x in sources]
    return pl.pallas_call(
        functools.partial(
            triad_kernel, sizes, slots, offset, prepared is not None, prior is not None, scale
        ),
        out_shape=out_shape,
        in_specs=[SMEM] + [VMEM] * (len(operands) - 1),
        out_specs=[VMEM] * len(out_shape),
        scratch_shapes=scratch,
        input_output_aliases=aliases,
        compiler_params=pltpu.CompilerParams(vmem_limit_bytes=8 * MIB),
        cost_estimate=pl.CostEstimate(
            flops=packs * 2 * LANES * LANES * width,
            bytes_accessed=NB * rows * width * 2,
            transcendentals=0,
        ),
        name="triads",
    )(*operands)[0]


def finish_kernel(part_ref, out_ref):
    packs = out_ref.shape[0] // PACK
    group = lax.broadcasted_iota(jnp.int32, (8, LANES), 1) // NB
    for pack in range(packs):
        total = part_ref[pack].astype(jnp.float32)
        for device in range(1, part_ref.shape[0] // packs):
            total = total + part_ref[device * packs + pack].astype(jnp.float32)
        for half in range(2):
            skewed = pltpu.roll(total[half * 8 : half * 8 + 8], 0, 1, stride=NB, stride_axis=0)
            moved = skewed
            for shift in range(1, 8):
                moved = jnp.where(group == shift, pltpu.roll(skewed, 8 - shift, 0), moved)
            rows = pltpu.roll(moved, 0, 1, stride=NB, stride_axis=0)
            for column in range(2 * PACK):
                triad, part = divmod(column, 2)
                row = pack * PACK + triad
                start = part * NB * NB + half * LANES
                out_ref[row : row + 1, start : start + LANES] = rows[column : column + 1]


def finish(pieces, devices):
    rows = pieces.shape[0] // devices * PACK
    return pl.pallas_call(
        finish_kernel,
        out_shape=jax.ShapeDtypeStruct((rows, 2 * NB * NB), jnp.float32),
        in_specs=[VMEM],
        out_specs=VMEM,
        compiler_params=pltpu.CompilerParams(vmem_limit_bytes=8 * MIB),
        name="finish",
    )(pieces)


def mode_decomposition(snapshots, weights, triads):
    points = snapshots.shape[2]
    snapshots = pltpu.with_memory_space_constraint(snapshots, pltpu.HBM)
    freqs, bands = sizes = lax.axis_size("freq"), lax.axis_size("band")
    shards = freqs * bands
    own_points = points // shards
    widths = split_widths(own_points)
    offsets = [sum(widths[:i]) for i in range(len(widths))]
    scale = 1.0 / math.sqrt(points * lax.axis_size("space"))
    weights = weights.reshape(1, points)

    def send(value, slot):
        if slot == 0:
            return value
        shift_freq, shift_band = divmod(slot, bands)
        pairs = [
            (f * bands + b, (f + shift_freq) % freqs * bands + (b + shift_band) % bands)
            for f in range(freqs)
            for b in range(bands)
        ]
        return lax.ppermute(value, ("freq", "band"), pairs)

    def send_all(values, slots):
        return [send(value, slot) for slot, value in zip(slots, values)]

    near = list(range(bands))
    far = list(range(bands, shards))
    table, *outs = dft_far(snapshots, None, sizes, far, own_points, 0, widths[0])
    arrived = [send_all(outs, far)]
    outs = dft_far(snapshots, table, sizes, far, own_points, offsets[1], widths[1])
    arrived.append(send_all(outs, far))
    plan = [
        (slot, offset, width)
        for offset, width in list(zip(offsets, widths))[2:]
        for slot in far
    ] + [(slot, 0, own_points) for slot in near]
    rest = dft_rest(snapshots, table, sizes, plan, own_points, outs[0])
    for _ in range(2, len(widths)):
        arrived.append(send_all(rest[: len(far)], far))
        rest = rest[len(far) :]
    near_sources = send_all(rest, near)

    ids, ready = prepare(triads.T, near_sources, sizes, near, offsets[-1], widths[-1])
    total = None
    for chunk, (offset, width) in enumerate(zip(offsets, widths)):
        slots = [(slot, 0) for slot in far]
        sources = arrived[chunk]
        prepared = None
        if chunk == len(widths) - 1:
            prepared = extend(ready, sources[:-1], sizes, far[:-1])
            slots, sources = slots[-1:], sources[-1:]
        else:
            slots = [(slot, offset) for slot in near] + slots
            sources = near_sources + sources
        total = triad_chunk(
            ids, weights, sources, slots, sizes, offset, width, total, scale, prepared
        )

    axes = ("space", "freq", "band")
    devices = lax.axis_size("space") * shards
    pieces = lax.all_to_all(total, axes, split_axis=0, concat_axis=0, tiled=True)
    return finish(pieces, devices)


def solution(mesh):
    return jax.shard_map(
        mode_decomposition,
        mesh=mesh,
        in_specs=(P(("freq", "band"), None, ("groups", "space")), P(("groups", "space")), P()),
        out_specs=P(("groups", "space", "freq", "band"), None),
        check_vma=False,
    )
```

```python
import functools
import math

import jax
import jax.numpy as jnp
from jax import lax
from jax.experimental import pallas as pl
from jax.experimental.pallas import tpu as pltpu
from jax.sharding import PartitionSpec as P


NB = 16
NF = 64
LANES = 128
PACK = 4
MIB = 1 << 20


VMEM = pl.BlockSpec(memory_space=pltpu.VMEM)
SMEM = pl.BlockSpec(memory_space=pltpu.SMEM)
ANY = pl.BlockSpec(memory_space=pl.ANY)


def split_widths(points):
    tiles = points // LANES
    rest = tiles - 2
    late = min(rest, 2)
    count = -(-(rest - late) // 4)
    middle = [(rest - late) // count + (i < (rest - late) % count) for i in range(count)] + [late]
    return [w * LANES for w in [1] + middle + [1]]


def make_table(table_ref):
    rows, length = table_ref.shape
    turn = 2.0 * math.pi / length
    gain = 1.0 / math.sqrt(3.0 * length / 8.0)
    quarter = length // 4

    def cosine(phase):
        moved = phase + quarter // 2
        quadrant = lax.div(moved, quarter) & 3
        angle = (lax.rem(moved, quarter) - quarter // 2).astype(jnp.float32) * turn
        square = angle * angle
        even = 1.0 + square * (
            -1 / 2 + square * (1 / 24 + square * (-1 / 720 + square * (1 / 40320)))
        )
        odd = angle * (
            1.0 + square * (-1 / 6 + square * (1 / 120 + square * (-1 / 5040 + square / 362880)))
        )
        value = jnp.where(quadrant & 1 == 0, even, odd)
        return jnp.where((quadrant == 1) | (quadrant == 2), -value, value)

    step = 16
    row = lax.broadcasted_iota(jnp.int32, (step, length), 0)
    time = lax.broadcasted_iota(jnp.int32, (step, length), 1)
    window = (0.5 - 0.5 * cosine(time)) * gain

    def some_rows(index, carry):
        first = pl.multiple_of(index * step, step)
        freq = (row + first) & (NF - 1)
        ahead = jnp.where(first < NF, 0, quarter)
        table_ref[pl.ds(first, step), :] = (window * cosine(freq * time + ahead)).astype(
            table_ref.dtype
        )
        return carry

    lax.fori_loop(0, rows // step, some_rows, 0)


def shifted_part(slot, sign, freqs, bands):
    step_freq, step_band = divmod(slot, bands)
    freq = lax.axis_index("freq") + (step_freq if sign > 0 else freqs - step_freq)
    band = lax.axis_index("band") + (step_band if sign > 0 else bands - step_band)
    return lax.rem(freq, freqs) * bands + lax.rem(band, bands)


def dft_far_kernel(sizes, far, points, offset, own_table, *refs):
    snap_ref, table_ref = refs[:2]
    outs = refs[len(refs) - 2 - len(far) : len(refs) - 2]
    buffer, arrived = refs[-2:]
    blocks, _, width = outs[0].shape
    copies = []
    for position, slot in enumerate(far):
        start = shifted_part(slot, 1, *sizes) * points + offset
        for block in range(blocks):
            index = position * blocks + block
            copy = pltpu.make_async_copy(
                snap_ref.at[block, :, pl.ds(pl.multiple_of(start, LANES), width)],
                buffer.at[:, index * width : (index + 1) * width],
                arrived.at[index],
            )
            copy.start()
            copies.append(copy)
    if own_table:
        make_table(table_ref)
    for copy in copies:
        copy.wait()
    spectra = jnp.dot(
        table_ref[...], buffer[...], preferred_element_type=jnp.float32
    ).astype(jnp.bfloat16)
    for index in range(len(copies)):
        position, block = divmod(index, blocks)
        outs[position][block] = spectra[:, index * width : (index + 1) * width]


def dft_far(snapshots, table, sizes, far, points, offset, width):
    blocks, length, _ = snapshots.shape
    count = len(far)
    own_table = table is None
    out_shape = [pltpu.VMEM((blocks, 2 * NF, width), jnp.bfloat16)] * count
    if own_table:
        out_shape = [pltpu.VMEM((2 * NF, length), jnp.bfloat16)] + out_shape
    return pl.pallas_call(
        functools.partial(dft_far_kernel, sizes, far, points, offset, own_table),
        out_shape=out_shape,
        in_specs=[ANY] + ([] if own_table else [VMEM]),
        out_specs=[VMEM] * len(out_shape),
        scratch_shapes=[
            pltpu.VMEM((length, count * blocks * width), jnp.bfloat16),
            pltpu.SemaphoreType.DMA((count * blocks,)),
        ],
        compiler_params=pltpu.CompilerParams(vmem_limit_bytes=12 * MIB),
        name="dft_far",
    )(snapshots, *([] if own_table else [table]))


def dft_rest_kernel(sizes, plan, points, table_ref, snap_ref, after_ref, *outs):
    table = table_ref[...]
    for (slot, offset, width), target in zip(plan, outs):
        step = math.gcd(width, 2 * LANES)
        part = shifted_part(slot, 1, *sizes) * points
        for piece in range(0, width, step):
            start = pl.multiple_of(part + (offset + piece), LANES)
            target[0, :, piece : piece + step] = jnp.dot(
                table, snap_ref[0, :, pl.ds(start, step)], preferred_element_type=jnp.float32
            ).astype(jnp.bfloat16)


def dft_rest(snapshots, table, sizes, plan, points, after):
    blocks, length, columns = snapshots.shape
    return pl.pallas_call(
        functools.partial(dft_rest_kernel, sizes, plan, points),
        out_shape=[
            jax.ShapeDtypeStruct((blocks, 2 * NF, width), jnp.bfloat16) for _, _, width in plan
        ],
        grid=(blocks,),
        in_specs=[
            pl.BlockSpec((2 * NF, length), lambda i: (0, 0)),
            pl.BlockSpec((1, length, columns), lambda i: (i, 0, 0)),
            ANY,
        ],
        out_specs=[pl.BlockSpec((1, 2 * NF, width), lambda i: (i, 0, 0)) for _, _, width in plan],
        compiler_params=pltpu.CompilerParams(vmem_limit_bytes=16 * MIB),
        cost_estimate=pl.CostEstimate(
            flops=4 * NF * length * columns * blocks,
            bytes_accessed=blocks * columns * (2 * length + 4 * NF),
            transcendentals=0,
        ),
        name="dft_rest",
    )(table, snapshots, after)


def interleave(spec_ref, source, slot, sizes, base):
    blocks, rows, _ = source.shape
    first = shifted_part(slot, -1, *sizes) * blocks
    for block in range(blocks):
        for tile in range(spec_ref.shape[0]):
            lanes = slice(base + tile * LANES, base + (tile + 1) * LANES)
            spec_ref[tile, pl.ds(first + block, rows, stride=NB), :] = source[
                block, :, lanes
            ].astype(jnp.float32)


def prepare_kernel(sizes, near, offset, *refs):
    ids_any, *sources = refs[:-3]
    ids_ref, spec_ref, ids_arrived = refs[-3:]
    ids_copy = pltpu.make_async_copy(ids_any, ids_ref, ids_arrived)
    ids_copy.start()
    for slot, source in zip(near, sources):
        interleave(spec_ref, source, slot, sizes, offset)
    ids_copy.wait()


def prepare(ids, near_sources, sizes, near, offset, width):
    rows = near_sources[0].shape[1]
    return pl.pallas_call(
        functools.partial(prepare_kernel, sizes, near, offset),
        out_shape=[
            pltpu.SMEM(ids.shape, jnp.int32),
            pltpu.VMEM((width // LANES, rows * NB, LANES), jnp.float32),
        ],
        in_specs=[ANY] + [VMEM] * len(near),
        out_specs=[SMEM, VMEM],
        scratch_shapes=[pltpu.SemaphoreType.DMA],
        compiler_params=pltpu.CompilerParams(vmem_limit_bytes=8 * MIB),
        name="prepare",
    )(ids, *near_sources)


def extend_kernel(sizes, slots, *refs):
    for slot, source in zip(slots, refs[2:-1]):
        interleave(refs[-1], source, slot, sizes, 0)


def extend(spec, after, sources, sizes, slots):
    return pl.pallas_call(
        functools.partial(extend_kernel, sizes, slots),
        out_shape=pltpu.VMEM(spec.shape, jnp.float32),
        in_specs=[VMEM, ANY] + [VMEM] * len(sources),
        out_specs=VMEM,
        input_output_aliases={0: 0},
        compiler_params=pltpu.CompilerParams(vmem_limit_bytes=8 * MIB),
        name="extend",
    )(spec, after, *sources)


def triad_kernel(sizes, slots, offset, prepared, has_prior, scale, *refs):
    ids_ref, weights_ref = refs[:2]
    rest = list(refs[2:])
    prior_ref = rest.pop(0) if has_prior else None
    if prepared:
        rest.pop(0)
    sources = [rest.pop(0) for _ in slots]
    out_ref, spec_ref = rest
    tiles = spec_ref.shape[0]
    own_points = weights_ref.shape[1] // (sizes[0] * sizes[1])
    here = shifted_part(0, 1, *sizes) * own_points + offset

    for (slot, base), source in zip(slots, sources):
        interleave(spec_ref, source, slot, sizes, base)
    weights = [
        weights_ref[:, pl.ds(pl.multiple_of(here + tile * LANES, LANES), LANES)]
        for tile in range(tiles)
    ]
    column = lax.broadcasted_iota(jnp.int32, (NB, LANES), 1) // NB
    owner = ((2 * PACK - column) & (2 * PACK - 1)) // 2

    def one_pack(group, carry):
        fields = []
        thirds = []
        for member in range(PACK):
            first = ids_ref[0, group * PACK + member]
            second = ids_ref[1, group * PACK + member]
            third = first + second
            field_re, field_im, third_re, third_im, third_neg = [], [], [], [], []
            for tile in range(tiles):
                def load(freq, part):
                    start = pl.multiple_of((freq + part * NF) * NB, NB)
                    return spec_ref[tile, pl.ds(start, NB), :]

                first_re, first_im = load(first, 0), load(first, 1)
                second_re, second_im = load(second, 0), load(second, 1)
                weight = weights[tile]
                field_re.append(weight * (first_re * second_re - first_im * second_im))
                field_im.append(weight * (first_re * second_im + first_im * second_re))
                third_re.append(load(third, 0))
                third_im.append(load(third, 1))
                third_neg.append(-third_re[-1])
            for parts, rows_of in (
                (field_re + field_im, fields),
                (third_re + third_im, thirds),
                (third_im + third_neg, thirds),
            ):
                rows_of.append(jnp.concatenate(parts, axis=1).astype(jnp.bfloat16))
        product = lax.dot_general(
            jnp.concatenate(fields, axis=0),
            jnp.concatenate([thirds[-column] for column in range(2 * PACK)], axis=0),
            (((1,), (1,)), ((), ())),
            preferred_element_type=jnp.float32,
        )
        total = product[0:NB]
        for member in range(1, PACK):
            total = jnp.where(owner == member, product[member * NB : (member + 1) * NB], total)
        total = total * scale
        if has_prior:
            total = total + prior_ref[group]
        out_ref[group] = total.astype(out_ref.dtype)
        return carry

    lax.fori_loop(0, out_ref.shape[0], one_pack, 0, unroll=16 if prepared else 4)


def triad_chunk(ids, weights, sources, slots, sizes, offset, width, prior, scale, prepared=None):
    rows = sources[0].shape[1]
    packs = ids.shape[1] // PACK
    spec_shape = (width // LANES, rows * NB, LANES)
    operands = [ids, weights] + ([] if prior is None else [prior])
    aliases = {}
    kept = jnp.float32 if prepared is None else jnp.bfloat16
    out_shape = [jax.ShapeDtypeStruct((packs, NB, LANES), kept)]
    scratch = []
    if prepared is None:
        scratch.append(pltpu.VMEM(spec_shape, jnp.float32))
    else:
        aliases = {len(operands): 1}
        operands.append(prepared)
        out_shape.append(jax.ShapeDtypeStruct(spec_shape, jnp.float32))
    operands += [pltpu.with_memory_space_constraint(x, pltpu.VMEM) for x in sources]
    return pl.pallas_call(
        functools.partial(
            triad_kernel, sizes, slots, offset, prepared is not None, prior is not None, scale
        ),
        out_shape=out_shape,
        in_specs=[SMEM] + [VMEM] * (len(operands) - 1),
        out_specs=[VMEM] * len(out_shape),
        scratch_shapes=scratch,
        input_output_aliases=aliases,
        compiler_params=pltpu.CompilerParams(vmem_limit_bytes=8 * MIB),
        cost_estimate=pl.CostEstimate(
            flops=packs * 2 * LANES * LANES * width,
            bytes_accessed=NB * rows * width * 2,
            transcendentals=0,
        ),
        name="triads",
    )(*operands)[0]


def finish_kernel(part_ref, out_ref):
    packs = out_ref.shape[0] // PACK
    group = lax.broadcasted_iota(jnp.int32, (8, LANES), 1) // NB
    for pack in range(packs):
        total = part_ref[pack].astype(jnp.float32)
        for device in range(1, part_ref.shape[0] // packs):
            total = total + part_ref[device * packs + pack].astype(jnp.float32)
        for half in range(2):
            skewed = pltpu.roll(total[half * 8 : half * 8 + 8], 0, 1, stride=NB, stride_axis=0)
            moved = skewed
            for shift in range(1, 8):
                moved = jnp.where(group == shift, pltpu.roll(skewed, 8 - shift, 0), moved)
            rows = pltpu.roll(moved, 0, 1, stride=NB, stride_axis=0)
            for column in range(2 * PACK):
                triad, part = divmod(column, 2)
                row = pack * PACK + triad
                start = part * NB * NB + half * LANES
                out_ref[row : row + 1, start : start + LANES] = rows[column : column + 1]


def finish(pieces, devices):
    rows = pieces.shape[0] // devices * PACK
    return pl.pallas_call(
        finish_kernel,
        out_shape=jax.ShapeDtypeStruct((rows, 2 * NB * NB), jnp.float32),
        in_specs=[VMEM],
        out_specs=VMEM,
        compiler_params=pltpu.CompilerParams(vmem_limit_bytes=8 * MIB),
        name="finish",
    )(pieces)


def mode_decomposition(snapshots, weights, triads):
    points = snapshots.shape[2]
    snapshots = pltpu.with_memory_space_constraint(snapshots, pltpu.HBM)
    freqs, bands = sizes = lax.axis_size("freq"), lax.axis_size("band")
    shards = freqs * bands
    own_points = points // shards
    widths = split_widths(own_points)
    offsets = [sum(widths[:i]) for i in range(len(widths))]
    scale = 1.0 / math.sqrt(points * lax.axis_size("space"))
    weights = weights.reshape(1, points)

    def send(value, slot):
        if slot == 0:
            return value
        shift_freq, shift_band = divmod(slot, bands)
        pairs = [
            (f * bands + b, (f + shift_freq) % freqs * bands + (b + shift_band) % bands)
            for f in range(freqs)
            for b in range(bands)
        ]
        return lax.ppermute(value, ("freq", "band"), pairs)

    def send_all(values, slots):
        return [send(value, slot) for slot, value in zip(slots, values)]

    near = list(range(bands))
    far = list(range(bands, shards))
    table, *outs = dft_far(snapshots, None, sizes, far, own_points, 0, widths[0])
    arrived = [send_all(outs, far)]
    outs = dft_far(snapshots, table, sizes, far, own_points, offsets[1], widths[1])
    arrived.append(send_all(outs, far))
    plan = [
        (slot, offset, width)
        for offset, width in list(zip(offsets, widths))[2:]
        for slot in far
    ] + [(slot, 0, own_points) for slot in near]
    rest = dft_rest(snapshots, table, sizes, plan, own_points, outs[0])
    for _ in range(2, len(widths)):
        arrived.append(send_all(rest[: len(far)], far))
        rest = rest[len(far) :]
    near_sources = send_all(rest, near)

    ids, ready = prepare(triads.T, near_sources, sizes, near, offsets[-1], widths[-1])
    total = None
    for chunk, (offset, width) in enumerate(zip(offsets, widths)):
        slots = [(slot, 0) for slot in far]
        sources = arrived[chunk]
        prepared = None
        if chunk == len(widths) - 1:
            prepared = extend(ready, total, sources[:-1], sizes, far[:-1])
            slots, sources = slots[-1:], sources[-1:]
        else:
            slots = [(slot, offset) for slot in near] + slots
            sources = near_sources + sources
        total = triad_chunk(
            ids, weights, sources, slots, sizes, offset, width, total, scale, prepared
        )

    axes = ("space", "freq", "band")
    devices = lax.axis_size("space") * shards
    pieces = lax.all_to_all(total, axes, split_axis=0, concat_axis=0, tiled=True)
    return finish(pieces, devices)


def solution(mesh):
    return jax.shard_map(
        mode_decomposition,
        mesh=mesh,
        in_specs=(P(("freq", "band"), None, ("groups", "space")), P(("groups", "space")), P()),
        out_specs=P(("groups", "space", "freq", "band"), None),
        check_vma=False,
    )
```
